512 devices in a mesh: seq: 32 (over y, x, core), tp: 16 (over z).
Axes of the slice: x: 4, y: 4, z: 16, core: 2. Of those that a mesh axis runs over, the one named last changes fastest.
Arguments:
- tokens: bfloat16 [4096, 4096], P('seq', 'tp'), may hold values from -6 to 6
- in_weight: bfloat16 [4096, 8192], P(None, 'tp'), may hold values from -0.09375 to 0.09375
- conv_weight: float32 [4, 8192], P(None, 'tp'), may hold values from -3 to 3
- conv_bias: float32 [8192], P('tp'), may hold values from -0.5 to 0.5
- proj_weight: bfloat16 [8192, 288], P('tp'), may hold values from -0.0625 to 0.0625
- dt_weight: bfloat16 [256, 8192], P(None, 'tp'), may hold values from -0.375 to 0.375
- dt_bias: float32 [8192], P('tp'), may hold values from -7 to -2
- a_log: float32 [16, 8192], P(None, 'tp'), may hold values from -3 to 1.5
- skip_gain: float32 [8192], P('tp'), may hold values from 0.5 to 1.5
- threshold: float32 [8192], P('tp'), may hold values from -0.5 to 0.5
Outputs:
- gated: bfloat16 [4096, 8192], P('seq', 'tp')
The draws below stay inside these ranges and needn't reach their ends.
All inputs are finite; a program needn't handle non-finite values.
Results may differ from the reference program's by a relative error of at most 0.0085.
Values may be sent and summed in bfloat16 or wider, within the bound.
No kernel may reach another device: no remote copies, remote signals or barrier semaphores. Data moves between devices by JAX's collectives and lax.ppermute only.
A program may use at most 64 MiB of HBM per device.

```python
import jax
import jax.numpy as jnp
from jax import lax

D = 4096
DI = 8192
N = 16
R = 256
CONV = 4
TOKENS = 4096


def shard_levels(stream_key, shape, shards, smallest, high):
    def one(axis_at, shards_of):
        draws = jax.random.uniform(jax.random.fold_in(jax.random.fold_in(stream_key, 6), axis_at), (shards_of,), jnp.float32, smallest / len(shards), high / len(shards))
        return jnp.repeat(jnp.exp(draws), shape[axis_at] // shards_of).reshape((-1,) + (1,) * (len(shape) - axis_at - 1))

    loudness = one(*shards[0])
    for cut in shards[1:]:
        loudness = loudness * one(*cut)
    return loudness


def normal_values(key, shape, deviation, limit, split=(), dtype=jnp.bfloat16):
    drawn = deviation * jax.random.normal(key, shape, jnp.float32)
    if split:
        drawn = drawn * shard_levels(key, shape, split, -0.22, 0.18)
    return jnp.clip(drawn, -limit, limit).astype(dtype)


def setup_inputs(seed: int = 0) -> dict:
    splits = jax.random.split(jax.random.key(seed), 11)
    tokens = normal_values(splits[0], (TOKENS, D), 1.0, 6.0, ((0, 32), (1, 16)))
    in_weight = normal_values(splits[1], (D, DI), D ** -0.5, 0.09375, ((1, 16),))
    conv_weight = normal_values(splits[2], (CONV, DI), CONV ** -0.5, 3.0, ((1, 16),), jnp.float32)
    conv_bias = jnp.clip(jax.random.uniform(splits[3], (DI,), jnp.float32, -0.5, 0.5) * shard_levels(splits[3], (DI,), ((0, 16),), -0.4, 0.0), -0.5, 0.5)
    proj_weight = normal_values(splits[4], (DI, R + 2 * N), DI ** -0.5, 0.0625, ((0, 16),))
    dt_weight = normal_values(splits[5], (R, DI), R ** -0.5, 0.375, ((1, 16),))
    dt_bias = jnp.clip(-7.0 + 5.0 * jax.random.uniform(splits[6], (DI,), jnp.float32) ** shard_levels(splits[6], (DI,), ((0, 16),), -0.2, 0.2), -7.0, -2.0)
    a_log = jnp.clip(-3.0 + 4.5 * jax.random.uniform(splits[7], (N, DI), jnp.float32) ** shard_levels(splits[7], (N, DI), ((1, 16),), -0.2, 0.2), -3.0, 1.5)
    skip_gain = jnp.clip(0.5 + 1.0 * jax.random.uniform(splits[8], (DI,), jnp.float32) ** shard_levels(splits[8], (DI,), ((0, 16),), -0.2, 0.2), 0.5, 1.5)
    threshold = jnp.clip(jax.random.uniform(splits[9], (DI,), jnp.float32, -0.5, 0.5) * shard_levels(splits[9], (DI,), ((0, 16),), -0.4, 0.0), -0.5, 0.5)
    return {"tokens": tokens, "in_weight": in_weight, "conv_weight": conv_weight, "conv_bias": conv_bias, "proj_weight": proj_weight, "dt_weight": dt_weight, "dt_bias": dt_bias, "a_log": a_log, "skip_gain": skip_gain, "threshold": threshold}


def reference(tokens, in_weight, conv_weight, conv_bias, proj_weight, dt_weight, dt_bias, a_log, skip_gain, threshold):
    inner = jnp.dot(tokens, in_weight, preferred_element_type=jnp.float32).astype(jnp.bfloat16)
    padded = jnp.concatenate([jnp.zeros((CONV - 1, DI), jnp.bfloat16), inner], axis=0)
    pre = conv_bias[None, :] + jnp.zeros((TOKENS, DI), jnp.float32)
    for k in range(CONV):
        pre = pre + conv_weight[k][None, :] * padded[k:k + TOKENS].astype(jnp.float32)
    u = jax.nn.silu(pre).astype(jnp.bfloat16)
    total = jnp.dot(u, proj_weight, preferred_element_type=jnp.float32)
    dt_low = total[:, :R].astype(jnp.bfloat16)
    b_coef = total[:, R:R + N]
    c_coef = total[:, R + N:]
    dt = jax.nn.softplus(jnp.dot(dt_low, dt_weight, preferred_element_type=jnp.float32) + dt_bias[None, :])
    rate = -jnp.exp(a_log)
    u_float = u.astype(jnp.float32)

    def advance(state, items):
        dt_row, u_row, b_row, c_row = items
        state = jnp.exp(dt_row[None, :] * rate) * state + (dt_row * u_row)[None, :] * b_row[:, None]
        return state, jnp.sum(c_row[:, None] * state, axis=0)

    start = jnp.zeros((N, DI), jnp.float32)
    _, scanned = lax.scan(advance, start, (dt, u_float, b_coef, c_coef))
    y_full = scanned + skip_gain[None, :] * u_float
    return (y_full * jax.nn.sigmoid(4.0 * (y_full - threshold[None, :]))).astype(jnp.bfloat16)
```

```python
import math

import jax
import jax.numpy as jnp
from jax import lax
from jax.experimental import pallas as pl
from jax.experimental.pallas import tpu as pltpu
from jax.sharding import PartitionSpec as P

LOG2E = math.log2(math.e)
F32 = jnp.float32
BF16 = jnp.bfloat16
VMEM = pl.BlockSpec(memory_space=pltpu.VMEM)
SMEM = pl.BlockSpec(memory_space=pltpu.SMEM)


def struct(shape, dtype):
    return jax.ShapeDtypeStruct(shape, dtype)


def to_all(block, axis):
    peers = lax.axis_size(axis)
    return lax.all_to_all(jnp.broadcast_to(block[None], (peers,) + block.shape), axis, 0, 0)


def project_kernel(main_ref, tail_ref, weight_ref, inner_ref):
    shards, rows, depth = main_ref.shape
    tail_rows = tail_ref.shape[1]
    width = weight_ref.shape[1]
    acc = jnp.zeros((rows, width), F32)
    acc_tail = jnp.zeros((tail_rows, width), F32)
    for z in range(shards):
        w = weight_ref[z * depth : (z + 1) * depth, :]
        acc = acc + jnp.dot(main_ref[z], w, preferred_element_type=F32)
        acc_tail = acc_tail + jnp.dot(tail_ref[z], w, preferred_element_type=F32)
    inner_ref[:rows, :] = acc.astype(BF16)
    inner_ref[rows:, :] = acc_tail.astype(BF16)


def conv_kernel(inner_ref, rim_ref, taps_ref, bias_ref, proj_ref, u_ref, part_ref, pad_ref):
    rows, width = inner_ref.shape
    rim = rim_ref.shape[0]
    taps = taps_ref.shape[0]
    pad_ref[:rim, :] = rim_ref[...].astype(F32)
    pad_ref[rim:, :] = inner_ref[...].astype(F32)
    pre = jnp.broadcast_to(bias_ref[...], (rows, width))
    for k in range(taps):
        first = rim - taps + 1 + k
        pre = pre + taps_ref[k : k + 1, :] * pad_ref[first : first + rows, :]
    u = (pre / (1.0 + jnp.exp(-pre))).astype(BF16)
    u_ref[...] = u
    part_ref[...] = jnp.dot(u, proj_ref[...], preferred_element_type=F32).astype(BF16)


def split3(x):
    a = x.astype(BF16)
    r = x - a.astype(F32)
    b = r.astype(BF16)
    c = (r - b.astype(F32)).astype(BF16)
    return a, b, c


def state_kernel(
    mix_ref, dtw_ref, dtb_ref, alog_ref, u_ref, step_ref, cum_ref, pay_ref, left_ref, flow_ref, bx_ref
):
    rows, width = u_ref.shape
    rank = dtw_ref.shape[0]
    n = alog_ref.shape[0]
    tiles = rows // 8
    v = jnp.dot(mix_ref[:, :rank], dtw_ref[...], preferred_element_type=F32) + dtb_ref[...]
    step = jnp.maximum(v, 0.0) + jnp.log1p(jnp.exp(-jnp.abs(v)))
    step_ref[...] = step
    row_ids = lax.broadcasted_iota(jnp.int32, (rows, rows), 0)
    col_ids = lax.broadcasted_iota(jnp.int32, (rows, rows), 1)
    lower = (row_ids >= col_ids).astype(F32).astype(BF16)
    cum = sum(jnp.dot(lower, p, preferred_element_type=F32) for p in split3(step)[::-1])
    cum_ref[...] = cum
    whole = cum[rows - 1 : rows, :]
    left_ref[...] = (whole - cum).reshape(tiles, 8, width)
    flow_ref[...] = (step * u_ref[...].astype(F32)).reshape(tiles, 8, width)
    b = mix_ref[:, rank : rank + n].astype(F32) + mix_ref[:, rank + 2 * n : rank + 3 * n].astype(F32)
    for i in range(n):
        bx_ref[:, i] = jnp.broadcast_to(b[:, i : i + 1], (rows, 128)).reshape(tiles, 8, 128)
    rate2 = -jnp.exp(alog_ref[...]) * LOG2E
    for g in range(width // 128):
        lanes = slice(g * 128, (g + 1) * 128)
        rate_g = jnp.broadcast_to(rate2[:, None, lanes], (n, 8, 128))

        def turn(i, acc):
            grow = jnp.exp2(rate_g * left_ref[i, :, lanes][None])
            return acc + grow * (flow_ref[i, :, lanes][None] * bx_ref[i])

        acc = lax.fori_loop(0, tiles, turn, jnp.zeros((n, 8, 128), F32), unroll=2)
        pay_ref[:n, lanes] = jnp.sum(acc, axis=1).astype(BF16)
    hi, lo, _ = split3(whole)
    pay_ref[n : n + 1, :] = hi
    pay_ref[n + 1 : n + 2, :] = lo


def local_kernel(mix_ref, alog_ref, u_ref, step_ref, cum_ref, skip_ref, y_ref, grow_ref, bt_ref, ct_ref, flow_ref, cx_ref):
    rows, width = u_ref.shape
    n = alog_ref.shape[0]
    tiles = rows // 8
    rank = mix_ref.shape[1] - 4 * n
    b = mix_ref[:, rank : rank + n].astype(F32) + mix_ref[:, rank + 2 * n : rank + 3 * n].astype(F32)
    c = mix_ref[:, rank + n : rank + 2 * n].astype(F32) + mix_ref[:, rank + 3 * n :].astype(F32)
    rate2 = -jnp.exp(alog_ref[...]) * LOG2E
    for i in range(n):
        cx_ref[:, i] = jnp.broadcast_to(c[:, i : i + 1], (rows, 128)).reshape(tiles, 8, 128)
    b_t, c_t = b.T, c.T
    for t in range(rows):
        bt_ref[t] = jnp.broadcast_to(b_t[:, t : t + 1], (n, 128))
        ct_ref[t] = jnp.broadcast_to(c_t[:, t : t + 1], (n, 128))
    u_float = u_ref[...].astype(F32)
    flow_ref[...] = step_ref[...] * u_float
    groups = width // 128

    def turn(t, state):
        d = step_ref[pl.ds(t, 1), :]
        f = flow_ref[pl.ds(t, 1), :]
        bt = jnp.concatenate([bt_ref[t]] * groups, axis=1)
        ct = jnp.concatenate([ct_ref[t]] * groups, axis=1)
        state = jnp.exp2(rate2 * d) * state + bt * f
        y_ref[pl.ds(t, 1), :] = jnp.sum(ct * state, axis=0, keepdims=True)
        return state

    lax.fori_loop(0, rows, turn, jnp.zeros((n, width), F32), unroll=4)
    y_ref[...] = y_ref[...] + skip_ref[...] * u_float

    for g in range(groups):
        lanes = slice(g * 128, (g + 1) * 128)
        rate_g = jnp.broadcast_to(rate2[:, None, lanes], (n, 8, 128))

        def fill(i, _):
            cum = cum_ref[pl.ds(pl.multiple_of(i * 8, 8), 8), lanes]
            grow_ref[i, :, :, lanes] = cx_ref[i] * jnp.exp2(rate_g * cum[None])
            return 0

        lax.fori_loop(0, tiles, fill, 0, unroll=2)


def final_kernel(mine_ref, all_ref, alog_ref, y_ref, grow_ref, thr_ref, out_ref):
    rows, width = y_ref.shape
    n = alog_ref.shape[0]
    tiles = rows // 8
    peers = all_ref.shape[0]
    mine = mine_ref[0]
    rate2 = -jnp.exp(alog_ref[...]) * LOG2E

    def join(p, state):
        block = all_ref[p].astype(F32)
        whole = block[n : n + 1, :] + block[n + 1 : n + 2, :]
        longer = jnp.exp2(rate2 * whole) * state + block[:n, :]
        return jnp.where(p < mine, longer, state)

    entry = lax.fori_loop(0, peers - 1, join, jnp.zeros((n, width), F32), unroll=2)
    for g in range(width // 128):
        lanes = slice(g * 128, (g + 1) * 128)
        entry_g = jnp.broadcast_to(entry[:, None, lanes], (n, 8, 128))
        thr = thr_ref[:, lanes]

        def turn(i, _):
            at = pl.ds(pl.multiple_of(i * 8, 8), 8)
            y = y_ref[at, lanes] + jnp.sum(grow_ref[i, :, :, lanes] * entry_g, axis=0)
            y_ref[at, lanes] = y / (1.0 + jnp.exp(-4.0 * (y - thr)))
            return 0

        lax.fori_loop(0, tiles, turn, 0, unroll=2)
    out_ref[...] = y_ref[...].astype(BF16)


def call(kernel, outs, ins, scratch=(), flops=0, specs=None):
    return pl.pallas_call(
        kernel,
        out_shape=outs,
        in_specs=specs or [VMEM] * len(ins),
        out_specs=jax.tree.map(lambda _: VMEM, outs),
        scratch_shapes=scratch,
        cost_estimate=pl.CostEstimate(flops=flops, bytes_accessed=flops // 64, transcendentals=0),
        compiler_params=pltpu.CompilerParams(vmem_limit_bytes=48 << 20),
    )(*ins)


def per_device(
    tokens, in_weight, conv_weight, conv_bias, proj_weight, dt_weight, dt_bias, a_log, skip_gain, threshold
):
    rows = tokens.shape[0]
    width = in_weight.shape[1]
    taps = conv_weight.shape[0]
    rank = dt_weight.shape[0]
    n = a_log.shape[0]
    shards = lax.axis_size("tp")
    peers = lax.axis_size("seq")
    each = rows // shards
    cut = rows - 8

    tail = to_all(tokens[cut:], "tp")
    main = lax.all_gather(tokens[:cut], "tp")
    inner = call(project_kernel, struct((rows, width), BF16), (main, tail, in_weight), flops=1 << 29)
    rim = lax.ppermute(inner[rows - 8 :], "seq", [(i, i + 1) for i in range(peers - 1)])
    u, part = call(
        conv_kernel,
        (struct((rows, width), BF16), struct((rows, rank + 2 * n), BF16)),
        (inner, rim, conv_weight, conv_bias[None], proj_weight),
        (pltpu.VMEM((rows + 8, width), F32),),
        flops=1 << 26,
    )
    parts = lax.all_to_all(part.reshape(shards, each, rank + 2 * n), "tp", 0, 0)
    total = jnp.sum(parts.astype(F32), axis=0)
    high = lax.reduce_precision(total, 8, 7)
    low = total[:, rank:] - high[:, rank:]
    mix = to_all(jnp.concatenate([high, low], axis=1).astype(BF16), "tp").reshape(rows, rank + 4 * n)
    step, cum, pay = call(
        state_kernel,
        (struct((rows, width), F32), struct((rows, width), F32), struct((n + 2, width), BF16)),
        (mix, dt_weight, dt_bias[None], a_log, u),
        (
            pltpu.VMEM((rows // 8, 8, width), F32),
            pltpu.VMEM((rows // 8, 8, width), F32),
            pltpu.VMEM((rows // 8, n, 8, 128), F32),
        ),
        flops=1 << 26,
    )
    everyone = to_all(pay, "seq")
    y_local, grow = call(
        local_kernel,
        (struct((rows, width), F32), struct((rows // 8, n, 8, width), F32)),
        (mix, a_log, u, step, cum, skip_gain[None]),
        (
            pltpu.VMEM((rows, n, 128), F32),
            pltpu.VMEM((rows, n, 128), F32),
            pltpu.VMEM((rows, width), F32),
            pltpu.VMEM((rows // 8, n, 8, 128), F32),
        ),
        flops=1 << 28,
    )
    mine = lax.axis_index("seq").astype(jnp.int32)[None]
    return call(
        final_kernel,
        struct((rows, width), BF16),
        (mine, everyone, a_log, y_local, grow, threshold[None]),
        flops=1 << 26,
        specs=[SMEM] + [VMEM] * 5,
    )


def solution(mesh):
    return jax.shard_map(
        per_device,
        mesh=mesh,
        in_specs=(
            P("seq", "tp"),
            P(None, "tp"),
            P(None, "tp"),
            P("tp"),
            P("tp", None),
            P(None, "tp"),
            P("tp"),
            P(None, "tp"),
            P("tp"),
            P("tp"),
        ),
        out_specs=P("seq", "tp"),
        check_vma=False,
    )
```

```python
import math

import jax
import jax.numpy as jnp
from jax import lax
from jax.experimental import pallas as pl
from jax.experimental.pallas import tpu as pltpu
from jax.sharding import PartitionSpec as P

LOG2E = math.log2(math.e)
F32 = jnp.float32
BF16 = jnp.bfloat16
VMEM = pl.BlockSpec(memory_space=pltpu.VMEM)
SMEM = pl.BlockSpec(memory_space=pltpu.SMEM)


def struct(shape, dtype):
    return jax.ShapeDtypeStruct(shape, dtype)


def silu(v):
    return v / (1.0 + jnp.exp(-v))


def convolve(taps_ref, bias_ref, pad_ref, rows, width):
    taps = taps_ref.shape[0]
    pre = jnp.broadcast_to(bias_ref[...], (rows, width))
    for k in range(taps):
        first = 9 - taps + k
        pre = pre + taps_ref[k : k + 1, :] * pad_ref[first : first + rows, :]
    return silu(pre).astype(BF16)


def pieces(depth, room):
    return [(at, min(room, depth - at)) for at in range(0, depth, room)]


def project_kernel(
    main_ref, tokens_ref, weight_ref, taps_ref, bias_ref, proj_ref,
    send_ref, edge_ref, u_ref, pad_ref, wide_ref,
):
    shards, held, depth = main_ref.shape
    rows, width = u_ref.shape
    sums = proj_ref.shape[1]
    acc = jnp.zeros((held, width), F32)
    for z in range(shards):
        w = weight_ref[z * depth : (z + 1) * depth, :]
        acc = acc + jnp.dot(main_ref[z], w, preferred_element_type=F32)
    pad_ref[:16, :] = jnp.zeros((16, width), F32)
    pad_ref[8 + rows - held :, :] = acc.astype(BF16).astype(F32)
    edge_ref[:8, :] = pad_ref[rows : rows + 8, :].astype(BF16)
    edge_ref[8:, :] = pad_ref[8:16, :].astype(BF16)
    u = convolve(taps_ref, bias_ref, pad_ref, rows, width)
    u_ref[...] = u
    part = jnp.dot(u, proj_ref[...], preferred_element_type=F32)
    wide_ref[:, :, :sums] = part.reshape(shards, 8, sums)
    late = tokens_ref[0:8, :].astype(F32)[0:1, :]
    room = wide_ref.shape[2] - sums
    row_ids = lax.broadcasted_iota(jnp.int32, (8, room), 0)
    block = jnp.zeros((8, room), F32)
    for p, (at, size) in enumerate(pieces(depth, room)):
        piece = late[:, at : at + size]
        if size < room:
            piece = jnp.concatenate([piece, jnp.zeros((1, room - size), F32)], axis=1)
        block = jnp.where(row_ids == p, jnp.broadcast_to(piece, (8, room)), block)
    wide_ref[:, :, sums:] = jnp.broadcast_to(block[None], (shards, 8, room))
    send_ref[...] = wide_ref[...].astype(BF16)


def late_kernel(
    got_ref, rim_ref, edge_ref, weight_ref, taps_ref, bias_ref, proj_ref,
    mix_ref, u_ref, wide_ref, first_ref, pad_ref, pay_ref,
):
    shards, _, lanes = got_ref.shape
    depth = weight_ref.shape[0] // shards
    width = weight_ref.shape[1]
    sums = proj_ref.shape[1]
    room = lanes - sums
    wide_ref[...] = got_ref[...].astype(F32)
    total = jnp.sum(wide_ref[:, :, :sums], axis=0)
    for p, (at, size) in enumerate(pieces(depth, room)):
        first_ref[:, at : at + size] = wide_ref[:, p, sums : sums + size]
    first = first_ref[...].astype(BF16)
    row_ids = lax.broadcasted_iota(jnp.int32, (shards, width), 0)
    acc = jnp.zeros((shards, width), F32)
    for z in range(shards):
        d = jnp.dot(first, weight_ref[z * depth : (z + 1) * depth, :], preferred_element_type=F32)
        acc = acc + jnp.where(row_ids == z, d, 0.0)
    pad_ref[:8, :] = rim_ref[...].astype(F32)
    pad_ref[8:, :] = edge_ref[8:, :].astype(F32)
    pad_ref[8:9, :] = jnp.sum(acc, axis=0, keepdims=True).astype(BF16).astype(F32)
    u = convolve(taps_ref, bias_ref, pad_ref, 8, width)
    u_ref[...] = u
    part = jnp.dot(u, proj_ref[...], preferred_element_type=F32)
    high = total.astype(BF16).astype(F32)
    rank = mix_ref.shape[2] - 256
    coefs = sums - rank
    half = sums // 2
    late = taps_ref.shape[0]
    pay_ref[...] = jnp.zeros_like(pay_ref)
    pay_ref[:, :sums] = high
    pay_ref[:, sums : sums + coefs] = total[:, rank:] - high[:, rank:]
    at = sums + coefs
    pay_ref[:late, at : at + half] = part[:late, :half]
    pay_ref[late : 2 * late, at : at + half] = part[:late, half:]
    pay = pay_ref[...].astype(BF16)
    for z in range(shards):
        mix_ref[z] = pay


def split3(x):
    a = x.astype(BF16)
    r = x - a.astype(F32)
    b = r.astype(BF16)
    c = (r - b.astype(F32)).astype(BF16)
    return a, b, c


def running_sum(x):
    rows = x.shape[0]
    row_ids = lax.broadcasted_iota(jnp.int32, (rows, rows), 0)
    col_ids = lax.broadcasted_iota(jnp.int32, (rows, rows), 1)
    lower = (row_ids >= col_ids).astype(F32).astype(BF16)
    return sum(jnp.dot(lower, p, preferred_element_type=F32) for p in split3(x)[::-1])


def state_kernel(
    mix_ref, dtw_ref, dtb_ref, alog_ref, u_ref, late_u_ref,
    step_ref, coef_ref, pay_ref,
    uf_ref, flow_ref, left_ref, bx_ref, end_ref, low_ref,
):
    shards, each, _ = mix_ref.shape
    rows, width = u_ref.shape
    rank = dtw_ref.shape[0]
    n = alog_ref.shape[0]
    sums = rank + 2 * n
    half = sums // 2
    at = sums + 2 * n
    late = each // 2
    tiles = rows // 8
    low_ref[...] = mix_ref[:, :, :rank].astype(F32).reshape(rows, rank)
    coef = mix_ref[:, :, rank:sums].astype(F32) + mix_ref[:, :, sums:at].astype(F32)
    coef_ref[...] = coef.reshape(rows, 2 * n)
    pairs = jnp.sum(mix_ref[:, :, at : at + half].astype(F32), axis=0)
    early = jnp.concatenate([pairs[:late], pairs[late:]], axis=1)
    low_ref[:late, :] = early[:, :rank]
    coef_ref[:late, :] = early[:, rank:]
    v = jnp.dot(low_ref[...].astype(BF16), dtw_ref[...], preferred_element_type=F32) + dtb_ref[...]
    step = jnp.maximum(v, 0.0) + jnp.log1p(jnp.exp(-jnp.abs(v)))
    step_ref[...] = step
    cum = running_sum(step)
    whole = cum[rows - 1 : rows, :]
    left_ref[...] = (whole - cum).reshape(tiles, 8, width)
    uf_ref[...] = u_ref[...].astype(F32)
    uf_ref[:8, :] = late_u_ref[...].astype(F32)
    flow_ref[...] = (step * uf_ref[...]).reshape(tiles, 8, width)
    b = coef_ref[:, :n]
    for i in range(n):
        bx_ref[:, i] = jnp.broadcast_to(b[:, i : i + 1], (rows, 128)).reshape(tiles, 8, 128)
    rate2 = -jnp.exp(alog_ref[...]) * LOG2E
    groups = width // 128
    for g in range(groups):
        lanes = slice(g * 128, (g + 1) * 128)
        rate_g = jnp.broadcast_to(rate2[:, None, lanes], (n, 8, 128))

        def turn(i, acc):
            grow = jnp.exp2(rate_g * left_ref[i, :, lanes][None])
            return acc + grow * (flow_ref[i, :, lanes][None] * bx_ref[i])

        acc = lax.fori_loop(0, tiles, turn, jnp.zeros((n, 8, 128), F32), unroll=2)
        hi, lo, _ = split3(whole[:, lanes])
        end_ref[g * n : (g + 1) * n, :] = jnp.sum(acc, axis=1)
        end_ref[groups * n + g : groups * n + g + 1, :] = hi.astype(F32)
        end_ref[groups * n + groups + g : groups * n + groups + g + 1, :] = lo.astype(F32)
    end = end_ref[...].astype(BF16)
    for p in range(pay_ref.shape[0]):
        pay_ref[p] = end


def local_kernel(
    coef_ref, alog_ref, u_ref, late_u_ref, step_ref, skip_ref,
    y_ref, grow_ref, bt_ref, ct_ref, cx_ref, uf_ref, flow_ref, cum_ref,
):
    rows, width = u_ref.shape
    uf_ref[...] = u_ref[...].astype(F32)
    uf_ref[:8, :] = late_u_ref[...].astype(F32)
    flow_ref[...] = (step_ref[...] * uf_ref[...]).reshape(rows // 8, 8, width)
    cum_ref[...] = running_sum(step_ref[...])
    n = alog_ref.shape[0]
    blocks = rows // 16
    b, c = coef_ref[:, :n], coef_ref[:, n:]
    rate2 = -jnp.exp(alog_ref[...]) * LOG2E
    for i in range(n):
        cx_ref[:, i] = jnp.broadcast_to(c[:, i : i + 1], (rows, 128)).reshape(blocks, 16, 128)
    b_t, c_t = b.T, c.T
    for t in range(rows):
        bt_ref[t] = jnp.broadcast_to(b_t[:, t : t + 1], (n, 128))
        ct_ref[t] = jnp.broadcast_to(c_t[:, t : t + 1], (n, 128))
    groups = width // 128

    def block_turn(i, state):
        for r in range(8):
            t = i * 8 + r
            d = step_ref[pl.ds(t, 1), :]
            f = flow_ref[i, r : r + 1, :]
            bt = jnp.concatenate([bt_ref[t]] * groups, axis=1)
            ct = jnp.concatenate([ct_ref[t]] * groups, axis=1)
            state = jnp.exp2(rate2 * d) * state + bt * f
            y_ref[pl.ds(t, 1), :] = jnp.sum(ct * state, axis=0, keepdims=True)
        return state

    lax.fori_loop(0, rows // 8, block_turn, jnp.zeros((n, width), F32))
    y_ref[...] = y_ref[...] + skip_ref[...] * uf_ref[...]

    for g in range(groups):
        lanes = slice(g * 128, (g + 1) * 128)
        rate_g = jnp.broadcast_to(rate2[:, None, lanes], (n, 16, 128))

        def fill(i, _):
            cum = cum_ref[pl.ds(pl.multiple_of(i * 16, 16), 16), lanes]
            grow_ref[i, :, :, lanes] = (cx_ref[i] * jnp.exp2(rate_g * cum[None])).astype(BF16)
            return 0

        lax.fori_loop(0, blocks, fill, 0)


def final_kernel(mine_ref, all_ref, alog_ref, y_ref, grow_ref, thr_ref, out_ref):
    rows, width = y_ref.shape
    n = alog_ref.shape[0]
    blocks = rows // 16
    peers = all_ref.shape[0]
    mine = mine_ref[0]
    rate2 = -jnp.exp(alog_ref[...]) * LOG2E

    groups = width // 128
    for g in range(groups):
        lanes = slice(g * 128, (g + 1) * 128)
        rate_g = rate2[:, lanes]

        def join(p, state):
            block = all_ref[p].astype(F32)
            at = groups * n + g
            whole = block[at : at + 1, :] + block[at + groups : at + groups + 1, :]
            longer = jnp.exp2(rate_g * whole) * state + block[g * n : (g + 1) * n, :]
            return jnp.where(p < mine, longer, state)

        entry = jnp.zeros((n, 128), F32)
        for p in range(peers - 1):
            entry = join(p, entry)
        entry_g = jnp.broadcast_to(entry[:, None, :], (n, 16, 128))
        thr = thr_ref[:, lanes]

        def turn(i, _):
            at = pl.ds(pl.multiple_of(i * 16, 16), 16)
            y = y_ref[at, lanes] + jnp.sum(grow_ref[i, :, :, lanes].astype(F32) * entry_g, axis=0)
            y_ref[at, lanes] = y / (1.0 + jnp.exp(-4.0 * (y - thr)))
            return 0

        lax.fori_loop(0, blocks, turn, 0)
    out_ref[...] = y_ref[...].astype(BF16)


def call(kernel, outs, ins, scratch=(), flops=0, specs=None):
    return pl.pallas_call(
        kernel,
        out_shape=outs,
        in_specs=specs or [VMEM] * len(ins),
        out_specs=jax.tree.map(lambda _: VMEM, outs),
        scratch_shapes=scratch,
        cost_estimate=pl.CostEstimate(flops=flops, bytes_accessed=flops // 64, transcendentals=0),
        compiler_params=pltpu.CompilerParams(vmem_limit_bytes=12 << 20),
    )(*ins)


def per_device(
    tokens, in_weight, conv_weight, conv_bias, proj_weight, dt_weight, dt_bias, a_log, skip_gain, threshold
):
    rows = tokens.shape[0]
    width = in_weight.shape[1]
    taps = conv_weight.shape[0]
    rank = dt_weight.shape[0]
    n = a_log.shape[0]
    shards = lax.axis_size("tp")
    peers = lax.axis_size("seq")
    sums = rank + 2 * n
    lanes = -(-sums // 128) * 128
    bias = conv_bias[None]

    main = lax.all_gather(tokens[1:], "tp")
    send, edge, u = call(
        project_kernel,
        (struct((shards, 8, lanes), BF16), struct((16, width), BF16), struct((rows, width), BF16)),
        (main, tokens, in_weight, conv_weight, bias, proj_weight),
        (pltpu.VMEM((rows + 8, width), F32), pltpu.VMEM((shards, 8, lanes), F32)),
        flops=1 << 29,
    )
    rim = lax.ppermute(edge[:8], "seq", [(i, i + 1) for i in range(peers - 1)])
    got = lax.all_to_all(send, "tp", 0, 0)
    mix, late_u = call(
        late_kernel,
        (struct((shards, 8, rank + 256), BF16), struct((8, width), BF16)),
        (got, rim, edge, in_weight, conv_weight, bias, proj_weight),
        (
            pltpu.VMEM((shards, 8, lanes), F32),
            pltpu.VMEM((shards, tokens.shape[1]), F32),
            pltpu.VMEM((16, width), F32),
            pltpu.VMEM((8, rank + 256), F32),
        ),
        flops=1 << 28,
    )
    mix = lax.all_to_all(mix, "tp", 0, 0)
    whole = struct((rows, width), F32)
    step, coef, pay = call(
        state_kernel,
        (whole, struct((rows, 2 * n), F32), struct((peers, (n + 2) * width // 128, 128), BF16)),
        (mix, dt_weight, dt_bias[None], a_log, u, late_u),
        (
            pltpu.VMEM((rows, width), F32),
            pltpu.VMEM((rows // 8, 8, width), F32),
            pltpu.VMEM((rows // 8, 8, width), F32),
            pltpu.VMEM((rows // 8, n, 8, 128), F32),
            pltpu.VMEM(((n + 2) * width // 128, 128), F32),
            pltpu.VMEM((rows, rank), F32),
        ),
        flops=1 << 26,
    )
    everyone = lax.all_to_all(pay, "seq", 0, 0)
    y_local, grow = call(
        local_kernel,
        (whole, struct((rows // 16, n, 16, width), BF16)),
        (coef, a_log, u, late_u, step, skip_gain[None]),
        (
            pltpu.VMEM((rows, n, 128), F32),
            pltpu.VMEM((rows, n, 128), F32),
            pltpu.VMEM((rows // 16, n, 16, 128), F32),
            pltpu.VMEM((rows, width), F32),
            pltpu.VMEM((rows // 8, 8, width), F32),
            pltpu.VMEM((rows, width), F32),
        ),
        flops=1 << 28,
    )
    mine = lax.axis_index("seq").astype(jnp.int32)[None]
    return call(
        final_kernel,
        struct((rows, width), BF16),
        (mine, everyone, a_log, y_local, grow, threshold[None]),
        flops=1 << 26,
        specs=[SMEM] + [VMEM] * 5,
    )


def solution(mesh):
    return jax.shard_map(
        per_device,
        mesh=mesh,
        in_specs=(
            P("seq", "tp"),
            P(None, "tp"),
            P(None, "tp"),
            P("tp"),
            P("tp", None),
            P(None, "tp"),
            P("tp"),
            P(None, "tp"),
            P("tp"),
            P("tp"),
        ),
        out_specs=P("seq", "tp"),
        check_vma=False,
    )
```

```python
import math

import jax
import jax.numpy as jnp
from jax import lax
from jax.experimental import pallas as pl
from jax.experimental.pallas import tpu as pltpu
from jax.sharding import PartitionSpec as P

LOG2E = math.log2(math.e)
F32 = jnp.float32
BF16 = jnp.bfloat16
VMEM = pl.BlockSpec(memory_space=pltpu.VMEM)
SMEM = pl.BlockSpec(memory_space=pltpu.SMEM)
HBM = pl.BlockSpec(memory_space=pltpu.HBM)


def struct(shape, dtype):
    return jax.ShapeDtypeStruct(shape, dtype)


def silu(v):
    return v / (1.0 + jnp.exp(-v))


def convolve(taps_ref, bias_ref, pad_ref, rows, width):
    taps = taps_ref.shape[0]
    pre = jnp.broadcast_to(bias_ref[...], (rows, width))
    for k in range(taps):
        first = 9 - taps + k
        pre = pre + taps_ref[k : k + 1, :] * pad_ref[first : first + rows, :]
    return silu(pre).astype(BF16)


def pieces(depth, room):
    return [(at, min(room, depth - at)) for at in range(0, depth, room)]


def project_rows(u, proj_ref):
    return lax.dot_general(u, proj_ref[...], (((1,), (1,)), ((), ())), preferred_element_type=F32)


def fetches(pairs, sems):
    copies = [pltpu.make_async_copy(src, dst, sems.at[i]) for i, (src, dst) in enumerate(pairs)]
    for copy in copies:
        copy.start()
    return copies


def weight_fetches(hbm_ref, buf_ref, shards, depth):
    return [(hbm_ref.at[pl.ds(z * depth, depth)], buf_ref.at[pl.ds(z * depth, depth)]) for z in range(shards)]


def project_kernel(
    main_ref, tokens_hbm, weight_hbm, taps_hbm, bias_hbm, proj_hbm,
    send_ref, edge_ref, u_ref,
    pad_ref, wide_ref, weight_ref, taps_ref, bias_ref, proj_ref, tokens_ref, sems,
):
    shards, held, depth = main_ref.shape
    rows, width = u_ref.shape
    sums = proj_ref.shape[0]
    copies = fetches(
        weight_fetches(weight_hbm, weight_ref, shards, depth)
        + [(taps_hbm, taps_ref), (bias_hbm, bias_ref), (proj_hbm, proj_ref),
           (tokens_hbm.at[pl.ds(0, 8)], tokens_ref)],
        sems,
    )
    pad_ref[:16, :] = jnp.zeros((16, width), F32)
    acc = jnp.zeros((held, width), F32)
    for z in range(shards):
        copies[z].wait()
        w = weight_ref[z * depth : (z + 1) * depth, :]
        acc = acc + jnp.dot(main_ref[z], w, preferred_element_type=F32)
    for copy in copies[shards:]:
        copy.wait()
    pad_ref[8 + rows - held :, :] = acc.astype(BF16).astype(F32)
    edge_ref[:8, :] = pad_ref[rows : rows + 8, :].astype(BF16)
    edge_ref[8:, :] = pad_ref[8:16, :].astype(BF16)
    u = convolve(taps_ref, bias_ref, pad_ref, rows, width)
    u_ref[...] = u
    wide_ref[:, :, :sums] = project_rows(u, proj_ref).reshape(shards, 8, sums)
    late = tokens_ref[...].astype(F32)[0:1, :]
    room = wide_ref.shape[2] - sums
    row_ids = lax.broadcasted_iota(jnp.int32, (8, room), 0)
    block = jnp.zeros((8, room), F32)
    for p, (at, size) in enumerate(pieces(depth, room)):
        piece = late[:, at : at + size]
        if size < room:
            piece = jnp.concatenate([piece, jnp.zeros((1, room - size), F32)], axis=1)
        block = jnp.where(row_ids == p, jnp.broadcast_to(piece, (8, room)), block)
    wide_ref[:, :, sums:] = jnp.broadcast_to(block[None], (shards, 8, room))
    send_ref[...] = wide_ref[...].astype(BF16)


def late_kernel(
    got_ref, rim_ref, edge_ref, weight_hbm, taps_hbm, bias_hbm, proj_hbm,
    mix_ref, u_ref,
    wide_ref, first_ref, pad_ref, pay_ref, weight_ref, taps_ref, bias_ref, proj_ref, sems,
):
    shards, _, lanes = got_ref.shape
    depth = weight_ref.shape[0] // shards
    width = weight_ref.shape[1]
    sums = proj_ref.shape[0]
    copies = fetches(
        weight_fetches(weight_hbm, weight_ref, shards, depth)
        + [(taps_hbm, taps_ref), (bias_hbm, bias_ref), (proj_hbm, proj_ref)],
        sems,
    )
    room = lanes - sums
    wide_ref[...] = got_ref[...].astype(F32)
    for p, (at, size) in enumerate(pieces(depth, room)):
        first_ref[:, at : at + size] = wide_ref[:, p, sums : sums + size]
    total = jnp.sum(wide_ref[:, :, :sums], axis=0)
    high = total.astype(BF16).astype(F32)
    rank = mix_ref.shape[2] - 256
    coefs = sums - rank
    pay_ref[...] = jnp.zeros_like(pay_ref)
    pay_ref[:, :sums] = high
    pay_ref[:, sums : sums + coefs] = total[:, rank:] - high[:, rank:]
    pad_ref[:8, :] = rim_ref[...].astype(F32)
    pad_ref[8:, :] = edge_ref[8:, :].astype(F32)
    first = first_ref[...].astype(BF16)
    row_ids = lax.broadcasted_iota(jnp.int32, (shards, width), 0)
    acc = jnp.zeros((shards, width), F32)
    for z in range(shards):
        copies[z].wait()
        d = jnp.dot(first, weight_ref[z * depth : (z + 1) * depth, :], preferred_element_type=F32)
        acc = acc + jnp.where(row_ids == z, d, 0.0)
    for copy in copies[shards:]:
        copy.wait()
    pad_ref[8:9, :] = jnp.sum(acc, axis=0, keepdims=True).astype(BF16).astype(F32)
    u = convolve(taps_ref, bias_ref, pad_ref, 8, width)
    u_ref[...] = u
    part = project_rows(u, proj_ref)
    half = sums // 2
    late = taps_ref.shape[0]
    at = sums + coefs
    pay_ref[:late, at : at + half] = part[:late, :half]
    pay_ref[late : 2 * late, at : at + half] = part[:late, half:]
    pay = pay_ref[...].astype(BF16)
    for z in range(shards):
        mix_ref[z] = pay


def split3(x):
    a = x.astype(BF16)
    r = x - a.astype(F32)
    b = r.astype(BF16)
    c = (r - b.astype(F32)).astype(BF16)
    return a, b, c


def running_sum(x):
    rows = x.shape[0]
    row_ids = lax.broadcasted_iota(jnp.int32, (rows, rows), 0)
    col_ids = lax.broadcasted_iota(jnp.int32, (rows, rows), 1)
    lower = (row_ids >= col_ids).astype(F32).astype(BF16)
    return sum(jnp.dot(lower, p, preferred_element_type=F32) for p in split3(x)[::-1])


def state_kernel(
    mix_ref, dtw_ref, dtb_ref, alog_ref, u_ref, late_u_ref,
    step_ref, coef_ref, pay_ref,
    uf_ref, flow_ref, left_ref, bx_ref, end_ref, low_ref,
):
    shards, each, _ = mix_ref.shape
    rows, width = u_ref.shape
    rank = dtw_ref.shape[0]
    n = alog_ref.shape[0]
    sums = rank + 2 * n
    half = sums // 2
    at = sums + 2 * n
    late = each // 2
    tiles = rows // 8
    low_ref[...] = mix_ref[:, :, :rank].astype(F32).reshape(rows, rank)
    coef = mix_ref[:, :, rank:sums].astype(F32) + mix_ref[:, :, sums:at].astype(F32)
    coef_ref[...] = coef.reshape(rows, 2 * n)
    pairs = jnp.sum(mix_ref[:, :, at : at + half].astype(F32), axis=0)
    early = jnp.concatenate([pairs[:late], pairs[late:]], axis=1)
    low_ref[:late, :] = early[:, :rank]
    coef_ref[:late, :] = early[:, rank:]
    v = jnp.dot(low_ref[...].astype(BF16), dtw_ref[...], preferred_element_type=F32) + dtb_ref[...]
    step = jnp.maximum(v, 0.0) + jnp.log1p(jnp.exp(-jnp.abs(v)))
    step_ref[...] = step
    cum = running_sum(step)
    whole = cum[rows - 1 : rows, :]
    left_ref[...] = (whole - cum).reshape(tiles, 8, width)
    uf_ref[...] = u_ref[...].astype(F32)
    uf_ref[:8, :] = late_u_ref[...].astype(F32)
    flow_ref[...] = (step * uf_ref[...]).reshape(tiles, 8, width)
    b = coef_ref[:, :n]
    for i in range(n):
        bx_ref[:, i] = jnp.broadcast_to(b[:, i : i + 1], (rows, 128)).reshape(tiles, 8, 128)
    rate2 = -jnp.exp(alog_ref[...]) * LOG2E
    groups = width // 128
    for g in range(groups):
        lanes = slice(g * 128, (g + 1) * 128)
        rate_g = jnp.broadcast_to(rate2[:, None, lanes], (n, 8, 128))

        def turn(i, acc):
            grow = jnp.exp2(rate_g * left_ref[i, :, lanes][None])
            return acc + grow * (flow_ref[i, :, lanes][None] * bx_ref[i])

        acc = lax.fori_loop(0, tiles, turn, jnp.zeros((n, 8, 128), F32), unroll=2)
        hi, lo, _ = split3(whole[:, lanes])
        end_ref[g * n : (g + 1) * n, :] = jnp.sum(acc, axis=1)
        end_ref[groups * n + g : groups * n + g + 1, :] = hi.astype(F32)
        end_ref[groups * n + groups + g : groups * n + groups + g + 1, :] = lo.astype(F32)
    end = end_ref[...].astype(BF16)
    for p in range(pay_ref.shape[0]):
        pay_ref[p] = end


def local_kernel(
    coef_ref, alog_ref, u_ref, late_u_ref, step_ref, skip_ref,
    y_ref, grow_ref, bt_ref, ct_ref, cx_ref, uf_ref, flow_ref, cum_ref,
):
    rows, width = u_ref.shape
    uf_ref[...] = u_ref[...].astype(F32)
    uf_ref[:8, :] = late_u_ref[...].astype(F32)
    flow_ref[...] = (step_ref[...] * uf_ref[...]).reshape(rows // 8, 8, width)
    cum_ref[...] = running_sum(step_ref[...])
    n = alog_ref.shape[0]
    blocks = rows // 16
    b, c = coef_ref[:, :n], coef_ref[:, n:]
    rate2 = -jnp.exp(alog_ref[...]) * LOG2E
    for i in range(n):
        cx_ref[:, i] = jnp.broadcast_to(c[:, i : i + 1], (rows, 128)).reshape(blocks, 16, 128)
    b_t, c_t = b.T, c.T
    for t in range(rows):
        bt_ref[t] = jnp.broadcast_to(b_t[:, t : t + 1], (n, 128))
        ct_ref[t] = jnp.broadcast_to(c_t[:, t : t + 1], (n, 128))
    groups = width // 128

    def block_turn(i, state):
        for r in range(8):
            t = i * 8 + r
            d = step_ref[pl.ds(t, 1), :]
            f = flow_ref[i, r : r + 1, :]
            bt = jnp.concatenate([bt_ref[t]] * groups, axis=1)
            ct = jnp.concatenate([ct_ref[t]] * groups, axis=1)
            state = jnp.exp2(rate2 * d) * state + bt * f
            y_ref[pl.ds(t, 1), :] = jnp.sum(ct * state, axis=0, keepdims=True)
        return state

    lax.fori_loop(0, rows // 8, block_turn, jnp.zeros((n, width), F32))
    y_ref[...] = y_ref[...] + skip_ref[...] * uf_ref[...]

    for g in range(groups):
        lanes = slice(g * 128, (g + 1) * 128)
        rate_g = jnp.broadcast_to(rate2[:, None, lanes], (n, 16, 128))

        def fill(i, _):
            cum = cum_ref[pl.ds(pl.multiple_of(i * 16, 16), 16), lanes]
            grow_ref[i, :, :, lanes] = (cx_ref[i] * jnp.exp2(rate_g * cum[None])).astype(BF16)
            return 0

        lax.fori_loop(0, blocks, fill, 0)


def final_kernel(mine_ref, all_ref, alog_ref, y_ref, grow_ref, thr_ref, out_ref):
    rows, width = y_ref.shape
    n = alog_ref.shape[0]
    blocks = rows // 16
    peers = all_ref.shape[0]
    mine = mine_ref[0]
    rate2 = -jnp.exp(alog_ref[...]) * LOG2E

    groups = width // 128
    for g in range(groups):
        lanes = slice(g * 128, (g + 1) * 128)
        rate_g = rate2[:, lanes]

        def join(p, state):
            block = all_ref[p].astype(F32)
            at = groups * n + g
            whole = block[at : at + 1, :] + block[at + groups : at + groups + 1, :]
            longer = jnp.exp2(rate_g * whole) * state + block[g * n : (g + 1) * n, :]
            return jnp.where(p < mine, longer, state)

        entry = jnp.zeros((n, 128), F32)
        for p in range(peers - 1):
            entry = join(p, entry)
        entry_g = jnp.broadcast_to(entry[:, None, :], (n, 16, 128))
        thr = thr_ref[:, lanes]

        def turn(i, _):
            at = pl.ds(pl.multiple_of(i * 16, 16), 16)
            y = y_ref[at, lanes] + jnp.sum(grow_ref[i, :, :, lanes].astype(F32) * entry_g, axis=0)
            y_ref[at, lanes] = y / (1.0 + jnp.exp(-4.0 * (y - thr)))
            return 0

        lax.fori_loop(0, blocks, turn, 0)
    out_ref[...] = y_ref[...].astype(BF16)


def call(kernel, outs, ins, scratch=(), flops=0, specs=None, vmem=12 << 20):
    specs = specs or [VMEM] * len(ins)
    return pl.pallas_call(
        kernel,
        out_shape=outs,
        in_specs=specs,
        out_specs=jax.tree.map(lambda _: VMEM, outs),
        scratch_shapes=scratch,
        cost_estimate=pl.CostEstimate(flops=flops, bytes_accessed=flops // 64, transcendentals=0),
        compiler_params=pltpu.CompilerParams(vmem_limit_bytes=vmem),
    )(*[pltpu.with_memory_space_constraint(x, pltpu.HBM) if spec is HBM else x for x, spec in zip(ins, specs)])


def per_device(
    tokens, in_weight, conv_weight, conv_bias, proj_weight, dt_weight, dt_bias, a_log, skip_gain, threshold
):
    rows = tokens.shape[0]
    width = in_weight.shape[1]
    taps = conv_weight.shape[0]
    rank = dt_weight.shape[0]
    n = a_log.shape[0]
    shards = lax.axis_size("tp")
    peers = lax.axis_size("seq")
    sums = rank + 2 * n
    lanes = -(-sums // 128) * 128
    bias = conv_bias[None]
    proj = proj_weight.T
    held = (
        pltpu.VMEM(in_weight.shape, BF16),
        pltpu.VMEM(conv_weight.shape, F32),
        pltpu.VMEM(bias.shape, F32),
        pltpu.VMEM(proj.shape, BF16),
    )

    main = lax.all_gather(tokens[1:], "tp")
    send, edge, u = call(
        project_kernel,
        (struct((shards, 8, lanes), BF16), struct((16, width), BF16), struct((rows, width), BF16)),
        (main, tokens, in_weight, conv_weight, bias, proj),
        (pltpu.VMEM((rows + 8, width), F32), pltpu.VMEM((shards, 8, lanes), F32))
        + held
        + (pltpu.VMEM((8, tokens.shape[1]), BF16), pltpu.SemaphoreType.DMA((shards + 4,))),
        flops=1 << 29,
        specs=[VMEM] + [HBM] * 5,
    )
    rim = lax.ppermute(edge[:8], "seq", [(i, i + 1) for i in range(peers - 1)])
    got = lax.all_to_all(send, "tp", 0, 0)
    mix, late_u = call(
        late_kernel,
        (struct((shards, 8, rank + 256), BF16), struct((8, width), BF16)),
        (got, rim, edge, in_weight, conv_weight, bias, proj),
        (
            pltpu.VMEM((shards, 8, lanes), F32),
            pltpu.VMEM((shards, tokens.shape[1]), F32),
            pltpu.VMEM((16, width), F32),
            pltpu.VMEM((8, rank + 256), F32),
        )
        + held
        + (pltpu.SemaphoreType.DMA((shards + 3,)),),
        flops=1 << 28,
        specs=[VMEM] * 3 + [HBM] * 4,
    )
    mix = lax.all_to_all(mix, "tp", 0, 0)
    whole = struct((rows, width), F32)
    step, coef, pay = call(
        state_kernel,
        (whole, struct((rows, 2 * n), F32), struct((peers, (n + 2) * width // 128, 128), BF16)),
        (mix, dt_weight, dt_bias[None], a_log, u, late_u),
        (
            pltpu.VMEM((rows, width), F32),
            pltpu.VMEM((rows // 8, 8, width), F32),
            pltpu.VMEM((rows // 8, 8, width), F32),
            pltpu.VMEM((rows // 8, n, 8, 128), F32),
            pltpu.VMEM(((n + 2) * width // 128, 128), F32),
            pltpu.VMEM((rows, rank), F32),
        ),
        flops=1 << 26,
    )
    everyone = lax.all_to_all(pay, "seq", 0, 0)
    y_local, grow = call(
        local_kernel,
        (whole, struct((rows // 16, n, 16, width), BF16)),
        (coef, a_log, u, late_u, step, skip_gain[None]),
        (
            pltpu.VMEM((rows, n, 128), F32),
            pltpu.VMEM((rows, n, 128), F32),
            pltpu.VMEM((rows // 16, n, 16, 128), F32),
            pltpu.VMEM((rows, width), F32),
            pltpu.VMEM((rows // 8, 8, width), F32),
            pltpu.VMEM((rows, width), F32),
        ),
        flops=1 << 28,
    )
    mine = lax.axis_index("seq").astype(jnp.int32)[None]
    return call(
        final_kernel,
        struct((rows, width), BF16),
        (mine, everyone, a_log, y_local, grow, threshold[None]),
        flops=1 << 26,
        specs=[SMEM] + [VMEM] * 5,
    )


def solution(mesh):
    return jax.shard_map(
        per_device,
        mesh=mesh,
        in_specs=(
            P("seq", "tp"),
            P(None, "tp"),
            P(None, "tp"),
            P("tp"),
            P("tp", None),
            P(None, "tp"),
            P("tp"),
            P(None, "tp"),
            P("tp"),
            P("tp"),
        ),
        out_specs=P("seq", "tp"),
        check_vma=False,
    )
```

```python
import math

import jax
import jax.numpy as jnp
from jax import lax
from jax.experimental import pallas as pl
from jax.experimental.pallas import tpu as pltpu
from jax.sharding import PartitionSpec as P

LOG2E = math.log2(math.e)
F32 = jnp.float32
BF16 = jnp.bfloat16
VMEM = pl.BlockSpec(memory_space=pltpu.VMEM)
SMEM = pl.BlockSpec(memory_space=pltpu.SMEM)
HBM = pl.BlockSpec(memory_space=pltpu.HBM)


def struct(shape, dtype):
    return jax.ShapeDtypeStruct(shape, dtype)


def silu(v):
    return v / (1.0 + jnp.exp(-v))


def convolve(taps_ref, bias_ref, pad_ref, rows, width):
    taps = taps_ref.shape[0]
    pre = jnp.broadcast_to(bias_ref[...], (rows, width))
    for k in range(taps):
        first = 9 - taps + k
        pre = pre + taps_ref[k : k + 1, :] * pad_ref[first : first + rows, :]
    return silu(pre).astype(BF16)


def pieces(depth, room):
    return [(at, min(room, depth - at)) for at in range(0, depth, room)]


def project_rows(u, proj_ref):
    return lax.dot_general(u, proj_ref[...], (((1,), (1,)), ((), ())), preferred_element_type=F32)


AHEAD = 4
KEEP = 10


def fetches(pairs, sems):
    return [pltpu.make_async_copy(src, dst, sems.at[i]) for i, (src, dst) in enumerate(pairs)]


def weight_part(keep_ref, buf_ref, z, depth):
    if z < KEEP:
        return keep_ref.at[pl.ds(z * depth, depth)]
    return buf_ref.at[pl.ds((z - KEEP) * depth, depth)]


def weight_fetches(hbm_ref, keep_ref, buf_ref, first, shards, depth):
    return [
        (hbm_ref.at[pl.ds(z * depth, depth)], weight_part(keep_ref, buf_ref, z, depth))
        for z in range(first, shards)
    ]


def project_kernel(
    main_ref, tokens_hbm, weight_hbm, taps_hbm, bias_hbm, proj_hbm,
    send_ref, edge_ref, u_ref, keep_ref,
    pad_ref, wide_ref, weight_ref, taps_ref, bias_ref, proj_ref, tokens_ref, sems,
):
    shards, held, depth = main_ref.shape
    rows, width = u_ref.shape
    sums = proj_ref.shape[0]
    copies = fetches(
        weight_fetches(weight_hbm, keep_ref, weight_ref, 0, shards, depth)
        + [(proj_hbm, proj_ref), (taps_hbm, taps_ref), (bias_hbm, bias_ref),
           (tokens_hbm.at[pl.ds(0, 8)], tokens_ref)],
        sems,
    )
    for copy in copies[:AHEAD]:
        copy.start()
    pad_ref[:16, :] = jnp.zeros((16, width), F32)
    acc = jnp.zeros((held, width), F32)
    for z in range(shards):
        copies[z].wait()
        if z + AHEAD < len(copies):
            copies[z + AHEAD].start()
        w = weight_part(keep_ref, weight_ref, z, depth)[...]
        acc = acc + jnp.dot(main_ref[z], w, preferred_element_type=F32)
    for copy in copies[shards:]:
        copy.wait()
    pad_ref[8 + rows - held :, :] = acc.astype(BF16).astype(F32)
    edge_ref[:8, :] = pad_ref[rows : rows + 8, :].astype(BF16)
    edge_ref[8:, :] = pad_ref[8:16, :].astype(BF16)
    u = convolve(taps_ref, bias_ref, pad_ref, rows, width)
    u_ref[...] = u
    wide_ref[:, :, :sums] = project_rows(u, proj_ref).reshape(shards, 8, sums)
    late = tokens_ref[...].astype(F32)[0:1, :]
    room = wide_ref.shape[2] - sums
    row_ids = lax.broadcasted_iota(jnp.int32, (8, room), 0)
    block = jnp.zeros((8, room), F32)
    for p, (at, size) in enumerate(pieces(depth, room)):
        piece = late[:, at : at + size]
        if size < room:
            piece = jnp.concatenate([piece, jnp.zeros((1, room - size), F32)], axis=1)
        block = jnp.where(row_ids == p, jnp.broadcast_to(piece, (8, room)), block)
    wide_ref[:, :, sums:] = jnp.broadcast_to(block[None], (shards, 8, room))
    send_ref[...] = wide_ref[...].astype(BF16)


def late_kernel(
    got_ref, rim_ref, edge_ref, keep_ref, weight_hbm, taps_hbm, bias_hbm, proj_hbm,
    mix_ref, u_ref,
    wide_ref, first_ref, pad_ref, pay_ref, weight_ref, taps_ref, bias_ref, proj_ref, sems,
):
    shards, _, lanes = got_ref.shape
    depth = first_ref.shape[1]
    width = weight_ref.shape[1]
    sums = proj_ref.shape[0]
    copies = fetches(
        weight_fetches(weight_hbm, keep_ref, weight_ref, KEEP, shards, depth)
        + [(proj_hbm, proj_ref), (taps_hbm, taps_ref), (bias_hbm, bias_ref)],
        sems,
    )
    for copy in copies:
        copy.start()
    room = lanes - sums
    wide_ref[...] = got_ref[...].astype(F32)
    for p, (at, size) in enumerate(pieces(depth, room)):
        first_ref[:, at : at + size] = wide_ref[:, p, sums : sums + size]
    total = jnp.sum(wide_ref[:, :, :sums], axis=0)
    high = total.astype(BF16).astype(F32)
    rank = mix_ref.shape[2] - 256
    coefs = sums - rank
    pay_ref[...] = jnp.zeros_like(pay_ref)
    pay_ref[:, :sums] = high
    pay_ref[:, sums : sums + coefs] = total[:, rank:] - high[:, rank:]
    pad_ref[:8, :] = rim_ref[...].astype(F32)
    pad_ref[8:, :] = edge_ref[8:, :].astype(F32)
    first = first_ref[...].astype(BF16)
    row_ids = lax.broadcasted_iota(jnp.int32, (shards, width), 0)
    acc = jnp.zeros((shards, width), F32)
    for z in range(shards):
        if z >= KEEP:
            copies[z - KEEP].wait()
        w = weight_part(keep_ref, weight_ref, z, depth)[...]
        d = jnp.dot(first, w, preferred_element_type=F32)
        acc = acc + jnp.where(row_ids == z, d, 0.0)
    for copy in copies[shards - KEEP :]:
        copy.wait()
    pad_ref[8:9, :] = jnp.sum(acc, axis=0, keepdims=True).astype(BF16).astype(F32)
    u = convolve(taps_ref, bias_ref, pad_ref, 8, width)
    u_ref[...] = u
    part = project_rows(u, proj_ref)
    half = sums // 2
    late = taps_ref.shape[0]
    at = sums + coefs
    pay_ref[:late, at : at + half] = part[:late, :half]
    pay_ref[late : 2 * late, at : at + half] = part[:late, half:]
    pay = pay_ref[...].astype(BF16)
    for z in range(shards):
        mix_ref[z] = pay


def split3(x):
    a = x.astype(BF16)
    r = x - a.astype(F32)
    b = r.astype(BF16)
    c = (r - b.astype(F32)).astype(BF16)
    return a, b, c


def running_sum(x):
    rows = x.shape[0]
    row_ids = lax.broadcasted_iota(jnp.int32, (rows, rows), 0)
    col_ids = lax.broadcasted_iota(jnp.int32, (rows, rows), 1)
    lower = (row_ids >= col_ids).astype(F32).astype(BF16)
    return sum(jnp.dot(lower, p, preferred_element_type=F32) for p in split3(x)[::-1])


def state_kernel(
    mix_ref, dtw_ref, dtb_ref, alog_ref, u_ref, late_u_ref,
    step_ref, coef_ref, pay_ref,
    uf_ref, flow_ref, left_ref, bx_ref, end_ref, low_ref,
):
    shards, each, _ = mix_ref.shape
    rows, width = u_ref.shape
    rank = dtw_ref.shape[0]
    n = alog_ref.shape[0]
    sums = rank + 2 * n
    half = sums // 2
    at = sums + 2 * n
    late = each // 2
    tiles = rows // 8
    low_ref[...] = mix_ref[:, :, :rank].astype(F32).reshape(rows, rank)
    coef = mix_ref[:, :, rank:sums].astype(F32) + mix_ref[:, :, sums:at].astype(F32)
    coef_ref[...] = coef.reshape(rows, 2 * n)
    pairs = jnp.sum(mix_ref[:, :, at : at + half].astype(F32), axis=0)
    early = jnp.concatenate([pairs[:late], pairs[late:]], axis=1)
    low_ref[:late, :] = early[:, :rank]
    coef_ref[:late, :] = early[:, rank:]
    v = jnp.dot(low_ref[...].astype(BF16), dtw_ref[...], preferred_element_type=F32) + dtb_ref[...]
    step = jnp.maximum(v, 0.0) + jnp.log1p(jnp.exp(-jnp.abs(v)))
    step_ref[...] = step
    cum = running_sum(step)
    whole = cum[rows - 1 : rows, :]
    left_ref[...] = (whole - cum).reshape(tiles, 8, width)
    uf_ref[...] = u_ref[...].astype(F32)
    uf_ref[:8, :] = late_u_ref[...].astype(F32)
    flow_ref[...] = (step * uf_ref[...]).reshape(tiles, 8, width)
    b = coef_ref[:, :n]
    for i in range(n):
        bx_ref[:, i] = jnp.broadcast_to(b[:, i : i + 1], (rows, 128)).reshape(tiles, 8, 128)
    rate2 = -jnp.exp(alog_ref[...]) * LOG2E
    groups = width // 128
    for g in range(groups):
        lanes = slice(g * 128, (g + 1) * 128)
        rate_g = jnp.broadcast_to(rate2[:, None, lanes], (n, 8, 128))

        def turn(i, acc):
            grow = jnp.exp2(rate_g * left_ref[i, :, lanes][None])
            return acc + grow * (flow_ref[i, :, lanes][None] * bx_ref[i])

        acc = lax.fori_loop(0, tiles, turn, jnp.zeros((n, 8, 128), F32), unroll=2)
        hi, lo, _ = split3(whole[:, lanes])
        end_ref[g * n : (g + 1) * n, :] = jnp.sum(acc, axis=1)
        end_ref[groups * n + g : groups * n + g + 1, :] = hi.astype(F32)
        end_ref[groups * n + groups + g : groups * n + groups + g + 1, :] = lo.astype(F32)
    end = end_ref[...].astype(BF16)
    for p in range(pay_ref.shape[0]):
        pay_ref[p] = end


def local_kernel(
    coef_ref, alog_ref, u_ref, late_u_ref, step_ref, skip_ref,
    y_ref, grow_ref, bt_ref, ct_ref, cx_ref, uf_ref, flow_ref, cum_ref,
):
    rows, width = u_ref.shape
    uf_ref[...] = u_ref[...].astype(F32)
    uf_ref[:8, :] = late_u_ref[...].astype(F32)
    flow_ref[...] = (step_ref[...] * uf_ref[...]).reshape(rows // 8, 8, width)
    cum_ref[...] = running_sum(step_ref[...])
    n = alog_ref.shape[0]
    blocks = rows // 16
    b, c = coef_ref[:, :n], coef_ref[:, n:]
    rate2 = -jnp.exp(alog_ref[...]) * LOG2E
    for i in range(n):
        cx_ref[:, i] = jnp.broadcast_to(c[:, i : i + 1], (rows, 128)).reshape(blocks, 16, 128)
    b_t, c_t = b.T, c.T
    for t in range(rows):
        bt_ref[t] = jnp.broadcast_to(b_t[:, t : t + 1], (n, 128))
        ct_ref[t] = jnp.broadcast_to(c_t[:, t : t + 1], (n, 128))
    groups = width // 128

    def block_turn(i, state):
        for r in range(8):
            t = i * 8 + r
            d = step_ref[pl.ds(t, 1), :]
            f = flow_ref[i, r : r + 1, :]
            bt = jnp.concatenate([bt_ref[t]] * groups, axis=1)
            ct = jnp.concatenate([ct_ref[t]] * groups, axis=1)
            state = jnp.exp2(rate2 * d) * state + bt * f
            y_ref[pl.ds(t, 1), :] = jnp.sum(ct * state, axis=0, keepdims=True)
        return state

    lax.fori_loop(0, rows // 8, block_turn, jnp.zeros((n, width), F32))
    y_ref[...] = y_ref[...] + skip_ref[...] * uf_ref[...]

    for g in range(groups):
        lanes = slice(g * 128, (g + 1) * 128)
        rate_g = jnp.broadcast_to(rate2[:, None, lanes], (n, 16, 128))

        def fill(i, _):
            cum = cum_ref[pl.ds(pl.multiple_of(i * 16, 16), 16), lanes]
            grow_ref[i, :, :, lanes] = (cx_ref[i] * jnp.exp2(rate_g * cum[None])).astype(BF16)
            return 0

        lax.fori_loop(0, blocks, fill, 0)


def final_kernel(mine_ref, all_ref, alog_ref, y_ref, grow_ref, thr_ref, out_ref):
    rows, width = y_ref.shape
    n = alog_ref.shape[0]
    blocks = rows // 16
    peers = all_ref.shape[0]
    mine = mine_ref[0]
    rate2 = -jnp.exp(alog_ref[...]) * LOG2E

    groups = width // 128
    for g in range(groups):
        lanes = slice(g * 128, (g + 1) * 128)
        rate_g = rate2[:, lanes]

        def join(p, state):
            block = all_ref[p].astype(F32)
            at = groups * n + g
            whole = block[at : at + 1, :] + block[at + groups : at + groups + 1, :]
            longer = jnp.exp2(rate_g * whole) * state + block[g * n : (g + 1) * n, :]
            return jnp.where(p < mine, longer, state)

        entry = jnp.zeros((n, 128), F32)
        for p in range(peers - 1):
            entry = join(p, entry)
        entry_g = jnp.broadcast_to(entry[:, None, :], (n, 16, 128))
        thr = thr_ref[:, lanes]

        def turn(i, _):
            at = pl.ds(pl.multiple_of(i * 16, 16), 16)
            y = y_ref[at, lanes] + jnp.sum(grow_ref[i, :, :, lanes].astype(F32) * entry_g, axis=0)
            y_ref[at, lanes] = y / (1.0 + jnp.exp(-4.0 * (y - thr)))
            return 0

        lax.fori_loop(0, blocks, turn, 0)
    out_ref[...] = y_ref[...].astype(BF16)


def call(kernel, outs, ins, scratch=(), flops=0, specs=None, vmem=12 << 20):
    specs = specs or [VMEM] * len(ins)
    return pl.pallas_call(
        kernel,
        out_shape=outs,
        in_specs=specs,
        out_specs=jax.tree.map(lambda _: VMEM, outs),
        scratch_shapes=scratch,
        cost_estimate=pl.CostEstimate(flops=flops, bytes_accessed=flops // 64, transcendentals=0),
        compiler_params=pltpu.CompilerParams(vmem_limit_bytes=vmem),
    )(*[pltpu.with_memory_space_constraint(x, pltpu.HBM) if spec is HBM else x for x, spec in zip(ins, specs)])


def per_device(
    tokens, in_weight, conv_weight, conv_bias, proj_weight, dt_weight, dt_bias, a_log, skip_gain, threshold
):
    rows = tokens.shape[0]
    width = in_weight.shape[1]
    taps = conv_weight.shape[0]
    rank = dt_weight.shape[0]
    n = a_log.shape[0]
    shards = lax.axis_size("tp")
    peers = lax.axis_size("seq")
    sums = rank + 2 * n
    lanes = -(-sums // 128) * 128
    bias = conv_bias[None]
    proj = proj_weight.T
    kept = (KEEP * tokens.shape[1], width)
    held = (
        pltpu.VMEM((in_weight.shape[0] - kept[0], width), BF16),
        pltpu.VMEM(conv_weight.shape, F32),
        pltpu.VMEM(bias.shape, F32),
        pltpu.VMEM(proj.shape, BF16),
    )

    main = lax.all_gather(tokens[1:], "tp")
    send, edge, u, keep = call(
        project_kernel,
        (struct((shards, 8, lanes), BF16), struct((16, width), BF16), struct((rows, width), BF16),
         struct(kept, BF16)),
        (main, tokens, in_weight, conv_weight, bias, proj),
        (pltpu.VMEM((rows + 8, width), F32), pltpu.VMEM((shards, 8, lanes), F32))
        + held
        + (pltpu.VMEM((8, tokens.shape[1]), BF16), pltpu.SemaphoreType.DMA((shards + 4,))),
        flops=1 << 29,
        specs=[VMEM] + [HBM] * 5,
    )
    rim = lax.ppermute(edge[:8], "seq", [(i, i + 1) for i in range(peers - 1)])
    got = lax.all_to_all(send, "tp", 0, 0)
    mix, late_u = call(
        late_kernel,
        (struct((shards, 8, rank + 256), BF16), struct((8, width), BF16)),
        (got, rim, edge, keep, in_weight, conv_weight, bias, proj),
        (
            pltpu.VMEM((shards, 8, lanes), F32),
            pltpu.VMEM((shards, tokens.shape[1]), F32),
            pltpu.VMEM((16, width), F32),
            pltpu.VMEM((8, rank + 256), F32),
        )
        + held
        + (pltpu.SemaphoreType.DMA((shards + 3,)),),
        flops=1 << 28,
        specs=[VMEM] * 4 + [HBM] * 4,
    )
    mix = lax.all_to_all(mix, "tp", 0, 0)
    whole = struct((rows, width), F32)
    step, coef, pay = call(
        state_kernel,
        (whole, struct((rows, 2 * n), F32), struct((peers, (n + 2) * width // 128, 128), BF16)),
        (mix, dt_weight, dt_bias[None], a_log, u, late_u),
        (
            pltpu.VMEM((rows, width), F32),
            pltpu.VMEM((rows // 8, 8, width), F32),
            pltpu.VMEM((rows // 8, 8, width), F32),
            pltpu.VMEM((rows // 8, n, 8, 128), F32),
            pltpu.VMEM(((n + 2) * width // 128, 128), F32),
            pltpu.VMEM((rows, rank), F32),
        ),
        flops=1 << 26,
    )
    everyone = lax.all_to_all(pay, "seq", 0, 0)
    y_local, grow = call(
        local_kernel,
        (whole, struct((rows // 16, n, 16, width), BF16)),
        (coef, a_log, u, late_u, step, skip_gain[None]),
        (
            pltpu.VMEM((rows, n, 128), F32),
            pltpu.VMEM((rows, n, 128), F32),
            pltpu.VMEM((rows // 16, n, 16, 128), F32),
            pltpu.VMEM((rows, width), F32),
            pltpu.VMEM((rows // 8, 8, width), F32),
            pltpu.VMEM((rows, width), F32),
        ),
        flops=1 << 28,
    )
    mine = lax.axis_index("seq").astype(jnp.int32)[None]
    return call(
        final_kernel,
        struct((rows, width), BF16),
        (mine, everyone, a_log, y_local, grow, threshold[None]),
        flops=1 << 26,
        specs=[SMEM] + [VMEM] * 5,
    )


def solution(mesh):
    return jax.shard_map(
        per_device,
        mesh=mesh,
        in_specs=(
            P("seq", "tp"),
            P(None, "tp"),
            P(None, "tp"),
            P("tp"),
            P("tp", None),
            P(None, "tp"),
            P("tp"),
            P(None, "tp"),
            P("tp"),
            P("tp"),
        ),
        out_specs=P("seq", "tp"),
        check_vma=False,
    )
```

```python
import math

import jax
import jax.numpy as jnp
from jax import lax
from jax.experimental import pallas as pl
from jax.experimental.pallas import tpu as pltpu
from jax.sharding import PartitionSpec as P

LOG2E = math.log2(math.e)
F32 = jnp.float32
BF16 = jnp.bfloat16
VMEM = pl.BlockSpec(memory_space=pltpu.VMEM)
SMEM = pl.BlockSpec(memory_space=pltpu.SMEM)
HBM = pl.BlockSpec(memory_space=pltpu.HBM)


def struct(shape, dtype):
    return jax.ShapeDtypeStruct(shape, dtype)


def silu(v):
    return v / (1.0 + jnp.exp(-v))


def convolve(taps_ref, bias_ref, pad_ref, rows, width):
    taps = taps_ref.shape[0]
    pre = jnp.broadcast_to(bias_ref[...], (rows, width))
    for k in range(taps):
        first = 9 - taps + k
        pre = pre + taps_ref[k : k + 1, :] * pad_ref[first : first + rows, :]
    return silu(pre).astype(BF16)


def pieces(depth, room):
    return [(at, min(room, depth - at)) for at in range(0, depth, room)]


def project_rows(u, proj_ref):
    return lax.dot_general(u, proj_ref[...], (((1,), (1,)), ((), ())), preferred_element_type=F32)


KEEP = 12


def fetches(pairs, sems):
    return [pltpu.make_async_copy(src, dst, sems.at[i]) for i, (src, dst) in enumerate(pairs)]


def weight_part(keep_ref, buf_ref, z, depth):
    if z < KEEP:
        return keep_ref.at[pl.ds(z * depth, depth)]
    return buf_ref.at[pl.ds((z - KEEP) * depth, depth)]


def rows_kernel(tokens_hbm, out_ref, tokens_ref, sem):
    copy = pltpu.make_async_copy(tokens_hbm, tokens_ref, sem)
    copy.start()
    copy.wait()
    out_ref[...] = tokens_ref[...].astype(F32)[1:, :].astype(BF16)


def project_kernel(
    main_ref, weight_ref, tokens_hbm, taps_hbm, bias_hbm, proj_hbm,
    send_ref, edge_ref, u_ref, keep_ref,
    pad_ref, wide_ref, taps_ref, bias_ref, proj_ref, tokens_ref, sems,
):
    shards, held, depth = main_ref.shape
    rows, width = u_ref.shape
    sums = proj_ref.shape[0]
    copies = fetches(
        [(proj_hbm, proj_ref), (taps_hbm, taps_ref), (bias_hbm, bias_ref),
         (tokens_hbm.at[pl.ds(0, 8)], tokens_ref),
         (weight_ref.at[pl.ds(0, KEEP * depth)], keep_ref)],
        sems,
    )
    for copy in copies:
        copy.start()
    pad_ref[:16, :] = jnp.zeros((16, width), F32)
    acc = jnp.zeros((held, width), F32)
    for z in range(shards):
        w = weight_ref[z * depth : (z + 1) * depth, :]
        acc = acc + jnp.dot(main_ref[z], w, preferred_element_type=F32)
    for copy in copies[:4]:
        copy.wait()
    pad_ref[8 + rows - held :, :] = acc.astype(BF16).astype(F32)
    edge_ref[:8, :] = pad_ref[rows : rows + 8, :].astype(BF16)
    edge_ref[8:, :] = pad_ref[8:16, :].astype(BF16)
    u = convolve(taps_ref, bias_ref, pad_ref, rows, width)
    u_ref[...] = u
    wide_ref[:, :, :sums] = project_rows(u, proj_ref).reshape(shards, 8, sums)
    late = tokens_ref[...].astype(F32)[0:1, :]
    room = wide_ref.shape[2] - sums
    row_ids = lax.broadcasted_iota(jnp.int32, (8, room), 0)
    block = jnp.zeros((8, room), F32)
    for p, (at, size) in enumerate(pieces(depth, room)):
        piece = late[:, at : at + size]
        if size < room:
            piece = jnp.concatenate([piece, jnp.zeros((1, room - size), F32)], axis=1)
        block = jnp.where(row_ids == p, jnp.broadcast_to(piece, (8, room)), block)
    wide_ref[:, :, sums:] = jnp.broadcast_to(block[None], (shards, 8, room))
    send_ref[...] = wide_ref[...].astype(BF16)
    copies[4].wait()


def late_kernel(
    got_ref, rim_ref, edge_ref, keep_ref, weight_hbm, taps_hbm, bias_hbm, proj_hbm,
    mix_ref, u_ref,
    wide_ref, first_ref, pad_ref, pay_ref, weight_ref, taps_ref, bias_ref, proj_ref, sems,
):
    shards, _, lanes = got_ref.shape
    depth = first_ref.shape[1]
    width = weight_ref.shape[1]
    sums = proj_ref.shape[0]
    copies = fetches(
        [
            (weight_hbm.at[pl.ds(z * depth, depth)], weight_part(keep_ref, weight_ref, z, depth))
            for z in range(KEEP, shards)
        ]
        + [(proj_hbm, proj_ref), (taps_hbm, taps_ref), (bias_hbm, bias_ref)],
        sems,
    )
    for copy in copies:
        copy.start()
    room = lanes - sums
    wide_ref[...] = got_ref[...].astype(F32)
    for p, (at, size) in enumerate(pieces(depth, room)):
        first_ref[:, at : at + size] = wide_ref[:, p, sums : sums + size]
    total = jnp.sum(wide_ref[:, :, :sums], axis=0)
    high = total.astype(BF16).astype(F32)
    rank = mix_ref.shape[2] - 256
    coefs = sums - rank
    pay_ref[...] = jnp.zeros_like(pay_ref)
    pay_ref[:, :sums] = high
    pay_ref[:, sums : sums + coefs] = total[:, rank:] - high[:, rank:]
    pad_ref[:8, :] = rim_ref[...].astype(F32)
    pad_ref[8:, :] = edge_ref[8:, :].astype(F32)
    first = first_ref[...].astype(BF16)
    row_ids = lax.broadcasted_iota(jnp.int32, (shards, width), 0)
    acc = jnp.zeros((shards, width), F32)
    for z in range(shards):
        if z >= KEEP:
            copies[z - KEEP].wait()
        w = weight_part(keep_ref, weight_ref, z, depth)[...]
        d = jnp.dot(first, w, preferred_element_type=F32)
        acc = acc + jnp.where(row_ids == z, d, 0.0)
    for copy in copies[shards - KEEP :]:
        copy.wait()
    pad_ref[8:9, :] = jnp.sum(acc, axis=0, keepdims=True).astype(BF16).astype(F32)
    u = convolve(taps_ref, bias_ref, pad_ref, 8, width)
    u_ref[...] = u
    part = project_rows(u, proj_ref)
    half = sums // 2
    late = taps_ref.shape[0]
    at = sums + coefs
    pay_ref[:late, at : at + half] = part[:late, :half]
    pay_ref[late : 2 * late, at : at + half] = part[:late, half:]
    pay = pay_ref[...].astype(BF16)
    for z in range(shards):
        mix_ref[z] = pay


def split3(x):
    a = x.astype(BF16)
    r = x - a.astype(F32)
    b = r.astype(BF16)
    c = (r - b.astype(F32)).astype(BF16)
    return a, b, c


def running_sum(x):
    rows = x.shape[0]
    row_ids = lax.broadcasted_iota(jnp.int32, (rows, rows), 0)
    col_ids = lax.broadcasted_iota(jnp.int32, (rows, rows), 1)
    lower = (row_ids >= col_ids).astype(F32).astype(BF16)
    return sum(jnp.dot(lower, p, preferred_element_type=F32) for p in split3(x)[::-1])


def state_kernel(
    mix_ref, dtw_ref, dtb_ref, alog_ref, u_ref, late_u_ref,
    step_ref, coef_ref, pay_ref,
    uf_ref, flow_ref, left_ref, bx_ref, end_ref, low_ref,
):
    shards, each, _ = mix_ref.shape
    rows, width = u_ref.shape
    rank = dtw_ref.shape[0]
    n = alog_ref.shape[0]
    sums = rank + 2 * n
    half = sums // 2
    at = sums + 2 * n
    late = each // 2
    tiles = rows // 8
    low_ref[...] = mix_ref[:, :, :rank].astype(F32).reshape(rows, rank)
    coef = mix_ref[:, :, rank:sums].astype(F32) + mix_ref[:, :, sums:at].astype(F32)
    coef_ref[...] = coef.reshape(rows, 2 * n)
    pairs = jnp.sum(mix_ref[:, :, at : at + half].astype(F32), axis=0)
    early = jnp.concatenate([pairs[:late], pairs[late:]], axis=1)
    low_ref[:late, :] = early[:, :rank]
    coef_ref[:late, :] = early[:, rank:]
    v = jnp.dot(low_ref[...].astype(BF16), dtw_ref[...], preferred_element_type=F32) + dtb_ref[...]
    step = jnp.maximum(v, 0.0) + jnp.log1p(jnp.exp(-jnp.abs(v)))
    step_ref[...] = step
    cum = running_sum(step)
    whole = cum[rows - 1 : rows, :]
    left_ref[...] = (whole - cum).reshape(tiles, 8, width)
    uf_ref[...] = u_ref[...].astype(F32)
    uf_ref[:8, :] = late_u_ref[...].astype(F32)
    flow_ref[...] = (step * uf_ref[...]).reshape(tiles, 8, width)
    b = coef_ref[:, :n]
    for i in range(n):
        bx_ref[:, i] = jnp.broadcast_to(b[:, i : i + 1], (rows, 128)).reshape(tiles, 8, 128)
    rate2 = -jnp.exp(alog_ref[...]) * LOG2E
    groups = width // 128
    for g in range(groups):
        lanes = slice(g * 128, (g + 1) * 128)
        rate_g = jnp.broadcast_to(rate2[:, None, lanes], (n, 8, 128))

        def turn(i, acc):
            grow = jnp.exp2(rate_g * left_ref[i, :, lanes][None])
            return acc + grow * (flow_ref[i, :, lanes][None] * bx_ref[i])

        acc = lax.fori_loop(0, tiles, turn, jnp.zeros((n, 8, 128), F32), unroll=2)
        hi, lo, _ = split3(whole[:, lanes])
        end_ref[g * n : (g + 1) * n, :] = jnp.sum(acc, axis=1)
        end_ref[groups * n + g : groups * n + g + 1, :] = hi.astype(F32)
        end_ref[groups * n + groups + g : groups * n + groups + g + 1, :] = lo.astype(F32)
    end = end_ref[...].astype(BF16)
    for p in range(pay_ref.shape[0]):
        pay_ref[p] = end


def local_kernel(
    coef_ref, alog_ref, u_ref, late_u_ref, step_ref, skip_ref,
    y_ref, grow_ref, bt_ref, ct_ref, cx_ref, uf_ref, flow_ref, cum_ref,
):
    rows, width = u_ref.shape
    uf_ref[...] = u_ref[...].astype(F32)
    uf_ref[:8, :] = late_u_ref[...].astype(F32)
    flow_ref[...] = (step_ref[...] * uf_ref[...]).reshape(rows // 8, 8, width)
    cum_ref[...] = running_sum(step_ref[...])
    n = alog_ref.shape[0]
    blocks = rows // 16
    b, c = coef_ref[:, :n], coef_ref[:, n:]
    rate2 = -jnp.exp(alog_ref[...]) * LOG2E
    for i in range(n):
        cx_ref[:, i] = jnp.broadcast_to(c[:, i : i + 1], (rows, 128)).reshape(blocks, 16, 128)
    b_t, c_t = b.T, c.T
    for t in range(rows):
        bt_ref[t] = jnp.broadcast_to(b_t[:, t : t + 1], (n, 128))
        ct_ref[t] = jnp.broadcast_to(c_t[:, t : t + 1], (n, 128))
    groups = width // 128

    def block_turn(i, state):
        for r in range(8):
            t = i * 8 + r
            d = step_ref[pl.ds(t, 1), :]
            f = flow_ref[i, r : r + 1, :]
            bt = jnp.concatenate([bt_ref[t]] * groups, axis=1)
            ct = jnp.concatenate([ct_ref[t]] * groups, axis=1)
            state = jnp.exp2(rate2 * d) * state + bt * f
            y_ref[pl.ds(t, 1), :] = jnp.sum(ct * state, axis=0, keepdims=True)
        return state

    lax.fori_loop(0, rows // 8, block_turn, jnp.zeros((n, width), F32))
    y_ref[...] = y_ref[...] + skip_ref[...] * uf_ref[...]

    for g in range(groups):
        lanes = slice(g * 128, (g + 1) * 128)
        rate_g = jnp.broadcast_to(rate2[:, None, lanes], (n, 16, 128))

        def fill(i, _):
            cum = cum_ref[pl.ds(pl.multiple_of(i * 16, 16), 16), lanes]
            grow_ref[i, :, :, lanes] = (cx_ref[i] * jnp.exp2(rate_g * cum[None])).astype(BF16)
            return 0

        lax.fori_loop(0, blocks, fill, 0)


def final_kernel(mine_ref, all_ref, alog_ref, y_ref, grow_ref, thr_ref, out_ref):
    rows, width = y_ref.shape
    n = alog_ref.shape[0]
    blocks = rows // 16
    peers = all_ref.shape[0]
    mine = mine_ref[0]
    rate2 = -jnp.exp(alog_ref[...]) * LOG2E

    groups = width // 128
    for g in range(groups):
        lanes = slice(g * 128, (g + 1) * 128)
        rate_g = rate2[:, lanes]

        def join(p, state):
            block = all_ref[p].astype(F32)
            at = groups * n + g
            whole = block[at : at + 1, :] + block[at + groups : at + groups + 1, :]
            longer = jnp.exp2(rate_g * whole) * state + block[g * n : (g + 1) * n, :]
            return jnp.where(p < mine, longer, state)

        entry = jnp.zeros((n, 128), F32)
        for p in range(peers - 1):
            entry = join(p, entry)
        entry_g = jnp.broadcast_to(entry[:, None, :], (n, 16, 128))
        thr = thr_ref[:, lanes]

        def turn(i, _):
            at = pl.ds(pl.multiple_of(i * 16, 16), 16)
            y = y_ref[at, lanes] + jnp.sum(grow_ref[i, :, :, lanes].astype(F32) * entry_g, axis=0)
            y_ref[at, lanes] = y / (1.0 + jnp.exp(-4.0 * (y - thr)))
            return 0

        lax.fori_loop(0, blocks, turn, 0)
    out_ref[...] = y_ref[...].astype(BF16)


def call(kernel, outs, ins, scratch=(), flops=0, specs=None, vmem=12 << 20):
    specs = specs or [VMEM] * len(ins)
    return pl.pallas_call(
        kernel,
        out_shape=outs,
        in_specs=specs,
        out_specs=jax.tree.map(lambda _: VMEM, outs),
        scratch_shapes=scratch,
        cost_estimate=pl.CostEstimate(flops=flops, bytes_accessed=flops // 64, transcendentals=0),
        compiler_params=pltpu.CompilerParams(vmem_limit_bytes=vmem),
    )(*[pltpu.with_memory_space_constraint(x, pltpu.HBM) if spec is HBM else x for x, spec in zip(ins, specs)])


def per_device(
    tokens, in_weight, conv_weight, conv_bias, proj_weight, dt_weight, dt_bias, a_log, skip_gain, threshold
):
    rows = tokens.shape[0]
    width = in_weight.shape[1]
    taps = conv_weight.shape[0]
    rank = dt_weight.shape[0]
    n = a_log.shape[0]
    shards = lax.axis_size("tp")
    peers = lax.axis_size("seq")
    sums = rank + 2 * n
    lanes = -(-sums // 128) * 128
    bias = conv_bias[None]
    proj = proj_weight.T
    kept = (KEEP * tokens.shape[1], width)
    held = (
        pltpu.VMEM(conv_weight.shape, F32),
        pltpu.VMEM(bias.shape, F32),
        pltpu.VMEM(proj.shape, BF16),
    )

    most = call(
        rows_kernel,
        struct((rows - 1, tokens.shape[1]), BF16),
        (tokens,),
        (pltpu.VMEM(tokens.shape, BF16), pltpu.SemaphoreType.DMA),
        flops=1 << 34,
        specs=[HBM],
    )
    main = lax.all_gather(most, "tp")
    send, edge, u, keep = call(
        project_kernel,
        (struct((shards, 8, lanes), BF16), struct((16, width), BF16), struct((rows, width), BF16),
         struct(kept, BF16)),
        (main, in_weight, tokens, conv_weight, bias, proj),
        (pltpu.VMEM((rows + 8, width), F32), pltpu.VMEM((shards, 8, lanes), F32))
        + held
        + (pltpu.VMEM((8, tokens.shape[1]), BF16), pltpu.SemaphoreType.DMA((5,))),
        flops=1 << 29,
        specs=[VMEM] * 2 + [HBM] * 4,
    )
    rim = lax.ppermute(edge[:8], "seq", [(i, i + 1) for i in range(peers - 1)])
    got = lax.all_to_all(send, "tp", 0, 0)
    mix, late_u = call(
        late_kernel,
        (struct((shards, 8, rank + 256), BF16), struct((8, width), BF16)),
        (got, rim, edge, keep, in_weight, conv_weight, bias, proj),
        (
            pltpu.VMEM((shards, 8, lanes), F32),
            pltpu.VMEM((shards, tokens.shape[1]), F32),
            pltpu.VMEM((16, width), F32),
            pltpu.VMEM((8, rank + 256), F32),
        )
        + (pltpu.VMEM((in_weight.shape[0] - kept[0], width), BF16),)
        + held
        + (pltpu.SemaphoreType.DMA((shards + 3,)),),
        flops=1 << 28,
        specs=[VMEM] * 4 + [HBM] * 4,
    )
    mix = lax.all_to_all(mix, "tp", 0, 0)
    whole = struct((rows, width), F32)
    step, coef, pay = call(
        state_kernel,
        (whole, struct((rows, 2 * n), F32), struct((peers, (n + 2) * width // 128, 128), BF16)),
        (mix, dt_weight, dt_bias[None], a_log, u, late_u),
        (
            pltpu.VMEM((rows, width), F32),
            pltpu.VMEM((rows // 8, 8, width), F32),
            pltpu.VMEM((rows // 8, 8, width), F32),
            pltpu.VMEM((rows // 8, n, 8, 128), F32),
            pltpu.VMEM(((n + 2) * width // 128, 128), F32),
            pltpu.VMEM((rows, rank), F32),
        ),
        flops=1 << 26,
    )
    everyone = lax.all_to_all(pay, "seq", 0, 0)
    y_local, grow = call(
        local_kernel,
        (whole, struct((rows // 16, n, 16, width), BF16)),
        (coef, a_log, u, late_u, step, skip_gain[None]),
        (
            pltpu.VMEM((rows, n, 128), F32),
            pltpu.VMEM((rows, n, 128), F32),
            pltpu.VMEM((rows // 16, n, 16, 128), F32),
            pltpu.VMEM((rows, width), F32),
            pltpu.VMEM((rows // 8, 8, width), F32),
            pltpu.VMEM((rows, width), F32),
        ),
        flops=1 << 28,
    )
    mine = lax.axis_index("seq").astype(jnp.int32)[None]
    return call(
        final_kernel,
        struct((rows, width), BF16),
        (mine, everyone, a_log, y_local, grow, threshold[None]),
        flops=1 << 26,
        specs=[SMEM] + [VMEM] * 5,
    )


def solution(mesh):
    return jax.shard_map(
        per_device,
        mesh=mesh,
        in_specs=(
            P("seq", "tp"),
            P(None, "tp"),
            P(None, "tp"),
            P("tp"),
            P("tp", None),
            P(None, "tp"),
            P("tp"),
            P(None, "tp"),
            P("tp"),
            P("tp"),
        ),
        out_specs=P("seq", "tp"),
        check_vma=False,
    )
```

```python
import math

import jax
import jax.numpy as jnp
from jax import lax
from jax.experimental import pallas as pl
from jax.experimental.pallas import tpu as pltpu
from jax.sharding import PartitionSpec as P

LOG2E = math.log2(math.e)
F32 = jnp.float32
BF16 = jnp.bfloat16
VMEM = pl.BlockSpec(memory_space=pltpu.VMEM)
SMEM = pl.BlockSpec(memory_space=pltpu.SMEM)
HBM = pl.BlockSpec(memory_space=pltpu.HBM)


def struct(shape, dtype):
    return jax.ShapeDtypeStruct(shape, dtype)


def silu(v):
    return v / (1.0 + jnp.exp(-v))


def convolve(taps_ref, bias_ref, pad_ref, rows, width):
    taps = taps_ref.shape[0]
    pre = jnp.broadcast_to(bias_ref[...], (rows, width))
    for k in range(taps):
        first = 9 - taps + k
        pre = pre + taps_ref[k : k + 1, :] * pad_ref[first : first + rows, :]
    return silu(pre).astype(BF16)


def pieces(depth, room):
    return [(at, min(room, depth - at)) for at in range(0, depth, room)]


def project_rows(u, proj_ref):
    return lax.dot_general(u, proj_ref[...], (((1,), (1,)), ((), ())), preferred_element_type=F32)


KEEP = 12


def fetches(pairs, sems):
    return [pltpu.make_async_copy(src, dst, sems.at[i]) for i, (src, dst) in enumerate(pairs)]


def weight_part(keep_ref, buf_ref, z, depth):
    if z < KEEP:
        return keep_ref.at[pl.ds(z * depth, depth)]
    return buf_ref.at[pl.ds((z - KEEP) * depth, depth)]


def rows_kernel(tokens_hbm, out_ref, tokens_ref, sem):
    copy = pltpu.make_async_copy(tokens_hbm, tokens_ref, sem)
    copy.start()
    copy.wait()
    out_ref[...] = tokens_ref[...].astype(F32)[1:, :].astype(BF16)


def project_kernel(
    main_ref, weight_ref, tokens_hbm, taps_hbm, bias_hbm, proj_hbm,
    send_ref, edge_ref, u_ref, keep_ref,
    pad_ref, wide_ref, taps_ref, bias_ref, proj_ref, tokens_ref, sems,
):
    shards, held, depth = main_ref.shape
    rows, width = u_ref.shape
    sums = proj_ref.shape[0]
    copies = fetches(
        [(proj_hbm, proj_ref), (taps_hbm, taps_ref), (bias_hbm, bias_ref),
         (tokens_hbm.at[pl.ds(0, 8)], tokens_ref),
         (weight_ref.at[pl.ds(0, KEEP * depth)], keep_ref)],
        sems,
    )
    for copy in copies:
        copy.start()
    pad_ref[:16, :] = jnp.zeros((16, width), F32)
    acc = jnp.zeros((held, width), F32)
    for z in range(shards):
        w = weight_ref[z * depth : (z + 1) * depth, :]
        acc = acc + jnp.dot(main_ref[z], w, preferred_element_type=F32)
    for copy in copies[:4]:
        copy.wait()
    pad_ref[8 + rows - held :, :] = acc.astype(BF16).astype(F32)
    edge_ref[:8, :] = pad_ref[rows : rows + 8, :].astype(BF16)
    edge_ref[8:, :] = pad_ref[8:16, :].astype(BF16)
    u = convolve(taps_ref, bias_ref, pad_ref, rows, width)
    u_ref[...] = u
    wide_ref[:, :, :sums] = project_rows(u, proj_ref).reshape(shards, 8, sums)
    late = tokens_ref[...].astype(F32)[0:1, :]
    room = wide_ref.shape[2] - sums
    row_ids = lax.broadcasted_iota(jnp.int32, (8, room), 0)
    block = jnp.zeros((8, room), F32)
    for p, (at, size) in enumerate(pieces(depth, room)):
        piece = late[:, at : at + size]
        if size < room:
            piece = jnp.concatenate([piece, jnp.zeros((1, room - size), F32)], axis=1)
        block = jnp.where(row_ids == p, jnp.broadcast_to(piece, (8, room)), block)
    wide_ref[:, :, sums:] = jnp.broadcast_to(block[None], (shards, 8, room))
    send_ref[...] = wide_ref[...].astype(BF16)
    copies[4].wait()


def late_kernel(
    got_ref, rim_ref, edge_ref, keep_ref, weight_hbm, taps_hbm, bias_hbm, proj_hbm,
    mix_ref, u_ref,
    wide_ref, first_ref, pad_ref, pay_ref, weight_ref, taps_ref, bias_ref, proj_ref, sems,
):
    shards, _, lanes = got_ref.shape
    depth = first_ref.shape[1]
    width = weight_ref.shape[1]
    sums = proj_ref.shape[0]
    copies = fetches(
        [
            (weight_hbm.at[pl.ds(z * depth, depth)], weight_part(keep_ref, weight_ref, z, depth))
            for z in range(KEEP, shards)
        ]
        + [(proj_hbm, proj_ref), (taps_hbm, taps_ref), (bias_hbm, bias_ref)],
        sems,
    )
    for copy in copies:
        copy.start()
    room = lanes - sums
    wide_ref[...] = got_ref[...].astype(F32)
    for p, (at, size) in enumerate(pieces(depth, room)):
        first_ref[:, at : at + size] = wide_ref[:, p, sums : sums + size]
    total = jnp.sum(wide_ref[:, :, :sums], axis=0)
    high = total.astype(BF16).astype(F32)
    rank = mix_ref.shape[2] - 256
    coefs = sums - rank
    pay_ref[...] = jnp.zeros_like(pay_ref)
    pay_ref[:, :sums] = high
    pay_ref[:, sums : sums + coefs] = total[:, rank:] - high[:, rank:]
    pad_ref[:8, :] = rim_ref[...].astype(F32)
    pad_ref[8:, :] = edge_ref[8:, :].astype(F32)
    first = first_ref[...].astype(BF16)
    row_ids = lax.broadcasted_iota(jnp.int32, (shards, width), 0)
    acc = jnp.zeros((shards, width), F32)
    for z in range(shards):
        if z >= KEEP:
            copies[z - KEEP].wait()
        w = weight_part(keep_ref, weight_ref, z, depth)[...]
        d = jnp.dot(first, w, preferred_element_type=F32)
        acc = acc + jnp.where(row_ids == z, d, 0.0)
    for copy in copies[shards - KEEP :]:
        copy.wait()
    pad_ref[8:9, :] = jnp.sum(acc, axis=0, keepdims=True).astype(BF16).astype(F32)
    u = convolve(taps_ref, bias_ref, pad_ref, 8, width)
    u_ref[...] = u
    part = project_rows(u, proj_ref)
    half = sums // 2
    late = taps_ref.shape[0]
    at = sums + coefs
    pay_ref[:late, at : at + half] = part[:late, :half]
    pay_ref[late : 2 * late, at : at + half] = part[:late, half:]
    pay = pay_ref[...].astype(BF16)
    for z in range(shards):
        mix_ref[z] = pay


def split3(x):
    a = x.astype(BF16)
    r = x - a.astype(F32)
    b = r.astype(BF16)
    c = (r - b.astype(F32)).astype(BF16)
    return a, b, c


def running_sum(x):
    rows = x.shape[0]
    row_ids = lax.broadcasted_iota(jnp.int32, (rows, rows), 0)
    col_ids = lax.broadcasted_iota(jnp.int32, (rows, rows), 1)
    lower = (row_ids >= col_ids).astype(F32).astype(BF16)
    return sum(jnp.dot(lower, p, preferred_element_type=F32) for p in split3(x)[::-1])


def state_kernel(
    mix_ref, dtw_ref, dtb_ref, alog_ref, u_ref, late_u_ref,
    step_ref, coef_ref, pay_hbm,
    uf_ref, flow_ref, left_ref, bx_ref, end_ref, low_ref, pack_ref, sems,
):
    shards, each, _ = mix_ref.shape
    rows, width = u_ref.shape
    rank = dtw_ref.shape[0]
    n = alog_ref.shape[0]
    sums = rank + 2 * n
    half = sums // 2
    at = sums + 2 * n
    late = each // 2
    tiles = rows // 8
    low_ref[...] = mix_ref[:, :, :rank].astype(F32).reshape(rows, rank)
    coef = mix_ref[:, :, rank:sums].astype(F32) + mix_ref[:, :, sums:at].astype(F32)
    coef_ref[...] = coef.reshape(rows, 2 * n)
    pairs = jnp.sum(mix_ref[:, :, at : at + half].astype(F32), axis=0)
    early = jnp.concatenate([pairs[:late], pairs[late:]], axis=1)
    low_ref[:late, :] = early[:, :rank]
    coef_ref[:late, :] = early[:, rank:]
    v = jnp.dot(low_ref[...].astype(BF16), dtw_ref[...], preferred_element_type=F32) + dtb_ref[...]
    step = jnp.maximum(v, 0.0) + jnp.log1p(jnp.exp(-jnp.abs(v)))
    step_ref[...] = step
    cum = running_sum(step)
    whole = cum[rows - 1 : rows, :]
    left_ref[...] = (whole - cum).reshape(tiles, 8, width)
    uf_ref[...] = u_ref[...].astype(F32)
    uf_ref[:8, :] = late_u_ref[...].astype(F32)
    flow_ref[...] = (step * uf_ref[...]).reshape(tiles, 8, width)
    b = coef_ref[:, :n]
    for i in range(n):
        bx_ref[:, i] = jnp.broadcast_to(b[:, i : i + 1], (rows, 128)).reshape(tiles, 8, 128)
    rate2 = -jnp.exp(alog_ref[...]) * LOG2E
    groups = width // 128
    for g in range(groups):
        lanes = slice(g * 128, (g + 1) * 128)
        rate_g = jnp.broadcast_to(rate2[:, None, lanes], (n, 8, 128))

        def turn(i, acc):
            grow = jnp.exp2(rate_g * left_ref[i, :, lanes][None])
            return acc + grow * (flow_ref[i, :, lanes][None] * bx_ref[i])

        acc = lax.fori_loop(0, tiles, turn, jnp.zeros((n, 8, 128), F32), unroll=tiles)
        hi, lo, _ = split3(whole[:, lanes])
        end_ref[g * n : (g + 1) * n, :] = jnp.sum(acc, axis=1)
        end_ref[groups * n + g : groups * n + g + 1, :] = hi.astype(F32)
        end_ref[groups * n + groups + g : groups * n + groups + g + 1, :] = lo.astype(F32)
    pack_ref[...] = end_ref[...].astype(BF16)
    copies = [
        pltpu.make_async_copy(pack_ref, pay_hbm.at[p], sems.at[p]) for p in range(pay_hbm.shape[0])
    ]
    for copy in copies:
        copy.start()
    for copy in copies:
        copy.wait()


def local_kernel(
    coef_ref, alog_ref, u_ref, late_u_ref, step_ref, skip_ref,
    y_ref, grow_ref, bt_ref, ct_ref, cx_ref, uf_ref, flow_ref, cum_ref,
):
    rows, width = u_ref.shape
    uf_ref[...] = u_ref[...].astype(F32)
    uf_ref[:8, :] = late_u_ref[...].astype(F32)
    flow_ref[...] = (step_ref[...] * uf_ref[...]).reshape(rows // 8, 8, width)
    cum_ref[...] = running_sum(step_ref[...])
    n = alog_ref.shape[0]
    blocks = rows // 16
    b, c = coef_ref[:, :n], coef_ref[:, n:]
    rate2 = -jnp.exp(alog_ref[...]) * LOG2E
    for i in range(n):
        cx_ref[:, i] = jnp.broadcast_to(c[:, i : i + 1], (rows, 128)).reshape(blocks, 16, 128)
    b_t, c_t = b.T, c.T
    for t in range(rows):
        bt_ref[t] = jnp.broadcast_to(b_t[:, t : t + 1], (n, 128))
        ct_ref[t] = jnp.broadcast_to(c_t[:, t : t + 1], (n, 128))
    groups = width // 128

    def block_turn(i, state):
        for r in range(8):
            t = i * 8 + r
            d = step_ref[pl.ds(t, 1), :]
            f = flow_ref[i, r : r + 1, :]
            bt = jnp.concatenate([bt_ref[t]] * groups, axis=1)
            ct = jnp.concatenate([ct_ref[t]] * groups, axis=1)
            state = jnp.exp2(rate2 * d) * state + bt * f
            y_ref[pl.ds(t, 1), :] = jnp.sum(ct * state, axis=0, keepdims=True)
        return state

    lax.fori_loop(0, rows // 8, block_turn, jnp.zeros((n, width), F32))
    y_ref[...] = y_ref[...] + skip_ref[...] * uf_ref[...]

    for g in range(groups):
        lanes = slice(g * 128, (g + 1) * 128)
        rate_g = jnp.broadcast_to(rate2[:, None, lanes], (n, 16, 128))

        def fill(i, _):
            cum = cum_ref[pl.ds(pl.multiple_of(i * 16, 16), 16), lanes]
            grow_ref[i, :, :, lanes] = (cx_ref[i] * jnp.exp2(rate_g * cum[None])).astype(BF16)
            return 0

        lax.fori_loop(0, blocks, fill, 0)


def final_kernel(mine_ref, all_ref, alog_ref, y_ref, grow_ref, thr_ref, out_ref):
    rows, width = y_ref.shape
    n = alog_ref.shape[0]
    blocks = rows // 16
    peers = all_ref.shape[0]
    mine = mine_ref[0]
    rate2 = -jnp.exp(alog_ref[...]) * LOG2E

    groups = width // 128
    for g in range(groups):
        lanes = slice(g * 128, (g + 1) * 128)
        rate_g = rate2[:, lanes]

        def join(p, state):
            block = all_ref[p].astype(F32)
            at = groups * n + g
            whole = block[at : at + 1, :] + block[at + groups : at + groups + 1, :]
            longer = jnp.exp2(rate_g * whole) * state + block[g * n : (g + 1) * n, :]
            return jnp.where(p < mine, longer, state)

        entry = jnp.zeros((n, 128), F32)
        for p in range(peers - 1):
            entry = join(p, entry)
        entry_g = jnp.broadcast_to(entry[:, None, :], (n, 16, 128))
        thr = thr_ref[:, lanes]

        def turn(i, _):
            at = pl.ds(pl.multiple_of(i * 16, 16), 16)
            y = y_ref[at, lanes] + jnp.sum(grow_ref[i, :, :, lanes].astype(F32) * entry_g, axis=0)
            out_ref[at, lanes] = (y / (1.0 + jnp.exp(-4.0 * (y - thr)))).astype(BF16)
            return 0

        lax.fori_loop(0, blocks, turn, 0, unroll=blocks)


def call(kernel, outs, ins, scratch=(), flops=0, specs=None, vmem=12 << 20, outs_in=None):
    specs = specs or [VMEM] * len(ins)
    return pl.pallas_call(
        kernel,
        out_shape=outs,
        in_specs=specs,
        out_specs=outs_in or jax.tree.map(lambda _: VMEM, outs),
        scratch_shapes=scratch,
        cost_estimate=pl.CostEstimate(flops=flops, bytes_accessed=flops // 64, transcendentals=0),
        compiler_params=pltpu.CompilerParams(vmem_limit_bytes=vmem),
    )(*[pltpu.with_memory_space_constraint(x, pltpu.HBM) if spec is HBM else x for x, spec in zip(ins, specs)])


def per_device(
    tokens, in_weight, conv_weight, conv_bias, proj_weight, dt_weight, dt_bias, a_log, skip_gain, threshold
):
    rows = tokens.shape[0]
    width = in_weight.shape[1]
    taps = conv_weight.shape[0]
    rank = dt_weight.shape[0]
    n = a_log.shape[0]
    shards = lax.axis_size("tp")
    peers = lax.axis_size("seq")
    sums = rank + 2 * n
    lanes = -(-sums // 128) * 128
    bias = conv_bias[None]
    proj = proj_weight.T
    kept = (KEEP * tokens.shape[1], width)
    held = (
        pltpu.VMEM(conv_weight.shape, F32),
        pltpu.VMEM(bias.shape, F32),
        pltpu.VMEM(proj.shape, BF16),
    )

    most = call(
        rows_kernel,
        struct((rows - 1, tokens.shape[1]), BF16),
        (tokens,),
        (pltpu.VMEM(tokens.shape, BF16), pltpu.SemaphoreType.DMA),
        flops=1 << 34,
        specs=[HBM],
    )
    main = lax.all_gather(most, "tp")
    send, edge, u, keep = call(
        project_kernel,
        (struct((shards, 8, lanes), BF16), struct((16, width), BF16), struct((rows, width), BF16),
         struct(kept, BF16)),
        (main, in_weight, tokens, conv_weight, bias, proj),
        (pltpu.VMEM((rows + 8, width), F32), pltpu.VMEM((shards, 8, lanes), F32))
        + held
        + (pltpu.VMEM((8, tokens.shape[1]), BF16), pltpu.SemaphoreType.DMA((5,))),
        flops=1 << 29,
        specs=[VMEM] * 2 + [HBM] * 4,
    )
    rim = lax.ppermute(edge[:8], "seq", [(i, i + 1) for i in range(peers - 1)])
    got = lax.all_to_all(send, "tp", 0, 0)
    mix, late_u = call(
        late_kernel,
        (struct((shards, 8, rank + 256), BF16), struct((8, width), BF16)),
        (got, rim, edge, keep, in_weight, conv_weight, bias, proj),
        (
            pltpu.VMEM((shards, 8, lanes), F32),
            pltpu.VMEM((shards, tokens.shape[1]), F32),
            pltpu.VMEM((16, width), F32),
            pltpu.VMEM((8, rank + 256), F32),
        )
        + (pltpu.VMEM((in_weight.shape[0] - kept[0], width), BF16),)
        + held
        + (pltpu.SemaphoreType.DMA((shards + 3,)),),
        flops=1 << 28,
        specs=[VMEM] * 4 + [HBM] * 4,
    )
    mix = lax.all_to_all(mix, "tp", 0, 0)
    whole = struct((rows, width), F32)
    step, coef, pay = call(
        state_kernel,
        (whole, struct((rows, 2 * n), F32), struct((peers, (n + 2) * width // 128, 128), BF16)),
        (mix, dt_weight, dt_bias[None], a_log, u, late_u),
        (
            pltpu.VMEM((rows, width), F32),
            pltpu.VMEM((rows // 8, 8, width), F32),
            pltpu.VMEM((rows // 8, 8, width), F32),
            pltpu.VMEM((rows // 8, n, 8, 128), F32),
            pltpu.VMEM(((n + 2) * width // 128, 128), F32),
            pltpu.VMEM((rows, rank), F32),
            pltpu.VMEM(((n + 2) * width // 128, 128), BF16),
            pltpu.SemaphoreType.DMA((peers,)),
        ),
        flops=1 << 26,
        outs_in=(VMEM, VMEM, HBM),
    )
    everyone = lax.all_to_all(pay, "seq", 0, 0)
    y_local, grow = call(
        local_kernel,
        (whole, struct((rows // 16, n, 16, width), BF16)),
        (coef, a_log, u, late_u, step, skip_gain[None]),
        (
            pltpu.VMEM((rows, n, 128), F32),
            pltpu.VMEM((rows, n, 128), F32),
            pltpu.VMEM((rows // 16, n, 16, 128), F32),
            pltpu.VMEM((rows, width), F32),
            pltpu.VMEM((rows // 8, 8, width), F32),
            pltpu.VMEM((rows, width), F32),
        ),
        flops=1 << 28,
    )
    mine = lax.axis_index("seq").astype(jnp.int32)[None]
    return call(
        final_kernel,
        struct((rows, width), BF16),
        (mine, everyone, a_log, y_local, grow, threshold[None]),
        flops=1 << 26,
        specs=[SMEM] + [VMEM] * 5,
    )


def solution(mesh):
    return jax.shard_map(
        per_device,
        mesh=mesh,
        in_specs=(
            P("seq", "tp"),
            P(None, "tp"),
            P(None, "tp"),
            P("tp"),
            P("tp", None),
            P(None, "tp"),
            P("tp"),
            P(None, "tp"),
            P("tp"),
            P("tp"),
        ),
        out_specs=P("seq", "tp"),
        check_vma=False,
    )
```

```python
import math

import jax
import jax.numpy as jnp
from jax import lax
from jax.experimental import pallas as pl
from jax.experimental.pallas import tpu as pltpu
from jax.sharding import PartitionSpec as P

LOG2E = math.log2(math.e)
F32 = jnp.float32
BF16 = jnp.bfloat16
VMEM = pl.BlockSpec(memory_space=pltpu.VMEM)
SMEM = pl.BlockSpec(memory_space=pltpu.SMEM)
HBM = pl.BlockSpec(memory_space=pltpu.HBM)


def struct(shape, dtype):
    return jax.ShapeDtypeStruct(shape, dtype)


def silu(v):
    return v / (1.0 + jnp.exp(-v))


def convolve(taps_ref, bias_ref, pad_ref, rows, width):
    taps = taps_ref.shape[0]
    pre = jnp.broadcast_to(bias_ref[...], (rows, width))
    for k in range(taps):
        first = 9 - taps + k
        pre = pre + taps_ref[k : k + 1, :] * pad_ref[first : first + rows, :]
    return silu(pre).astype(BF16)


def pieces(depth, room):
    return [(at, min(room, depth - at)) for at in range(0, depth, room)]


def project_rows(u, proj_ref):
    return lax.dot_general(u, proj_ref[...], (((1,), (1,)), ((), ())), preferred_element_type=F32)


KEEP = 12


def fetches(pairs, sems):
    return [pltpu.make_async_copy(src, dst, sems.at[i]) for i, (src, dst) in enumerate(pairs)]


def weight_part(keep_ref, buf_ref, z, depth):
    if z < KEEP:
        return keep_ref.at[pl.ds(z * depth, depth)]
    return buf_ref.at[pl.ds((z - KEEP) * depth, depth)]


def rows_kernel(tokens_hbm, out_ref, tokens_ref, sem):
    copy = pltpu.make_async_copy(tokens_hbm, tokens_ref, sem)
    copy.start()
    copy.wait()
    out_ref[...] = tokens_ref[...].astype(F32)[1:, :].astype(BF16)


def project_kernel(
    main_ref, weight_ref, tokens_hbm, taps_hbm, bias_hbm, proj_hbm,
    send_ref, edge_ref, u_ref, keep_ref,
    pad_ref, wide_ref, taps_ref, bias_ref, proj_ref, tokens_ref, sems,
):
    shards, held, depth = main_ref.shape
    rows, width = u_ref.shape
    sums = proj_ref.shape[0]
    copies = fetches(
        [(proj_hbm, proj_ref), (taps_hbm, taps_ref), (bias_hbm, bias_ref),
         (tokens_hbm.at[pl.ds(0, 8)], tokens_ref),
         (weight_ref.at[pl.ds(0, KEEP * depth)], keep_ref)],
        sems,
    )
    for copy in copies:
        copy.start()
    pad_ref[:16, :] = jnp.zeros((16, width), F32)
    acc = jnp.zeros((held, width), F32)
    for z in range(shards):
        w = weight_ref[z * depth : (z + 1) * depth, :]
        acc = acc + jnp.dot(main_ref[z], w, preferred_element_type=F32)
    for copy in copies[:4]:
        copy.wait()
    pad_ref[8 + rows - held :, :] = acc.astype(BF16).astype(F32)
    edge_ref[:8, :] = pad_ref[rows : rows + 8, :].astype(BF16)
    edge_ref[8:, :] = pad_ref[8:16, :].astype(BF16)
    u = convolve(taps_ref, bias_ref, pad_ref, rows, width)
    u_ref[...] = u
    wide_ref[:, :, :sums] = project_rows(u, proj_ref).reshape(shards, 8, sums)
    late = tokens_ref[...].astype(F32)[0:1, :]
    room = wide_ref.shape[2] - sums
    row_ids = lax.broadcasted_iota(jnp.int32, (8, room), 0)
    block = jnp.zeros((8, room), F32)
    for p, (at, size) in enumerate(pieces(depth, room)):
        piece = late[:, at : at + size]
        if size < room:
            piece = jnp.concatenate([piece, jnp.zeros((1, room - size), F32)], axis=1)
        block = jnp.where(row_ids == p, jnp.broadcast_to(piece, (8, room)), block)
    wide_ref[:, :, sums:] = jnp.broadcast_to(block[None], (shards, 8, room))
    send_ref[...] = wide_ref[...].astype(BF16)
    copies[4].wait()


def late_kernel(
    got_ref, rim_ref, edge_ref, keep_ref, weight_hbm, taps_hbm, bias_hbm, proj_hbm,
    mix_ref, u_ref,
    wide_ref, first_ref, pad_ref, pay_ref, weight_ref, taps_ref, bias_ref, proj_ref, sems,
):
    shards, _, lanes = got_ref.shape
    depth = first_ref.shape[1]
    width = weight_ref.shape[1]
    sums = proj_ref.shape[0]
    copies = fetches(
        [
            (weight_hbm.at[pl.ds(z * depth, depth)], weight_part(keep_ref, weight_ref, z, depth))
            for z in range(KEEP, shards)
        ]
        + [(proj_hbm, proj_ref), (taps_hbm, taps_ref), (bias_hbm, bias_ref)],
        sems,
    )
    for copy in copies:
        copy.start()
    room = lanes - sums
    wide_ref[...] = got_ref[...].astype(F32)
    for p, (at, size) in enumerate(pieces(depth, room)):
        first_ref[:, at : at + size] = wide_ref[:, p, sums : sums + size]
    total = jnp.sum(wide_ref[:, :, :sums], axis=0)
    high = total.astype(BF16).astype(F32)
    rank = mix_ref.shape[2] - 256
    coefs = sums - rank
    pay_ref[...] = jnp.zeros_like(pay_ref)
    pay_ref[:, :sums] = high
    pay_ref[:, sums : sums + coefs] = total[:, rank:] - high[:, rank:]
    pad_ref[:8, :] = rim_ref[...].astype(F32)
    pad_ref[8:, :] = edge_ref[8:, :].astype(F32)
    first = first_ref[...].astype(BF16)
    row_ids = lax.broadcasted_iota(jnp.int32, (shards, width), 0)
    acc = jnp.zeros((shards, width), F32)
    for z in range(shards):
        if z >= KEEP:
            copies[z - KEEP].wait()
        w = weight_part(keep_ref, weight_ref, z, depth)[...]
        d = jnp.dot(first, w, preferred_element_type=F32)
        acc = acc + jnp.where(row_ids == z, d, 0.0)
    for copy in copies[shards - KEEP :]:
        copy.wait()
    pad_ref[8:9, :] = jnp.sum(acc, axis=0, keepdims=True).astype(BF16).astype(F32)
    u = convolve(taps_ref, bias_ref, pad_ref, 8, width)
    u_ref[...] = u
    part = project_rows(u, proj_ref)
    half = sums // 2
    late = taps_ref.shape[0]
    at = sums + coefs
    pay_ref[:late, at : at + half] = part[:late, :half]
    pay_ref[late : 2 * late, at : at + half] = part[:late, half:]
    pay = pay_ref[...].astype(BF16)
    for z in range(shards):
        mix_ref[z] = pay


def split2(x):
    a = x.astype(BF16)
    return a, (x - a.astype(F32)).astype(BF16)


def running_sum(x):
    rows = x.shape[0]
    row_ids = lax.broadcasted_iota(jnp.int32, (rows, rows), 0)
    col_ids = lax.broadcasted_iota(jnp.int32, (rows, rows), 1)
    lower = (row_ids >= col_ids).astype(F32).astype(BF16)
    return sum(jnp.dot(lower, p, preferred_element_type=F32) for p in split2(x)[::-1])


def state_kernel(
    mix_ref, dtw_ref, dtb_ref, alog_ref, u_ref, late_u_ref,
    step_ref, coef_ref, pay_ref,
    uf_ref, flow_ref, left_ref, bx_ref, rate_ref, low_ref, pack_ref,
):
    shards, each, _ = mix_ref.shape
    rows, width = u_ref.shape
    rank = dtw_ref.shape[0]
    n = alog_ref.shape[0]
    sums = rank + 2 * n
    half = sums // 2
    at = sums + 2 * n
    late = each // 2
    tiles = rows // 8
    low_ref[...] = mix_ref[:, :, :rank].astype(F32).reshape(rows, rank)
    coef = mix_ref[:, :, rank:sums].astype(F32) + mix_ref[:, :, sums:at].astype(F32)
    coef_ref[...] = coef.reshape(rows, 2 * n)
    pairs = jnp.sum(mix_ref[:, :, at : at + half].astype(F32), axis=0)
    early = jnp.concatenate([pairs[:late], pairs[late:]], axis=1)
    low_ref[:late, :] = early[:, :rank]
    coef_ref[:late, :] = early[:, rank:]
    low = low_ref[...].astype(BF16)
    rate_ref[...] = -jnp.exp(alog_ref[...]) * LOG2E
    uf_ref[...] = u_ref[...].astype(F32)
    uf_ref[:8, :] = late_u_ref[...].astype(F32)
    b = coef_ref[:, :n]
    for i in range(n):
        bx_ref[:, i] = jnp.broadcast_to(b[:, i : i + 1], (rows, 128)).reshape(tiles, 8, 128)
    groups = width // 128
    span = 128
    for h in range(width // span):
        cols = slice(h * span, (h + 1) * span)
        v = jnp.dot(low, dtw_ref[:, cols], preferred_element_type=F32) + dtb_ref[:, cols]
        step = jnp.maximum(v, 0.0) + jnp.log1p(jnp.exp(-jnp.abs(v)))
        step_ref[:, cols] = step
        cum = running_sum(step)
        whole = cum[rows - 1 : rows, :]
        left_ref[:, :, cols] = (whole - cum).reshape(tiles, 8, span)
        flow_ref[:, :, cols] = (step * uf_ref[:, cols]).reshape(tiles, 8, span)
        for k in range(span // 128):
            g = h * (span // 128) + k
            lanes = slice(g * 128, (g + 1) * 128)
            hi, lo = split2(whole[:, k * 128 : (k + 1) * 128])
            ends = []
            for first in range(0, n, 8):
                rates = [jnp.broadcast_to(rate_ref[i : i + 1, lanes], (8, 128)) for i in range(first, first + 8)]
                accs = [None] * 8
                for t in range(tiles):
                    left = left_ref[t, :, lanes]
                    flow = flow_ref[t, :, lanes]
                    for i in range(8):
                        term = jnp.exp2(rates[i] * left) * (flow * bx_ref[t, first + i])
                        accs[i] = term if t == 0 else accs[i] + term
                ends += [jnp.sum(acc, axis=0, keepdims=True) for acc in accs]
            pack_ref[g * n : (g + 1) * n, :] = jnp.concatenate(ends, axis=0).astype(BF16)
            low_ref[g : g + 1, :128] = hi.astype(F32)
            low_ref[groups + g : groups + g + 1, :128] = lo.astype(F32)
    pack_ref[groups * n :, :] = low_ref[: 2 * groups, :128].astype(BF16)
    pack = pack_ref[...]
    for p in range(pay_ref.shape[0]):
        pay_ref[p] = pack


def local_kernel(
    coef_ref, alog_ref, u_ref, late_u_ref, step_ref, skip_ref,
    y_ref, grow_ref, bt_ref, ct_ref, cx_ref, uf_ref, flow_ref, cum_ref,
):
    rows, width = u_ref.shape
    uf_ref[...] = u_ref[...].astype(F32)
    uf_ref[:8, :] = late_u_ref[...].astype(F32)
    flow_ref[...] = (step_ref[...] * uf_ref[...]).reshape(rows // 8, 8, width)
    cum_ref[...] = running_sum(step_ref[...])
    n = alog_ref.shape[0]
    blocks = rows // 16
    b, c = coef_ref[:, :n], coef_ref[:, n:]
    rate2 = -jnp.exp(alog_ref[...]) * LOG2E
    for i in range(n):
        cx_ref[:, i] = jnp.broadcast_to(c[:, i : i + 1], (rows, 128)).reshape(blocks, 16, 128)
    b_t, c_t = b.T, c.T
    for t in range(rows):
        bt_ref[t] = jnp.broadcast_to(b_t[:, t : t + 1], (n, 128))
        ct_ref[t] = jnp.broadcast_to(c_t[:, t : t + 1], (n, 128))
    groups = width // 128

    def block_turn(i, state):
        for r in range(8):
            t = i * 8 + r
            d = step_ref[pl.ds(t, 1), :]
            f = flow_ref[i, r : r + 1, :]
            bt = jnp.concatenate([bt_ref[t]] * groups, axis=1)
            ct = jnp.concatenate([ct_ref[t]] * groups, axis=1)
            state = jnp.exp2(rate2 * d) * state + bt * f
            y_ref[pl.ds(t, 1), :] = jnp.sum(ct * state, axis=0, keepdims=True)
        return state

    lax.fori_loop(0, rows // 8, block_turn, jnp.zeros((n, width), F32))
    y_ref[...] = y_ref[...] + skip_ref[...] * uf_ref[...]

    for g in range(groups):
        lanes = slice(g * 128, (g + 1) * 128)
        rate_g = jnp.broadcast_to(rate2[:, None, lanes], (n, 16, 128))

        def fill(i, _):
            cum = cum_ref[pl.ds(pl.multiple_of(i * 16, 16), 16), lanes]
            grow_ref[i, :, :, lanes] = (cx_ref[i] * jnp.exp2(rate_g * cum[None])).astype(BF16)
            return 0

        lax.fori_loop(0, blocks, fill, 0)


def final_kernel(mine_ref, all_ref, alog_ref, y_ref, grow_ref, thr_ref, out_ref):
    rows, width = y_ref.shape
    n = alog_ref.shape[0]
    blocks = rows // 16
    peers = all_ref.shape[0]
    mine = mine_ref[0]
    rate2 = -jnp.exp(alog_ref[...]) * LOG2E

    groups = width // 128
    for g in range(groups):
        lanes = slice(g * 128, (g + 1) * 128)
        rate_g = rate2[:, lanes]

        def join(p, state):
            block = all_ref[p].astype(F32)
            at = groups * n + g
            whole = block[at : at + 1, :] + block[at + groups : at + groups + 1, :]
            longer = jnp.exp2(rate_g * whole) * state + block[g * n : (g + 1) * n, :]
            return jnp.where(p < mine, longer, state)

        entry = jnp.zeros((n, 128), F32)
        for p in range(peers - 1):
            entry = join(p, entry)
        entry_g = jnp.broadcast_to(entry[:, None, :], (n, 16, 128))
        thr = thr_ref[:, lanes]

        def turn(i, _):
            at = pl.ds(pl.multiple_of(i * 16, 16), 16)
            y = y_ref[at, lanes] + jnp.sum(grow_ref[i, :, :, lanes].astype(F32) * entry_g, axis=0)
            out_ref[at, lanes] = (y / (1.0 + jnp.exp(-4.0 * (y - thr)))).astype(BF16)
            return 0

        lax.fori_loop(0, blocks, turn, 0, unroll=blocks)


def call(kernel, outs, ins, scratch=(), flops=0, specs=None, vmem=12 << 20, outs_in=None):
    specs = specs or [VMEM] * len(ins)
    return pl.pallas_call(
        kernel,
        out_shape=outs,
        in_specs=specs,
        out_specs=outs_in or jax.tree.map(lambda _: VMEM, outs),
        scratch_shapes=scratch,
        cost_estimate=pl.CostEstimate(flops=flops, bytes_accessed=flops // 64, transcendentals=0),
        compiler_params=pltpu.CompilerParams(vmem_limit_bytes=vmem),
    )(*[pltpu.with_memory_space_constraint(x, pltpu.HBM) if spec is HBM else x for x, spec in zip(ins, specs)])


def per_device(
    tokens, in_weight, conv_weight, conv_bias, proj_weight, dt_weight, dt_bias, a_log, skip_gain, threshold
):
    rows = tokens.shape[0]
    width = in_weight.shape[1]
    taps = conv_weight.shape[0]
    rank = dt_weight.shape[0]
    n = a_log.shape[0]
    shards = lax.axis_size("tp")
    peers = lax.axis_size("seq")
    sums = rank + 2 * n
    lanes = -(-sums // 128) * 128
    bias = conv_bias[None]
    proj = proj_weight.T
    kept = (KEEP * tokens.shape[1], width)
    held = (
        pltpu.VMEM(conv_weight.shape, F32),
        pltpu.VMEM(bias.shape, F32),
        pltpu.VMEM(proj.shape, BF16),
    )

    most = call(
        rows_kernel,
        struct((rows - 1, tokens.shape[1]), BF16),
        (tokens,),
        (pltpu.VMEM(tokens.shape, BF16), pltpu.SemaphoreType.DMA),
        flops=1 << 34,
        specs=[HBM],
    )
    main = lax.all_gather(most, "tp")
    send, edge, u, keep = call(
        project_kernel,
        (struct((shards, 8, lanes), BF16), struct((16, width), BF16), struct((rows, width), BF16),
         struct(kept, BF16)),
        (main, in_weight, tokens, conv_weight, bias, proj),
        (pltpu.VMEM((rows + 8, width), F32), pltpu.VMEM((shards, 8, lanes), F32))
        + held
        + (pltpu.VMEM((8, tokens.shape[1]), BF16), pltpu.SemaphoreType.DMA((5,))),
        flops=1 << 29,
        specs=[VMEM] * 2 + [HBM] * 4,
    )
    rim = lax.ppermute(edge[:8], "seq", [(i, i + 1) for i in range(peers - 1)])
    got = lax.all_to_all(send, "tp", 0, 0)
    mix, late_u = call(
        late_kernel,
        (struct((shards, 8, rank + 256), BF16), struct((8, width), BF16)),
        (got, rim, edge, keep, in_weight, conv_weight, bias, proj),
        (
            pltpu.VMEM((shards, 8, lanes), F32),
            pltpu.VMEM((shards, tokens.shape[1]), F32),
            pltpu.VMEM((16, width), F32),
            pltpu.VMEM((8, rank + 256), F32),
        )
        + (pltpu.VMEM((in_weight.shape[0] - kept[0], width), BF16),)
        + held
        + (pltpu.SemaphoreType.DMA((shards + 3,)),),
        flops=1 << 28,
        specs=[VMEM] * 4 + [HBM] * 4,
    )
    mix = lax.all_to_all(mix, "tp", 0, 0)
    whole = struct((rows, width), F32)
    step, coef, pay = call(
        state_kernel,
        (whole, struct((rows, 2 * n), F32), struct((peers, (n + 2) * width // 128, 128), BF16)),
        (mix, dt_weight, dt_bias[None], a_log, u, late_u),
        (
            pltpu.VMEM((rows, width), F32),
            pltpu.VMEM((rows // 8, 8, width), F32),
            pltpu.VMEM((rows // 8, 8, width), F32),
            pltpu.VMEM((rows // 8, n, 8, 128), F32),
            pltpu.VMEM((n, width), F32),
            pltpu.VMEM((rows, rank), F32),
            pltpu.VMEM(((n + 2) * width // 128, 128), BF16),
        ),
        flops=1 << 26,
    )
    everyone = lax.all_to_all(pay, "seq", 0, 0)
    y_local, grow = call(
        local_kernel,
        (whole, struct((rows // 16, n, 16, width), BF16)),
        (coef, a_log, u, late_u, step, skip_gain[None]),
        (
            pltpu.VMEM((rows, n, 128), F32),
            pltpu.VMEM((rows, n, 128), F32),
            pltpu.VMEM((rows // 16, n, 16, 128), F32),
            pltpu.VMEM((rows, width), F32),
            pltpu.VMEM((rows // 8, 8, width), F32),
            pltpu.VMEM((rows, width), F32),
        ),
        flops=1 << 28,
    )
    mine = lax.axis_index("seq").astype(jnp.int32)[None]
    return call(
        final_kernel,
        struct((rows, width), BF16),
        (mine, everyone, a_log, y_local, grow, threshold[None]),
        flops=1 << 26,
        specs=[SMEM] + [VMEM] * 5,
    )


def solution(mesh):
    return jax.shard_map(
        per_device,
        mesh=mesh,
        in_specs=(
            P("seq", "tp"),
            P(None, "tp"),
            P(None, "tp"),
            P("tp"),
            P("tp", None),
            P(None, "tp"),
            P("tp"),
            P(None, "tp"),
            P("tp"),
            P("tp"),
        ),
        out_specs=P("seq", "tp"),
        check_vma=False,
    )
```

```python
import math

import jax
import jax.numpy as jnp
from jax import lax
from jax.experimental import pallas as pl
from jax.experimental.pallas import tpu as pltpu
from jax.sharding import PartitionSpec as P

LOG2E = math.log2(math.e)
F32 = jnp.float32
BF16 = jnp.bfloat16
VMEM = pl.BlockSpec(memory_space=pltpu.VMEM)
SMEM = pl.BlockSpec(memory_space=pltpu.SMEM)
HBM = pl.BlockSpec(memory_space=pltpu.HBM)


def struct(shape, dtype):
    return jax.ShapeDtypeStruct(shape, dtype)


def silu(v):
    return v / (1.0 + jnp.exp(-v))


def convolve(taps_ref, bias_ref, pad_ref, rows, width):
    taps = taps_ref.shape[0]
    pre = jnp.broadcast_to(bias_ref[...], (rows, width))
    for k in range(taps):
        first = 9 - taps + k
        pre = pre + taps_ref[k : k + 1, :] * pad_ref[first : first + rows, :]
    return silu(pre).astype(BF16)


def pieces(depth, room):
    return [(at, min(room, depth - at)) for at in range(0, depth, room)]


def project_rows(u, proj_ref):
    return lax.dot_general(u, proj_ref[...], (((1,), (1,)), ((), ())), preferred_element_type=F32)


KEEP = 12


def fetches(pairs, sems):
    return [pltpu.make_async_copy(src, dst, sems.at[i]) for i, (src, dst) in enumerate(pairs)]


def weight_part(keep_ref, buf_ref, z, depth):
    if z < KEEP:
        return keep_ref.at[pl.ds(z * depth, depth)]
    return buf_ref.at[pl.ds((z - KEEP) * depth, depth)]


def rows_kernel(tokens_hbm, out_ref, tokens_ref, sem):
    copy = pltpu.make_async_copy(tokens_hbm, tokens_ref, sem)
    copy.start()
    copy.wait()
    out_ref[...] = tokens_ref[...].astype(F32)[1:, :].astype(BF16)


def project_kernel(
    main_ref, weight_ref, tokens_hbm, taps_hbm, bias_hbm, proj_hbm,
    send_ref, edge_ref, u_ref, keep_ref,
    pad_ref, wide_ref, taps_ref, bias_ref, proj_ref, tokens_ref, sems,
):
    shards, held, depth = main_ref.shape
    rows, width = u_ref.shape
    sums = proj_ref.shape[0]
    copies = fetches(
        [(proj_hbm, proj_ref), (taps_hbm, taps_ref), (bias_hbm, bias_ref),
         (tokens_hbm.at[pl.ds(0, 8)], tokens_ref),
         (weight_ref.at[pl.ds(0, KEEP * depth)], keep_ref)],
        sems,
    )
    for copy in copies:
        copy.start()
    pad_ref[:16, :] = jnp.zeros((16, width), F32)
    acc = jnp.zeros((held, width), F32)
    for z in range(shards):
        w = weight_ref[z * depth : (z + 1) * depth, :]
        acc = acc + jnp.dot(main_ref[z], w, preferred_element_type=F32)
    for copy in copies[:4]:
        copy.wait()
    pad_ref[8 + rows - held :, :] = acc.astype(BF16).astype(F32)
    edge_ref[:8, :] = pad_ref[rows : rows + 8, :].astype(BF16)
    edge_ref[8:, :] = pad_ref[8:16, :].astype(BF16)
    u = convolve(taps_ref, bias_ref, pad_ref, rows, width)
    u_ref[...] = u
    wide_ref[:, :, :sums] = project_rows(u, proj_ref).reshape(shards, 8, sums)
    late = tokens_ref[...].astype(F32)[0:1, :]
    room = wide_ref.shape[2] - sums
    row_ids = lax.broadcasted_iota(jnp.int32, (8, room), 0)
    block = jnp.zeros((8, room), F32)
    for p, (at, size) in enumerate(pieces(depth, room)):
        piece = late[:, at : at + size]
        if size < room:
            piece = jnp.concatenate([piece, jnp.zeros((1, room - size), F32)], axis=1)
        block = jnp.where(row_ids == p, jnp.broadcast_to(piece, (8, room)), block)
    wide_ref[:, :, sums:] = jnp.broadcast_to(block[None], (shards, 8, room))
    send_ref[...] = wide_ref[...].astype(BF16)
    copies[4].wait()


def late_kernel(
    got_ref, rim_ref, edge_ref, keep_ref, weight_hbm, taps_hbm, bias_hbm, proj_hbm,
    mix_ref, u_ref,
    wide_ref, first_ref, pad_ref, pay_ref, weight_ref, taps_ref, bias_ref, proj_ref, sems,
):
    shards, _, lanes = got_ref.shape
    depth = first_ref.shape[1]
    width = weight_ref.shape[1]
    sums = proj_ref.shape[0]
    copies = fetches(
        [
            (weight_hbm.at[pl.ds(z * depth, depth)], weight_part(keep_ref, weight_ref, z, depth))
            for z in range(KEEP, shards)
        ]
        + [(proj_hbm, proj_ref), (taps_hbm, taps_ref), (bias_hbm, bias_ref)],
        sems,
    )
    for copy in copies:
        copy.start()
    room = lanes - sums
    wide_ref[...] = got_ref[...].astype(F32)
    for p, (at, size) in enumerate(pieces(depth, room)):
        first_ref[:, at : at + size] = wide_ref[:, p, sums : sums + size]
    total = jnp.sum(wide_ref[:, :, :sums], axis=0)
    high = total.astype(BF16).astype(F32)
    rank = mix_ref.shape[2] - 256
    coefs = sums - rank
    pay_ref[...] = jnp.zeros_like(pay_ref)
    pay_ref[:, :sums] = high
    pay_ref[:, sums : sums + coefs] = total[:, rank:] - high[:, rank:]
    pad_ref[:8, :] = rim_ref[...].astype(F32)
    pad_ref[8:, :] = edge_ref[8:, :].astype(F32)
    first = first_ref[...].astype(BF16)
    row_ids = lax.broadcasted_iota(jnp.int32, (shards, width), 0)
    acc = jnp.zeros((shards, width), F32)
    for z in range(shards):
        if z >= KEEP:
            copies[z - KEEP].wait()
        w = weight_part(keep_ref, weight_ref, z, depth)[...]
        d = jnp.dot(first, w, preferred_element_type=F32)
        acc = acc + jnp.where(row_ids == z, d, 0.0)
    for copy in copies[shards - KEEP :]:
        copy.wait()
    pad_ref[8:9, :] = jnp.sum(acc, axis=0, keepdims=True).astype(BF16).astype(F32)
    u = convolve(taps_ref, bias_ref, pad_ref, 8, width)
    u_ref[...] = u
    part = project_rows(u, proj_ref)
    half = sums // 2
    late = taps_ref.shape[0]
    at = sums + coefs
    pay_ref[:late, at : at + half] = part[:late, :half]
    pay_ref[late : 2 * late, at : at + half] = part[:late, half:]
    pay = pay_ref[...].astype(BF16)
    for z in range(shards):
        mix_ref[z] = pay


def split2(x):
    a = x.astype(BF16)
    return a, (x - a.astype(F32)).astype(BF16)


def running_sum(x):
    rows = x.shape[0]
    row_ids = lax.broadcasted_iota(jnp.int32, (rows, rows), 0)
    col_ids = lax.broadcasted_iota(jnp.int32, (rows, rows), 1)
    lower = (row_ids >= col_ids).astype(F32).astype(BF16)
    return sum(jnp.dot(lower, p, preferred_element_type=F32) for p in split2(x)[::-1])


def state_kernel(
    mix_ref, dtw_ref, dtb_ref, alog_ref, u_ref, late_u_ref,
    step_ref, coef_ref, pack_ref,
    uf_ref, flow_ref, left_ref, bx_ref, rate_ref, low_ref,
):
    shards, each, _ = mix_ref.shape
    rows, width = u_ref.shape
    rank = dtw_ref.shape[0]
    n = alog_ref.shape[0]
    sums = rank + 2 * n
    half = sums // 2
    at = sums + 2 * n
    late = each // 2
    tiles = rows // 8
    low_ref[...] = mix_ref[:, :, :rank].astype(F32).reshape(rows, rank)
    coef = mix_ref[:, :, rank:sums].astype(F32) + mix_ref[:, :, sums:at].astype(F32)
    coef_ref[...] = coef.reshape(rows, 2 * n)
    pairs = jnp.sum(mix_ref[:, :, at : at + half].astype(F32), axis=0)
    early = jnp.concatenate([pairs[:late], pairs[late:]], axis=1)
    low_ref[:late, :] = early[:, :rank]
    coef_ref[:late, :] = early[:, rank:]
    low = low_ref[...].astype(BF16)
    rate_ref[...] = -jnp.exp(alog_ref[...]) * LOG2E
    uf_ref[...] = u_ref[...].astype(F32)
    uf_ref[:8, :] = late_u_ref[...].astype(F32)
    b = coef_ref[:, :n]
    for i in range(n):
        bx_ref[:, i] = jnp.broadcast_to(b[:, i : i + 1], (rows, 128)).reshape(tiles, 8, 128)
    groups = width // 128
    span = 128
    for h in range(width // span):
        cols = slice(h * span, (h + 1) * span)
        v = jnp.dot(low, dtw_ref[:, cols], preferred_element_type=F32) + dtb_ref[:, cols]
        step = jnp.maximum(v, 0.0) + jnp.log1p(jnp.exp(-jnp.abs(v)))
        step_ref[:, cols] = step
        cum = running_sum(step)
        whole = cum[rows - 1 : rows, :]
        left_ref[:, :, cols] = (whole - cum).reshape(tiles, 8, span)
        flow_ref[:, :, cols] = (step * uf_ref[:, cols]).reshape(tiles, 8, span)
        for k in range(span // 128):
            g = h * (span // 128) + k
            lanes = slice(g * 128, (g + 1) * 128)
            hi, lo = split2(whole[:, k * 128 : (k + 1) * 128])
            ends = []
            for first in range(0, n, 8):
                rates = [jnp.broadcast_to(rate_ref[i : i + 1, lanes], (8, 128)) for i in range(first, first + 8)]
                accs = [None] * 8
                for t in range(tiles):
                    left = left_ref[t, :, lanes]
                    flow = flow_ref[t, :, lanes]
                    for i in range(8):
                        term = jnp.exp2(rates[i] * left) * (flow * bx_ref[t, first + i])
                        accs[i] = term if t == 0 else accs[i] + term
                ends += [jnp.sum(acc, axis=0, keepdims=True) for acc in accs]
            pack_ref[g * n : (g + 1) * n, :] = jnp.concatenate(ends, axis=0).astype(BF16)
            low_ref[g : g + 1, :128] = hi.astype(F32)
            low_ref[groups + g : groups + g + 1, :128] = lo.astype(F32)
    pack_ref[groups * n :, :] = low_ref[: 2 * groups, :128].astype(BF16)


def merge_kernel(mine_ref, own_ref, other_ref, alog_ref, pay_ref, pack_ref):
    n, width = alog_ref.shape
    groups = width // 128
    near = groups // 2
    second_core = lax.rem(mine_ref[0], 2) == 1
    own = own_ref[...].astype(F32)
    other = other_ref[...].astype(F32)
    early = jnp.where(second_core, other, own)
    later = jnp.where(second_core, own, other)
    rate2 = -jnp.exp(alog_ref[...]) * LOG2E

    def rows(block, g, first, size):
        low = block[first + g * size : first + (g + 1) * size, :]
        high = block[first + (near + g) * size : first + (near + g + 1) * size, :]
        return jnp.where(second_core, high, low)

    for g in range(near):
        at = groups * n
        sum_early = rows(early, g, at, 1) + rows(early, g, at + groups, 1)
        sum_later = rows(later, g, at, 1) + rows(later, g, at + groups, 1)
        rate_g = jnp.where(
            second_core,
            rate2[:, (near + g) * 128 : (near + g + 1) * 128],
            rate2[:, g * 128 : (g + 1) * 128],
        )
        pack_ref[g * n : (g + 1) * n, :] = (
            jnp.exp2(rate_g * sum_later) * rows(early, g, 0, n) + rows(later, g, 0, n)
        )
        hi, lo = split2(sum_early + sum_later)
        pack_ref[near * n + g : near * n + g + 1, :] = hi.astype(F32)
        pack_ref[near * n + near + g : near * n + near + g + 1, :] = lo.astype(F32)
    pack = pack_ref[...].astype(BF16)
    for p in range(pay_ref.shape[0]):
        pay_ref[p] = pack


def local_kernel(
    coef_ref, alog_ref, u_ref, late_u_ref, step_ref, skip_ref,
    y_ref, grow_ref, bt_ref, ct_ref, cx_ref, uf_ref, flow_ref, cum_ref,
):
    rows, width = u_ref.shape
    uf_ref[...] = u_ref[...].astype(F32)
    uf_ref[:8, :] = late_u_ref[...].astype(F32)
    flow_ref[...] = (step_ref[...] * uf_ref[...]).reshape(rows // 8, 8, width)
    cum_ref[...] = running_sum(step_ref[...])
    n = alog_ref.shape[0]
    blocks = rows // 16
    b, c = coef_ref[:, :n], coef_ref[:, n:]
    rate2 = -jnp.exp(alog_ref[...]) * LOG2E
    for i in range(n):
        cx_ref[:, i] = jnp.broadcast_to(c[:, i : i + 1], (rows, 128)).reshape(blocks, 16, 128)
    b_t, c_t = b.T, c.T
    for t in range(rows):
        bt_ref[t] = jnp.broadcast_to(b_t[:, t : t + 1], (n, 128))
        ct_ref[t] = jnp.broadcast_to(c_t[:, t : t + 1], (n, 128))
    groups = width // 128

    def block_turn(i, state):
        for r in range(8):
            t = i * 8 + r
            d = step_ref[pl.ds(t, 1), :]
            f = flow_ref[i, r : r + 1, :]
            bt = jnp.concatenate([bt_ref[t]] * groups, axis=1)
            ct = jnp.concatenate([ct_ref[t]] * groups, axis=1)
            state = jnp.exp2(rate2 * d) * state + bt * f
            y_ref[pl.ds(t, 1), :] = jnp.sum(ct * state, axis=0, keepdims=True)
        return state

    lax.fori_loop(0, rows // 8, block_turn, jnp.zeros((n, width), F32))
    y_ref[...] = y_ref[...] + skip_ref[...] * uf_ref[...]

    for g in range(groups):
        lanes = slice(g * 128, (g + 1) * 128)
        rate_g = jnp.broadcast_to(rate2[:, None, lanes], (n, 16, 128))

        def fill(i, _):
            cum = cum_ref[pl.ds(pl.multiple_of(i * 16, 16), 16), lanes]
            grow_ref[i, :, :, lanes] = (cx_ref[i] * jnp.exp2(rate_g * cum[None])).astype(BF16)
            return 0

        lax.fori_loop(0, blocks, fill, 0)


def final_kernel(mine_ref, all_ref, other_ref, alog_ref, y_ref, grow_ref, thr_ref, out_ref):
    rows, width = y_ref.shape
    n = alog_ref.shape[0]
    blocks = rows // 16
    chips = all_ref.shape[0] // 2
    mine = mine_ref[0]
    second_core = lax.rem(mine, 2) == 1
    rate2 = -jnp.exp(alog_ref[...]) * LOG2E
    groups = width // 128
    near = groups // 2
    other = other_ref[...].astype(F32)
    for g in range(groups):
        lanes = slice(g * 128, (g + 1) * 128)
        rate_g = rate2[:, lanes]
        half, place = g // near, g % near
        entry = jnp.zeros((n, 128), F32)
        for p in range(chips - 1):
            block = all_ref[2 * p + half].astype(F32)
            at = near * n + place
            whole = block[at : at + 1, :] + block[at + near : at + near + 1, :]
            longer = jnp.exp2(rate_g * whole) * entry + block[place * n : (place + 1) * n, :]
            entry = jnp.where(2 * p + 1 < mine, longer, entry)
        at = groups * n + g
        whole = other[at : at + 1, :] + other[at + groups : at + groups + 1, :]
        longer = jnp.exp2(rate_g * whole) * entry + other[g * n : (g + 1) * n, :]
        entry = jnp.where(second_core, longer, entry)
        entry_g = jnp.broadcast_to(entry[:, None, :], (n, 16, 128))
        thr = thr_ref[:, lanes]

        def turn(i, _):
            at = pl.ds(pl.multiple_of(i * 16, 16), 16)
            y = y_ref[at, lanes] + jnp.sum(grow_ref[i, :, :, lanes].astype(F32) * entry_g, axis=0)
            out_ref[at, lanes] = (y / (1.0 + jnp.exp(-4.0 * (y - thr)))).astype(BF16)
            return 0

        lax.fori_loop(0, blocks, turn, 0, unroll=blocks)


def call(kernel, outs, ins, scratch=(), flops=0, specs=None, vmem=12 << 20, outs_in=None):
    specs = specs or [VMEM] * len(ins)
    return pl.pallas_call(
        kernel,
        out_shape=outs,
        in_specs=specs,
        out_specs=outs_in or jax.tree.map(lambda _: VMEM, outs),
        scratch_shapes=scratch,
        cost_estimate=pl.CostEstimate(flops=flops, bytes_accessed=flops // 64, transcendentals=0),
        compiler_params=pltpu.CompilerParams(vmem_limit_bytes=vmem),
    )(*[pltpu.with_memory_space_constraint(x, pltpu.HBM) if spec is HBM else x for x, spec in zip(ins, specs)])


def per_device(
    tokens, in_weight, conv_weight, conv_bias, proj_weight, dt_weight, dt_bias, a_log, skip_gain, threshold
):
    rows = tokens.shape[0]
    width = in_weight.shape[1]
    taps = conv_weight.shape[0]
    rank = dt_weight.shape[0]
    n = a_log.shape[0]
    shards = lax.axis_size("tp")
    peers = lax.axis_size("seq")
    sums = rank + 2 * n
    lanes = -(-sums // 128) * 128
    bias = conv_bias[None]
    proj = proj_weight.T
    kept = (KEEP * tokens.shape[1], width)
    held = (
        pltpu.VMEM(conv_weight.shape, F32),
        pltpu.VMEM(bias.shape, F32),
        pltpu.VMEM(proj.shape, BF16),
    )

    most = call(
        rows_kernel,
        struct((rows - 1, tokens.shape[1]), BF16),
        (tokens,),
        (pltpu.VMEM(tokens.shape, BF16), pltpu.SemaphoreType.DMA),
        flops=1 << 34,
        specs=[HBM],
    )
    main = lax.all_gather(most, "tp")
    send, edge, u, keep = call(
        project_kernel,
        (struct((shards, 8, lanes), BF16), struct((16, width), BF16), struct((rows, width), BF16),
         struct(kept, BF16)),
        (main, in_weight, tokens, conv_weight, bias, proj),
        (pltpu.VMEM((rows + 8, width), F32), pltpu.VMEM((shards, 8, lanes), F32))
        + held
        + (pltpu.VMEM((8, tokens.shape[1]), BF16), pltpu.SemaphoreType.DMA((5,))),
        flops=1 << 29,
        specs=[VMEM] * 2 + [HBM] * 4,
    )
    rim = lax.ppermute(edge[:8], "seq", [(i, i + 1) for i in range(peers - 1)])
    got = lax.all_to_all(send, "tp", 0, 0)
    mix, late_u = call(
        late_kernel,
        (struct((shards, 8, rank + 256), BF16), struct((8, width), BF16)),
        (got, rim, edge, keep, in_weight, conv_weight, bias, proj),
        (
            pltpu.VMEM((shards, 8, lanes), F32),
            pltpu.VMEM((shards, tokens.shape[1]), F32),
            pltpu.VMEM((16, width), F32),
            pltpu.VMEM((8, rank + 256), F32),
        )
        + (pltpu.VMEM((in_weight.shape[0] - kept[0], width), BF16),)
        + held
        + (pltpu.SemaphoreType.DMA((shards + 3,)),),
        flops=1 << 28,
        specs=[VMEM] * 4 + [HBM] * 4,
    )
    mix = lax.all_to_all(mix, "tp", 0, 0)
    whole = struct((rows, width), F32)
    step, coef, own = call(
        state_kernel,
        (whole, struct((rows, 2 * n), F32), struct(((n + 2) * width // 128, 128), BF16)),
        (mix, dt_weight, dt_bias[None], a_log, u, late_u),
        (
            pltpu.VMEM((rows, width), F32),
            pltpu.VMEM((rows // 8, 8, width), F32),
            pltpu.VMEM((rows // 8, 8, width), F32),
            pltpu.VMEM((rows // 8, n, 8, 128), F32),
            pltpu.VMEM((n, width), F32),
            pltpu.VMEM((rows, rank), F32),
        ),
        flops=1 << 26,
    )
    mine = lax.axis_index("seq").astype(jnp.int32)[None]
    other = lax.ppermute(own, "seq", [(i, i ^ 1) for i in range(peers)])
    half = (n + 2) * width // 256
    pay = call(
        merge_kernel,
        struct((peers, half, 128), BF16),
        (mine, own, other, a_log),
        (pltpu.VMEM((half, 128), F32),),
        flops=1 << 20,
        specs=[SMEM] + [VMEM] * 3,
    )
    pay, coef = lax.optimization_barrier((pay, coef))
    everyone = lax.all_to_all(pay, "seq", 0, 0)
    y_local, grow = call(
        local_kernel,
        (whole, struct((rows // 16, n, 16, width), BF16)),
        (coef, a_log, u, late_u, step, skip_gain[None]),
        (
            pltpu.VMEM((rows, n, 128), F32),
            pltpu.VMEM((rows, n, 128), F32),
            pltpu.VMEM((rows // 16, n, 16, 128), F32),
            pltpu.VMEM((rows, width), F32),
            pltpu.VMEM((rows // 8, 8, width), F32),
            pltpu.VMEM((rows, width), F32),
        ),
        flops=1 << 28,
    )
    return call(
        final_kernel,
        struct((rows, width), BF16),
        (mine, everyone, other, a_log, y_local, grow, threshold[None]),
        flops=1 << 26,
        specs=[SMEM] + [VMEM] * 6,
    )


def solution(mesh):
    return jax.shard_map(
        per_device,
        mesh=mesh,
        in_specs=(
            P("seq", "tp"),
            P(None, "tp"),
            P(None, "tp"),
            P("tp"),
            P("tp", None),
            P(None, "tp"),
            P("tp"),
            P(None, "tp"),
            P("tp"),
            P("tp"),
        ),
        out_specs=P("seq", "tp"),
        check_vma=False,
    )
```

```python
import math

import jax
import jax.numpy as jnp
from jax import lax
from jax.experimental import pallas as pl
from jax.experimental.pallas import tpu as pltpu
from jax.sharding import PartitionSpec as P

LOG2E = math.log2(math.e)
F32 = jnp.float32
BF16 = jnp.bfloat16
VMEM = pl.BlockSpec(memory_space=pltpu.VMEM)
SMEM = pl.BlockSpec(memory_space=pltpu.SMEM)
HBM = pl.BlockSpec(memory_space=pltpu.HBM)


def struct(shape, dtype):
    return jax.ShapeDtypeStruct(shape, dtype)


def silu(v):
    return v / (1.0 + jnp.exp(-v))


def convolve(taps_ref, bias_ref, pad_ref, rows, width):
    taps = taps_ref.shape[0]
    pre = jnp.broadcast_to(bias_ref[...], (rows, width))
    for k in range(taps):
        first = 9 - taps + k
        pre = pre + taps_ref[k : k + 1, :] * pad_ref[first : first + rows, :]
    return silu(pre).astype(BF16)


def pieces(depth, room):
    return [(at, min(room, depth - at)) for at in range(0, depth, room)]


def project_rows(u, proj_ref):
    return lax.dot_general(u, proj_ref[...], (((1,), (1,)), ((), ())), preferred_element_type=F32)


KEEP = 12


def fetches(pairs, sems):
    return [pltpu.make_async_copy(src, dst, sems.at[i]) for i, (src, dst) in enumerate(pairs)]


def weight_part(keep_ref, buf_ref, z, depth):
    if z < KEEP:
        return keep_ref.at[pl.ds(z * depth, depth)]
    return buf_ref.at[pl.ds((z - KEEP) * depth, depth)]


def rows_kernel(tokens_hbm, out_ref, tokens_ref, sem):
    copy = pltpu.make_async_copy(tokens_hbm, tokens_ref, sem)
    copy.start()
    copy.wait()
    out_ref[...] = tokens_ref[...].astype(F32)[1:, :].astype(BF16)


def project_kernel(
    main_ref, weight_ref, tokens_hbm, taps_hbm, bias_hbm, proj_hbm,
    send_ref, edge_ref, u_ref, keep_ref,
    pad_ref, wide_ref, taps_ref, bias_ref, proj_ref, tokens_ref, sems,
):
    shards, held, depth = main_ref.shape
    rows, width = u_ref.shape
    sums = proj_ref.shape[0]
    copies = fetches(
        [(proj_hbm, proj_ref), (taps_hbm, taps_ref), (bias_hbm, bias_ref),
         (tokens_hbm.at[pl.ds(0, 8)], tokens_ref)],
        sems,
    )
    for copy in copies:
        copy.start()
    pad_ref[:16, :] = jnp.zeros((16, width), F32)
    acc = jnp.zeros((held, width), F32)
    for z in range(shards):
        w = weight_ref[z * depth : (z + 1) * depth, :]
        if z < KEEP:
            keep_ref[z * depth : (z + 1) * depth, :] = w
        acc = acc + jnp.dot(main_ref[z], w, preferred_element_type=F32)
    for copy in copies:
        copy.wait()
    pad_ref[8 + rows - held :, :] = acc.astype(BF16).astype(F32)
    edge_ref[:8, :] = pad_ref[rows : rows + 8, :].astype(BF16)
    edge_ref[8:, :] = pad_ref[8:16, :].astype(BF16)
    u = convolve(taps_ref, bias_ref, pad_ref, rows, width)
    u_ref[...] = u
    wide_ref[:, :, :sums] = project_rows(u, proj_ref).reshape(shards, 8, sums)
    late = tokens_ref[...].astype(F32)[0:1, :]
    room = wide_ref.shape[2] - sums
    row_ids = lax.broadcasted_iota(jnp.int32, (8, room), 0)
    block = jnp.zeros((8, room), F32)
    for p, (at, size) in enumerate(pieces(depth, room)):
        piece = late[:, at : at + size]
        if size < room:
            piece = jnp.concatenate([piece, jnp.zeros((1, room - size), F32)], axis=1)
        block = jnp.where(row_ids == p, jnp.broadcast_to(piece, (8, room)), block)
    wide_ref[:, :, sums:] = jnp.broadcast_to(block[None], (shards, 8, room))
    send_ref[...] = wide_ref[...].astype(BF16)


def late_kernel(
    got_ref, rim_ref, edge_ref, keep_ref, weight_hbm, taps_hbm, bias_hbm, proj_hbm,
    mix_ref, u_ref,
    wide_ref, first_ref, pad_ref, pay_ref, weight_ref, taps_ref, bias_ref, proj_ref, sems,
):
    shards, _, lanes = got_ref.shape
    depth = first_ref.shape[1]
    width = weight_ref.shape[1]
    sums = proj_ref.shape[0]
    copies = fetches(
        [
            (weight_hbm.at[pl.ds(z * depth, depth)], weight_part(keep_ref, weight_ref, z, depth))
            for z in range(KEEP, shards)
        ]
        + [(proj_hbm, proj_ref), (taps_hbm, taps_ref), (bias_hbm, bias_ref)],
        sems,
    )
    for copy in copies:
        copy.start()
    room = lanes - sums
    wide_ref[...] = got_ref[...].astype(F32)
    for p, (at, size) in enumerate(pieces(depth, room)):
        first_ref[:, at : at + size] = wide_ref[:, p, sums : sums + size]
    total = jnp.sum(wide_ref[:, :, :sums], axis=0)
    high = total.astype(BF16).astype(F32)
    rank = mix_ref.shape[2] - 256
    coefs = sums - rank
    pay_ref[...] = jnp.zeros_like(pay_ref)
    pay_ref[:, :sums] = high
    pay_ref[:, sums : sums + coefs] = total[:, rank:] - high[:, rank:]
    pad_ref[:8, :] = rim_ref[...].astype(F32)
    pad_ref[8:, :] = edge_ref[8:, :].astype(F32)
    first = first_ref[...].astype(BF16)
    row_ids = lax.broadcasted_iota(jnp.int32, (shards, width), 0)
    acc = jnp.zeros((shards, width), F32)
    for z in range(shards):
        if z >= KEEP:
            copies[z - KEEP].wait()
        w = weight_part(keep_ref, weight_ref, z, depth)[...]
        d = jnp.dot(first, w, preferred_element_type=F32)
        acc = acc + jnp.where(row_ids == z, d, 0.0)
    for copy in copies[shards - KEEP :]:
        copy.wait()
    pad_ref[8:9, :] = jnp.sum(acc, axis=0, keepdims=True).astype(BF16).astype(F32)
    u = convolve(taps_ref, bias_ref, pad_ref, 8, width)
    u_ref[...] = u
    part = project_rows(u, proj_ref)
    half = sums // 2
    late = taps_ref.shape[0]
    at = sums + coefs
    pay_ref[:late, at : at + half] = part[:late, :half]
    pay_ref[late : 2 * late, at : at + half] = part[:late, half:]
    pay = pay_ref[...].astype(BF16)
    for z in range(shards):
        mix_ref[z] = pay


def split2(x):
    a = x.astype(BF16)
    return a, (x - a.astype(F32)).astype(BF16)


def running_sum(x):
    rows = x.shape[0]
    row_ids = lax.broadcasted_iota(jnp.int32, (rows, rows), 0)
    col_ids = lax.broadcasted_iota(jnp.int32, (rows, rows), 1)
    lower = (row_ids >= col_ids).astype(F32).astype(BF16)
    return sum(jnp.dot(lower, p, preferred_element_type=F32) for p in split2(x)[::-1])


def state_kernel(
    mix_ref, dtw_ref, dtb_ref, alog_ref, u_ref, late_u_ref,
    step_ref, coef_ref, pack_ref,
    uf_ref, flow_ref, left_ref, bx_ref, rate_ref, low_ref,
):
    shards, each, _ = mix_ref.shape
    rows, width = u_ref.shape
    rank = dtw_ref.shape[0]
    n = alog_ref.shape[0]
    sums = rank + 2 * n
    half = sums // 2
    at = sums + 2 * n
    late = each // 2
    tiles = rows // 8
    low_ref[...] = mix_ref[:, :, :rank].astype(F32).reshape(rows, rank)
    coef = mix_ref[:, :, rank:sums].astype(F32) + mix_ref[:, :, sums:at].astype(F32)
    coef_ref[...] = coef.reshape(rows, 2 * n)
    pairs = jnp.sum(mix_ref[:, :, at : at + half].astype(F32), axis=0)
    early = jnp.concatenate([pairs[:late], pairs[late:]], axis=1)
    low_ref[:late, :] = early[:, :rank]
    coef_ref[:late, :] = early[:, rank:]
    low = low_ref[...].astype(BF16)
    rate_ref[...] = -jnp.exp(alog_ref[...]) * LOG2E
    uf_ref[...] = u_ref[...].astype(F32)
    uf_ref[:8, :] = late_u_ref[...].astype(F32)
    b = coef_ref[:, :n]
    for i in range(n):
        bx_ref[:, i] = jnp.broadcast_to(b[:, i : i + 1], (rows, 128)).reshape(tiles, 8, 128)
    groups = width // 128
    span = 128
    for h in range(width // span):
        cols = slice(h * span, (h + 1) * span)
        v = jnp.dot(low, dtw_ref[:, cols], preferred_element_type=F32) + dtb_ref[:, cols]
        step = jnp.maximum(v, 0.0) + jnp.log1p(jnp.exp(-jnp.abs(v)))
        step_ref[:, cols] = step
        cum = running_sum(step)
        whole = cum[rows - 1 : rows, :]
        left_ref[:, :, cols] = (whole - cum).reshape(tiles, 8, span)
        flow_ref[:, :, cols] = (step * uf_ref[:, cols]).reshape(tiles, 8, span)
        for k in range(span // 128):
            g = h * (span // 128) + k
            lanes = slice(g * 128, (g + 1) * 128)
            hi, lo = split2(whole[:, k * 128 : (k + 1) * 128])
            ends = []
            for first in range(0, n, 8):
                rates = [jnp.broadcast_to(rate_ref[i : i + 1, lanes], (8, 128)) for i in range(first, first + 8)]
                accs = [None] * 8
                for t in range(tiles):
                    left = left_ref[t, :, lanes]
                    flow = flow_ref[t, :, lanes]
                    for i in range(8):
                        term = jnp.exp2(rates[i] * left) * (flow * bx_ref[t, first + i])
                        accs[i] = term if t == 0 else accs[i] + term
                ends += [jnp.sum(acc, axis=0, keepdims=True) for acc in accs]
            pack_ref[g * n : (g + 1) * n, :] = jnp.concatenate(ends, axis=0).astype(BF16)
            low_ref[g : g + 1, :128] = hi.astype(F32)
            low_ref[groups + g : groups + g + 1, :128] = lo.astype(F32)
    pack_ref[groups * n :, :] = low_ref[: 2 * groups, :128].astype(BF16)


def merge_kernel(mine_ref, own_ref, other_ref, alog_ref, pay_ref, pack_ref):
    n, width = alog_ref.shape
    groups = width // 128
    near = groups // 2
    second_core = lax.rem(mine_ref[0], 2) == 1
    own = own_ref[...].astype(F32)
    other = other_ref[...].astype(F32)
    early = jnp.where(second_core, other, own)
    later = jnp.where(second_core, own, other)
    rate2 = -jnp.exp(alog_ref[...]) * LOG2E

    def rows(block, g, first, size):
        low = block[first + g * size : first + (g + 1) * size, :]
        high = block[first + (near + g) * size : first + (near + g + 1) * size, :]
        return jnp.where(second_core, high, low)

    for g in range(near):
        at = groups * n
        sum_early = rows(early, g, at, 1) + rows(early, g, at + groups, 1)
        sum_later = rows(later, g, at, 1) + rows(later, g, at + groups, 1)
        rate_g = jnp.where(
            second_core,
            rate2[:, (near + g) * 128 : (near + g + 1) * 128],
            rate2[:, g * 128 : (g + 1) * 128],
        )
        pack_ref[g * n : (g + 1) * n, :] = (
            jnp.exp2(rate_g * sum_later) * rows(early, g, 0, n) + rows(later, g, 0, n)
        )
        hi, lo = split2(sum_early + sum_later)
        pack_ref[near * n + g : near * n + g + 1, :] = hi.astype(F32)
        pack_ref[near * n + near + g : near * n + near + g + 1, :] = lo.astype(F32)
    pack = pack_ref[...].astype(BF16)
    for p in range(pay_ref.shape[0]):
        pay_ref[p] = pack


def local_kernel(
    coef_ref, alog_ref, u_ref, late_u_ref, step_ref, skip_ref,
    y_ref, grow_ref, bt_ref, ct_ref, cx_ref, uf_ref, flow_ref, cum_ref,
):
    rows, width = u_ref.shape
    uf_ref[...] = u_ref[...].astype(F32)
    uf_ref[:8, :] = late_u_ref[...].astype(F32)
    flow_ref[...] = (step_ref[...] * uf_ref[...]).reshape(rows // 8, 8, width)
    cum_ref[...] = running_sum(step_ref[...])
    n = alog_ref.shape[0]
    blocks = rows // 16
    b, c = coef_ref[:, :n], coef_ref[:, n:]
    rate2 = -jnp.exp(alog_ref[...]) * LOG2E
    for i in range(n):
        cx_ref[:, i] = jnp.broadcast_to(c[:, i : i + 1], (rows, 128)).reshape(blocks, 16, 128)
    b_t, c_t = b.T, c.T
    for t in range(rows):
        bt_ref[t] = jnp.broadcast_to(b_t[:, t : t + 1], (n, 128))
        ct_ref[t] = jnp.broadcast_to(c_t[:, t : t + 1], (n, 128))
    groups = width // 128

    def block_turn(i, state):
        for r in range(8):
            t = i * 8 + r
            d = step_ref[pl.ds(t, 1), :]
            f = flow_ref[i, r : r + 1, :]
            bt = jnp.concatenate([bt_ref[t]] * groups, axis=1)
            ct = jnp.concatenate([ct_ref[t]] * groups, axis=1)
            state = jnp.exp2(rate2 * d) * state + bt * f
            y_ref[pl.ds(t, 1), :] = jnp.sum(ct * state, axis=0, keepdims=True)
        return state

    lax.fori_loop(0, rows // 8, block_turn, jnp.zeros((n, width), F32))
    y_ref[...] = y_ref[...] + skip_ref[...] * uf_ref[...]

    for g in range(groups):
        lanes = slice(g * 128, (g + 1) * 128)
        rate_g = jnp.broadcast_to(rate2[:, None, lanes], (n, 16, 128))

        def fill(i, _):
            cum = cum_ref[pl.ds(pl.multiple_of(i * 16, 16), 16), lanes]
            grow_ref[i, :, :, lanes] = (cx_ref[i] * jnp.exp2(rate_g * cum[None])).astype(BF16)
            return 0

        lax.fori_loop(0, blocks, fill, 0)


def final_kernel(mine_ref, all_ref, other_ref, alog_ref, y_ref, grow_ref, thr_ref, out_ref):
    rows, width = y_ref.shape
    n = alog_ref.shape[0]
    blocks = rows // 16
    chips = all_ref.shape[0] // 2
    mine = mine_ref[0]
    second_core = lax.rem(mine, 2) == 1
    rate2 = -jnp.exp(alog_ref[...]) * LOG2E
    groups = width // 128
    near = groups // 2
    other = other_ref[...].astype(F32)
    for g in range(groups):
        lanes = slice(g * 128, (g + 1) * 128)
        rate_g = rate2[:, lanes]
        half, place = g // near, g % near
        entry = jnp.zeros((n, 128), F32)
        for p in range(chips - 1):
            block = all_ref[2 * p + half].astype(F32)
            at = near * n + place
            whole = block[at : at + 1, :] + block[at + near : at + near + 1, :]
            longer = jnp.exp2(rate_g * whole) * entry + block[place * n : (place + 1) * n, :]
            entry = jnp.where(2 * p + 1 < mine, longer, entry)
        at = groups * n + g
        whole = other[at : at + 1, :] + other[at + groups : at + groups + 1, :]
        longer = jnp.exp2(rate_g * whole) * entry + other[g * n : (g + 1) * n, :]
        entry = jnp.where(second_core, longer, entry)
        entry_g = jnp.broadcast_to(entry[:, None, :], (n, 16, 128))
        thr = thr_ref[:, lanes]

        def turn(i, _):
            at = pl.ds(pl.multiple_of(i * 16, 16), 16)
            y = y_ref[at, lanes] + jnp.sum(grow_ref[i, :, :, lanes].astype(F32) * entry_g, axis=0)
            out_ref[at, lanes] = (y / (1.0 + jnp.exp(-4.0 * (y - thr)))).astype(BF16)
            return 0

        lax.fori_loop(0, blocks, turn, 0, unroll=blocks)


def call(kernel, outs, ins, scratch=(), flops=0, specs=None, vmem=12 << 20, outs_in=None):
    specs = specs or [VMEM] * len(ins)
    return pl.pallas_call(
        kernel,
        out_shape=outs,
        in_specs=specs,
        out_specs=outs_in or jax.tree.map(lambda _: VMEM, outs),
        scratch_shapes=scratch,
        cost_estimate=pl.CostEstimate(flops=flops, bytes_accessed=flops // 64, transcendentals=0),
        compiler_params=pltpu.CompilerParams(vmem_limit_bytes=vmem),
    )(*[pltpu.with_memory_space_constraint(x, pltpu.HBM) if spec is HBM else x for x, spec in zip(ins, specs)])


def per_device(
    tokens, in_weight, conv_weight, conv_bias, proj_weight, dt_weight, dt_bias, a_log, skip_gain, threshold
):
    rows = tokens.shape[0]
    width = in_weight.shape[1]
    taps = conv_weight.shape[0]
    rank = dt_weight.shape[0]
    n = a_log.shape[0]
    shards = lax.axis_size("tp")
    peers = lax.axis_size("seq")
    sums = rank + 2 * n
    lanes = -(-sums // 128) * 128
    bias = conv_bias[None]
    proj = proj_weight.T
    kept = (KEEP * tokens.shape[1], width)
    held = (
        pltpu.VMEM(conv_weight.shape, F32),
        pltpu.VMEM(bias.shape, F32),
        pltpu.VMEM(proj.shape, BF16),
    )

    most = call(
        rows_kernel,
        struct((rows - 1, tokens.shape[1]), BF16),
        (tokens,),
        (pltpu.VMEM(tokens.shape, BF16), pltpu.SemaphoreType.DMA),
        flops=1 << 34,
        specs=[HBM],
    )
    main = lax.all_gather(most, "tp")
    send, edge, u, keep = call(
        project_kernel,
        (struct((shards, 8, lanes), BF16), struct((16, width), BF16), struct((rows, width), BF16),
         struct(kept, BF16)),
        (main, in_weight, tokens, conv_weight, bias, proj),
        (pltpu.VMEM((rows + 8, width), F32), pltpu.VMEM((shards, 8, lanes), F32))
        + held
        + (pltpu.VMEM((8, tokens.shape[1]), BF16), pltpu.SemaphoreType.DMA((4,))),
        flops=1 << 29,
        specs=[VMEM] * 2 + [HBM] * 4,
    )
    rim = lax.ppermute(edge[:8], "seq", [(i, i + 1) for i in range(peers - 1)])
    got = lax.all_to_all(send, "tp", 0, 0)
    mix, late_u = call(
        late_kernel,
        (struct((shards, 8, rank + 256), BF16), struct((8, width), BF16)),
        (got, rim, edge, keep, in_weight, conv_weight, bias, proj),
        (
            pltpu.VMEM((shards, 8, lanes), F32),
            pltpu.VMEM((shards, tokens.shape[1]), F32),
            pltpu.VMEM((16, width), F32),
            pltpu.VMEM((8, rank + 256), F32),
        )
        + (pltpu.VMEM((in_weight.shape[0] - kept[0], width), BF16),)
        + held
        + (pltpu.SemaphoreType.DMA((shards + 3,)),),
        flops=1 << 28,
        specs=[VMEM] * 4 + [HBM] * 4,
    )
    mix = lax.all_to_all(mix, "tp", 0, 0)
    whole = struct((rows, width), F32)
    step, coef, own = call(
        state_kernel,
        (whole, struct((rows, 2 * n), F32), struct(((n + 2) * width // 128, 128), BF16)),
        (mix, dt_weight, dt_bias[None], a_log, u, late_u),
        (
            pltpu.VMEM((rows, width), F32),
            pltpu.VMEM((rows // 8, 8, width), F32),
            pltpu.VMEM((rows // 8, 8, width), F32),
            pltpu.VMEM((rows // 8, n, 8, 128), F32),
            pltpu.VMEM((n, width), F32),
            pltpu.VMEM((rows, rank), F32),
        ),
        flops=1 << 26,
    )
    mine = lax.axis_index("seq").astype(jnp.int32)[None]
    other = lax.ppermute(own, "seq", [(i, i ^ 1) for i in range(peers)])
    half = (n + 2) * width // 256
    pay = call(
        merge_kernel,
        struct((peers, half, 128), BF16),
        (mine, own, other, a_log),
        (pltpu.VMEM((half, 128), F32),),
        flops=1 << 20,
        specs=[SMEM] + [VMEM] * 3,
    )
    pay, coef = lax.optimization_barrier((pay, coef))
    everyone = lax.all_to_all(pay, "seq", 0, 0)
    y_local, grow = call(
        local_kernel,
        (whole, struct((rows // 16, n, 16, width), BF16)),
        (coef, a_log, u, late_u, step, skip_gain[None]),
        (
            pltpu.VMEM((rows, n, 128), F32),
            pltpu.VMEM((rows, n, 128), F32),
            pltpu.VMEM((rows // 16, n, 16, 128), F32),
            pltpu.VMEM((rows, width), F32),
            pltpu.VMEM((rows // 8, 8, width), F32),
            pltpu.VMEM((rows, width), F32),
        ),
        flops=1 << 28,
    )
    return call(
        final_kernel,
        struct((rows, width), BF16),
        (mine, everyone, other, a_log, y_local, grow, threshold[None]),
        flops=1 << 26,
        specs=[SMEM] + [VMEM] * 6,
    )


def solution(mesh):
    return jax.shard_map(
        per_device,
        mesh=mesh,
        in_specs=(
            P("seq", "tp"),
            P(None, "tp"),
            P(None, "tp"),
            P("tp"),
            P("tp", None),
            P(None, "tp"),
            P("tp"),
            P(None, "tp"),
            P("tp"),
            P("tp"),
        ),
        out_specs=P("seq", "tp"),
        check_vma=False,
    )
```

```python
import math

import jax
import jax.numpy as jnp
from jax import lax
from jax.experimental import pallas as pl
from jax.experimental.pallas import tpu as pltpu
from jax.sharding import PartitionSpec as P

LOG2E = math.log2(math.e)
F32 = jnp.float32
BF16 = jnp.bfloat16
VMEM = pl.BlockSpec(memory_space=pltpu.VMEM)
SMEM = pl.BlockSpec(memory_space=pltpu.SMEM)
HBM = pl.BlockSpec(memory_space=pltpu.HBM)


def struct(shape, dtype):
    return jax.ShapeDtypeStruct(shape, dtype)


def silu(v):
    return v / (1.0 + jnp.exp(-v))


def convolve(taps_ref, bias_ref, pad_ref, rows, width):
    taps = taps_ref.shape[0]
    pre = jnp.broadcast_to(bias_ref[...], (rows, width))
    for k in range(taps):
        first = 9 - taps + k
        pre = pre + taps_ref[k : k + 1, :] * pad_ref[first : first + rows, :]
    return silu(pre).astype(BF16)


def pieces(depth, room):
    return [(at, min(room, depth - at)) for at in range(0, depth, room)]


def project_rows(u, proj_ref):
    return lax.dot_general(u, proj_ref[...], (((1,), (1,)), ((), ())), preferred_element_type=F32)


KEEP = 12


def fetches(pairs, sems):
    return [pltpu.make_async_copy(src, dst, sems.at[i]) for i, (src, dst) in enumerate(pairs)]


def weight_part(keep_ref, buf_ref, z, depth):
    if z < KEEP:
        return keep_ref.at[pl.ds(z * depth, depth)]
    return buf_ref.at[pl.ds((z - KEEP) * depth, depth)]


def rows_kernel(tokens_hbm, out_ref, tokens_ref, sem):
    copy = pltpu.make_async_copy(tokens_hbm, tokens_ref, sem)
    copy.start()
    copy.wait()
    out_ref[...] = tokens_ref[...].astype(F32)[1:, :].astype(BF16)


def project_kernel(
    main_ref, weight_ref, tokens_hbm, taps_hbm, bias_hbm, proj_hbm,
    send_ref, edge_ref, u_ref, keep_ref,
    pad_ref, wide_ref, taps_ref, bias_ref, proj_ref, tokens_ref, sems,
):
    shards, held, depth = main_ref.shape
    rows, width = u_ref.shape
    sums = proj_ref.shape[0]
    copies = fetches(
        [(proj_hbm, proj_ref), (taps_hbm, taps_ref), (bias_hbm, bias_ref),
         (tokens_hbm.at[pl.ds(0, 8)], tokens_ref)]
        + [(weight_ref.at[pl.ds(z * depth, depth)], keep_ref.at[pl.ds(z * depth, depth)]) for z in range(KEEP)],
        sems,
    )
    for copy in copies:
        copy.start()
    pad_ref[:16, :] = jnp.zeros((16, width), F32)
    acc = jnp.zeros((held, width), F32)
    for z in range(shards):
        w = weight_ref[z * depth : (z + 1) * depth, :]
        acc = acc + jnp.dot(main_ref[z], w, preferred_element_type=F32)
    for copy in copies[:4]:
        copy.wait()
    pad_ref[8 + rows - held :, :] = acc.astype(BF16).astype(F32)
    edge_ref[:8, :] = pad_ref[rows : rows + 8, :].astype(BF16)
    edge_ref[8:, :] = pad_ref[8:16, :].astype(BF16)
    u = convolve(taps_ref, bias_ref, pad_ref, rows, width)
    u_ref[...] = u
    wide_ref[:, :, :sums] = project_rows(u, proj_ref).reshape(shards, 8, sums)
    late = tokens_ref[...].astype(F32)[0:1, :]
    room = wide_ref.shape[2] - sums
    row_ids = lax.broadcasted_iota(jnp.int32, (8, room), 0)
    block = jnp.zeros((8, room), F32)
    for p, (at, size) in enumerate(pieces(depth, room)):
        piece = late[:, at : at + size]
        if size < room:
            piece = jnp.concatenate([piece, jnp.zeros((1, room - size), F32)], axis=1)
        block = jnp.where(row_ids == p, jnp.broadcast_to(piece, (8, room)), block)
    wide_ref[:, :, sums:] = jnp.broadcast_to(block[None], (shards, 8, room))
    send_ref[...] = wide_ref[...].astype(BF16)
    for copy in copies[4:]:
        copy.wait()


def late_kernel(
    got_ref, rim_ref, edge_ref, keep_ref, weight_hbm, taps_hbm, bias_hbm, proj_hbm,
    mix_ref, u_ref,
    wide_ref, first_ref, pad_ref, pay_ref, weight_ref, taps_ref, bias_ref, proj_ref, sems,
):
    shards, _, lanes = got_ref.shape
    depth = first_ref.shape[1]
    width = weight_ref.shape[1]
    sums = proj_ref.shape[0]
    copies = fetches(
        [
            (weight_hbm.at[pl.ds(z * depth, depth)], weight_part(keep_ref, weight_ref, z, depth))
            for z in range(KEEP, shards)
        ]
        + [(proj_hbm, proj_ref), (taps_hbm, taps_ref), (bias_hbm, bias_ref)],
        sems,
    )
    for copy in copies:
        copy.start()
    room = lanes - sums
    wide_ref[...] = got_ref[...].astype(F32)
    for p, (at, size) in enumerate(pieces(depth, room)):
        first_ref[:, at : at + size] = wide_ref[:, p, sums : sums + size]
    total = jnp.sum(wide_ref[:, :, :sums], axis=0)
    high = total.astype(BF16).astype(F32)
    rank = mix_ref.shape[2] - 256
    coefs = sums - rank
    pay_ref[...] = jnp.zeros_like(pay_ref)
    pay_ref[:, :sums] = high
    pay_ref[:, sums : sums + coefs] = total[:, rank:] - high[:, rank:]
    pad_ref[:8, :] = rim_ref[...].astype(F32)
    pad_ref[8:, :] = edge_ref[8:, :].astype(F32)
    first = first_ref[...]
    row_ids = lax.broadcasted_iota(jnp.int32, (shards, depth), 0)
    acc = jnp.zeros((shards, width), F32)
    for z in range(shards):
        if z >= KEEP:
            copies[z - KEEP].wait()
        w = weight_part(keep_ref, weight_ref, z, depth)[...]
        only = jnp.where(row_ids == z, first, 0.0).astype(BF16)
        acc = acc + jnp.dot(only, w, preferred_element_type=F32)
    for copy in copies[shards - KEEP :]:
        copy.wait()
    pad_ref[8:9, :] = jnp.sum(acc, axis=0, keepdims=True).astype(BF16).astype(F32)
    u = convolve(taps_ref, bias_ref, pad_ref, 8, width)
    u_ref[...] = u
    part = project_rows(u, proj_ref)
    half = sums // 2
    late = taps_ref.shape[0]
    at = sums + coefs
    pay_ref[:late, at : at + half] = part[:late, :half]
    pay_ref[late : 2 * late, at : at + half] = part[:late, half:]
    pay = pay_ref[...].astype(BF16)
    for z in range(shards):
        mix_ref[z] = pay


def split2(x):
    a = x.astype(BF16)
    return a, (x - a.astype(F32)).astype(BF16)


def running_sum(x):
    rows = x.shape[0]
    row_ids = lax.broadcasted_iota(jnp.int32, (rows, rows), 0)
    col_ids = lax.broadcasted_iota(jnp.int32, (rows, rows), 1)
    lower = (row_ids >= col_ids).astype(F32).astype(BF16)
    return sum(jnp.dot(lower, p, preferred_element_type=F32) for p in split2(x)[::-1])


def state_kernel(
    mix_ref, dtw_ref, dtb_ref, alog_ref, u_ref, late_u_ref,
    step_ref, coef_ref, pack_ref,
    uf_ref, flow_ref, left_ref, bx_ref, rate_ref, low_ref,
):
    shards, each, _ = mix_ref.shape
    rows, width = u_ref.shape
    rank = dtw_ref.shape[0]
    n = alog_ref.shape[0]
    sums = rank + 2 * n
    half = sums // 2
    at = sums + 2 * n
    late = each // 2
    tiles = rows // 8
    low_ref[...] = mix_ref[:, :, :rank].astype(F32).reshape(rows, rank)
    coef = mix_ref[:, :, rank:sums].astype(F32) + mix_ref[:, :, sums:at].astype(F32)
    coef_ref[...] = coef.reshape(rows, 2 * n)
    pairs = jnp.sum(mix_ref[:, :, at : at + half].astype(F32), axis=0)
    early = jnp.concatenate([pairs[:late], pairs[late:]], axis=1)
    low_ref[:late, :] = early[:, :rank]
    coef_ref[:late, :] = early[:, rank:]
    low = low_ref[...].astype(BF16)
    rate_ref[...] = -jnp.exp(alog_ref[...]) * LOG2E
    uf_ref[...] = u_ref[...].astype(F32)
    uf_ref[:8, :] = late_u_ref[...].astype(F32)
    b = coef_ref[:, :n]
    for i in range(n):
        bx_ref[:, i] = jnp.broadcast_to(b[:, i : i + 1], (rows, 128)).reshape(tiles, 8, 128)
    groups = width // 128
    span = 128
    for h in range(width // span):
        cols = slice(h * span, (h + 1) * span)
        v = jnp.dot(low, dtw_ref[:, cols], preferred_element_type=F32) + dtb_ref[:, cols]
        step = jnp.maximum(v, 0.0) + jnp.log1p(jnp.exp(-jnp.abs(v)))
        step_ref[:, cols] = step
        cum = running_sum(step)
        whole = cum[rows - 1 : rows, :]
        left_ref[:, :, cols] = (whole - cum).reshape(tiles, 8, span)
        flow_ref[:, :, cols] = (step * uf_ref[:, cols]).reshape(tiles, 8, span)
        for k in range(span // 128):
            g = h * (span // 128) + k
            lanes = slice(g * 128, (g + 1) * 128)
            hi, lo = split2(whole[:, k * 128 : (k + 1) * 128])
            ends = []
            for first in range(0, n, 8):
                rates = [jnp.broadcast_to(rate_ref[i : i + 1, lanes], (8, 128)) for i in range(first, first + 8)]
                accs = [None] * 8
                for t in range(tiles):
                    left = left_ref[t, :, lanes]
                    flow = flow_ref[t, :, lanes]
                    for i in range(8):
                        term = jnp.exp2(rates[i] * left) * (flow * bx_ref[t, first + i])
                        accs[i] = term if t == 0 else accs[i] + term
                ends += [jnp.sum(acc, axis=0, keepdims=True) for acc in accs]
            pack_ref[g * n : (g + 1) * n, :] = jnp.concatenate(ends, axis=0).astype(BF16)
            low_ref[g : g + 1, :128] = hi.astype(F32)
            low_ref[groups + g : groups + g + 1, :128] = lo.astype(F32)
    pack_ref[groups * n :, :] = low_ref[: 2 * groups, :128].astype(BF16)


def merge_kernel(mine_ref, own_ref, other_ref, alog_ref, pay_ref, pack_ref):
    n, width = alog_ref.shape
    groups = width // 128
    near = groups // 2
    second_core = lax.rem(mine_ref[0], 2) == 1
    own = own_ref[...].astype(F32)
    other = other_ref[...].astype(F32)
    early = jnp.where(second_core, other, own)
    later = jnp.where(second_core, own, other)
    rate2 = -jnp.exp(alog_ref[...]) * LOG2E

    def rows(block, g, first, size):
        low = block[first + g * size : first + (g + 1) * size, :]
        high = block[first + (near + g) * size : first + (near + g + 1) * size, :]
        return jnp.where(second_core, high, low)

    for g in range(near):
        at = groups * n
        sum_early = rows(early, g, at, 1) + rows(early, g, at + groups, 1)
        sum_later = rows(later, g, at, 1) + rows(later, g, at + groups, 1)
        rate_g = jnp.where(
            second_core,
            rate2[:, (near + g) * 128 : (near + g + 1) * 128],
            rate2[:, g * 128 : (g + 1) * 128],
        )
        pack_ref[g * n : (g + 1) * n, :] = (
            jnp.exp2(rate_g * sum_later) * rows(early, g, 0, n) + rows(later, g, 0, n)
        )
        hi, lo = split2(sum_early + sum_later)
        pack_ref[near * n + g : near * n + g + 1, :] = hi.astype(F32)
        pack_ref[near * n + near + g : near * n + near + g + 1, :] = lo.astype(F32)
    pack = pack_ref[...].astype(BF16)
    for p in range(pay_ref.shape[0]):
        pay_ref[p] = pack


def local_kernel(
    coef_ref, alog_ref, u_ref, late_u_ref, step_ref, skip_ref,
    y_ref, grow_ref, bt_ref, ct_ref, cx_ref, uf_ref, flow_ref, cum_ref,
):
    rows, width = u_ref.shape
    uf_ref[...] = u_ref[...].astype(F32)
    uf_ref[:8, :] = late_u_ref[...].astype(F32)
    flow_ref[...] = (step_ref[...] * uf_ref[...]).reshape(rows // 8, 8, width)
    cum_ref[...] = running_sum(step_ref[...])
    n = alog_ref.shape[0]
    blocks = rows // 16
    b, c = coef_ref[:, :n], coef_ref[:, n:]
    rate2 = -jnp.exp(alog_ref[...]) * LOG2E
    for i in range(n):
        cx_ref[:, i] = jnp.broadcast_to(c[:, i : i + 1], (rows, 128)).reshape(blocks, 16, 128)
    b_t, c_t = b.T, c.T
    for t in range(rows):
        bt_ref[t] = jnp.broadcast_to(b_t[:, t : t + 1], (n, 128))
        ct_ref[t] = jnp.broadcast_to(c_t[:, t : t + 1], (n, 128))
    groups = width // 128

    def block_turn(i, state):
        for r in range(8):
            t = i * 8 + r
            d = step_ref[pl.ds(t, 1), :]
            f = flow_ref[i, r : r + 1, :]
            bt = jnp.concatenate([bt_ref[t]] * groups, axis=1)
            ct = jnp.concatenate([ct_ref[t]] * groups, axis=1)
            state = jnp.exp2(rate2 * d) * state + bt * f
            y_ref[pl.ds(t, 1), :] = jnp.sum(ct * state, axis=0, keepdims=True)
        return state

    lax.fori_loop(0, rows // 8, block_turn, jnp.zeros((n, width), F32))
    y_ref[...] = y_ref[...] + skip_ref[...] * uf_ref[...]

    for g in range(groups):
        lanes = slice(g * 128, (g + 1) * 128)
        rate_g = jnp.broadcast_to(rate2[:, None, lanes], (n, 16, 128))

        def fill(i, _):
            cum = cum_ref[pl.ds(pl.multiple_of(i * 16, 16), 16), lanes]
            grow_ref[i, :, :, lanes] = (cx_ref[i] * jnp.exp2(rate_g * cum[None])).astype(BF16)
            return 0

        lax.fori_loop(0, blocks, fill, 0)


def final_kernel(mine_ref, all_ref, other_ref, alog_ref, y_ref, grow_ref, thr_ref, out_ref):
    rows, width = y_ref.shape
    n = alog_ref.shape[0]
    blocks = rows // 16
    chips = all_ref.shape[0] // 2
    mine = mine_ref[0]
    second_core = lax.rem(mine, 2) == 1
    rate2 = -jnp.exp(alog_ref[...]) * LOG2E
    groups = width // 128
    near = groups // 2
    other = other_ref[...].astype(F32)
    for g in range(groups):
        lanes = slice(g * 128, (g + 1) * 128)
        rate_g = rate2[:, lanes]
        half, place = g // near, g % near
        entry = jnp.zeros((n, 128), F32)
        for p in range(chips - 1):
            block = all_ref[2 * p + half].astype(F32)
            at = near * n + place
            whole = block[at : at + 1, :] + block[at + near : at + near + 1, :]
            longer = jnp.exp2(rate_g * whole) * entry + block[place * n : (place + 1) * n, :]
            entry = jnp.where(2 * p + 1 < mine, longer, entry)
        at = groups * n + g
        whole = other[at : at + 1, :] + other[at + groups : at + groups + 1, :]
        longer = jnp.exp2(rate_g * whole) * entry + other[g * n : (g + 1) * n, :]
        entry = jnp.where(second_core, longer, entry)
        entry_g = jnp.broadcast_to(entry[:, None, :], (n, 16, 128))
        thr = thr_ref[:, lanes]

        def turn(i, _):
            at = pl.ds(pl.multiple_of(i * 16, 16), 16)
            y = y_ref[at, lanes] + jnp.sum(grow_ref[i, :, :, lanes].astype(F32) * entry_g, axis=0)
            out_ref[at, lanes] = (y / (1.0 + jnp.exp(-4.0 * (y - thr)))).astype(BF16)
            return 0

        lax.fori_loop(0, blocks, turn, 0, unroll=blocks)


def call(kernel, outs, ins, scratch=(), flops=0, specs=None, vmem=12 << 20, outs_in=None):
    specs = specs or [VMEM] * len(ins)
    return pl.pallas_call(
        kernel,
        out_shape=outs,
        in_specs=specs,
        out_specs=outs_in or jax.tree.map(lambda _: VMEM, outs),
        scratch_shapes=scratch,
        cost_estimate=pl.CostEstimate(flops=flops, bytes_accessed=flops // 64, transcendentals=0),
        compiler_params=pltpu.CompilerParams(vmem_limit_bytes=vmem),
    )(*[pltpu.with_memory_space_constraint(x, pltpu.HBM) if spec is HBM else x for x, spec in zip(ins, specs)])


def per_device(
    tokens, in_weight, conv_weight, conv_bias, proj_weight, dt_weight, dt_bias, a_log, skip_gain, threshold
):
    rows = tokens.shape[0]
    width = in_weight.shape[1]
    taps = conv_weight.shape[0]
    rank = dt_weight.shape[0]
    n = a_log.shape[0]
    shards = lax.axis_size("tp")
    peers = lax.axis_size("seq")
    sums = rank + 2 * n
    lanes = -(-sums // 128) * 128
    bias = conv_bias[None]
    proj = proj_weight.T
    kept = (KEEP * tokens.shape[1], width)
    held = (
        pltpu.VMEM(conv_weight.shape, F32),
        pltpu.VMEM(bias.shape, F32),
        pltpu.VMEM(proj.shape, BF16),
    )

    most = call(
        rows_kernel,
        struct((rows - 1, tokens.shape[1]), BF16),
        (tokens,),
        (pltpu.VMEM(tokens.shape, BF16), pltpu.SemaphoreType.DMA),
        flops=1 << 34,
        specs=[HBM],
    )
    main = lax.all_gather(most, "tp")
    send, edge, u, keep = call(
        project_kernel,
        (struct((shards, 8, lanes), BF16), struct((16, width), BF16), struct((rows, width), BF16),
         struct(kept, BF16)),
        (main, in_weight, tokens, conv_weight, bias, proj),
        (pltpu.VMEM((rows + 8, width), F32), pltpu.VMEM((shards, 8, lanes), F32))
        + held
        + (pltpu.VMEM((8, tokens.shape[1]), BF16), pltpu.SemaphoreType.DMA((4 + KEEP,))),
        flops=1 << 29,
        specs=[VMEM] * 2 + [HBM] * 4,
    )
    rim = lax.ppermute(edge[:8], "seq", [(i, i + 1) for i in range(peers - 1)])
    got = lax.all_to_all(send, "tp", 0, 0)
    mix, late_u = call(
        late_kernel,
        (struct((shards, 8, rank + 256), BF16), struct((8, width), BF16)),
        (got, rim, edge, keep, in_weight, conv_weight, bias, proj),
        (
            pltpu.VMEM((shards, 8, lanes), F32),
            pltpu.VMEM((shards, tokens.shape[1]), F32),
            pltpu.VMEM((16, width), F32),
            pltpu.VMEM((8, rank + 256), F32),
        )
        + (pltpu.VMEM((in_weight.shape[0] - kept[0], width), BF16),)
        + held
        + (pltpu.SemaphoreType.DMA((shards + 3,)),),
        flops=1 << 28,
        specs=[VMEM] * 4 + [HBM] * 4,
    )
    mix = lax.all_to_all(mix, "tp", 0, 0)
    whole = struct((rows, width), F32)
    step, coef, own = call(
        state_kernel,
        (whole, struct((rows, 2 * n), F32), struct(((n + 2) * width // 128, 128), BF16)),
        (mix, dt_weight, dt_bias[None], a_log, u, late_u),
        (
            pltpu.VMEM((rows, width), F32),
            pltpu.VMEM((rows // 8, 8, width), F32),
            pltpu.VMEM((rows // 8, 8, width), F32),
            pltpu.VMEM((rows // 8, n, 8, 128), F32),
            pltpu.VMEM((n, width), F32),
            pltpu.VMEM((rows, rank), F32),
        ),
        flops=1 << 26,
    )
    mine = lax.axis_index("seq").astype(jnp.int32)[None]
    other = lax.ppermute(own, "seq", [(i, i ^ 1) for i in range(peers)])
    half = (n + 2) * width // 256
    pay = call(
        merge_kernel,
        struct((peers, half, 128), BF16),
        (mine, own, other, a_log),
        (pltpu.VMEM((half, 128), F32),),
        flops=1 << 20,
        specs=[SMEM] + [VMEM] * 3,
    )
    pay, coef = lax.optimization_barrier((pay, coef))
    everyone = lax.all_to_all(pay, "seq", 0, 0)
    y_local, grow = call(
        local_kernel,
        (whole, struct((rows // 16, n, 16, width), BF16)),
        (coef, a_log, u, late_u, step, skip_gain[None]),
        (
            pltpu.VMEM((rows, n, 128), F32),
            pltpu.VMEM((rows, n, 128), F32),
            pltpu.VMEM((rows // 16, n, 16, 128), F32),
            pltpu.VMEM((rows, width), F32),
            pltpu.VMEM((rows // 8, 8, width), F32),
            pltpu.VMEM((rows, width), F32),
        ),
        flops=1 << 28,
    )
    return call(
        final_kernel,
        struct((rows, width), BF16),
        (mine, everyone, other, a_log, y_local, grow, threshold[None]),
        flops=1 << 26,
        specs=[SMEM] + [VMEM] * 6,
    )


def solution(mesh):
    return jax.shard_map(
        per_device,
        mesh=mesh,
        in_specs=(
            P("seq", "tp"),
            P(None, "tp"),
            P(None, "tp"),
            P("tp"),
            P("tp", None),
            P(None, "tp"),
            P("tp"),
            P(None, "tp"),
            P("tp"),
            P("tp"),
        ),
        out_specs=P("seq", "tp"),
        check_vma=False,
    )
```

```python
import math

import jax
import jax.numpy as jnp
from jax import lax
from jax.experimental import pallas as pl
from jax.experimental.pallas import tpu as pltpu
from jax.sharding import PartitionSpec as P

LOG2E = math.log2(math.e)
F32 = jnp.float32
BF16 = jnp.bfloat16
VMEM = pl.BlockSpec(memory_space=pltpu.VMEM)
SMEM = pl.BlockSpec(memory_space=pltpu.SMEM)
HBM = pl.BlockSpec(memory_space=pltpu.HBM)


def struct(shape, dtype):
    return jax.ShapeDtypeStruct(shape, dtype)


def silu(v):
    return v / (1.0 + jnp.exp(-v))


def convolve(taps_ref, bias_ref, pad_ref, rows, width):
    taps = taps_ref.shape[0]
    pre = jnp.broadcast_to(bias_ref[...], (rows, width))
    for k in range(taps):
        first = 9 - taps + k
        pre = pre + taps_ref[k : k + 1, :] * pad_ref[first : first + rows, :]
    return silu(pre).astype(BF16)


def pieces(depth, room):
    return [(at, min(room, depth - at)) for at in range(0, depth, room)]


def project_rows(u, proj_ref):
    return lax.dot_general(u, proj_ref[...], (((1,), (1,)), ((), ())), preferred_element_type=F32)


KEEP = 12


def fetches(pairs, sems):
    return [pltpu.make_async_copy(src, dst, sems.at[i]) for i, (src, dst) in enumerate(pairs)]


def weight_part(keep_ref, buf_ref, z, depth):
    if z < KEEP:
        return keep_ref.at[pl.ds(z * depth, depth)]
    return buf_ref.at[pl.ds((z - KEEP) * depth, depth)]


def rows_kernel(tokens_hbm, out_ref, tokens_ref, sem):
    copy = pltpu.make_async_copy(tokens_hbm, tokens_ref, sem)
    copy.start()
    copy.wait()
    out_ref[...] = tokens_ref[...].astype(F32)[1:, :].astype(BF16)


def project_kernel(
    main_ref, weight_ref, tokens_hbm, taps_hbm, bias_hbm, proj_hbm,
    send_ref, edge_ref, u_ref, keep_ref,
    pad_ref, wide_ref, taps_ref, bias_ref, proj_ref, tokens_ref, sems,
):
    shards, held, depth = main_ref.shape
    rows, width = u_ref.shape
    sums = proj_ref.shape[0]
    copies = fetches(
        [(proj_hbm, proj_ref), (taps_hbm, taps_ref), (bias_hbm, bias_ref),
         (tokens_hbm.at[pl.ds(0, 8)], tokens_ref)]
        + [(weight_ref.at[pl.ds(0, KEEP * depth)], keep_ref)],
        sems,
    )
    for copy in copies:
        copy.start()
    pad_ref[:16, :] = jnp.zeros((16, width), F32)
    acc = jnp.zeros((held, width), F32)
    for z in range(shards):
        w = weight_ref[z * depth : (z + 1) * depth, :]
        acc = acc + jnp.dot(main_ref[z], w, preferred_element_type=F32)
    for copy in copies[:4]:
        copy.wait()
    pad_ref[8 + rows - held :, :] = acc.astype(BF16).astype(F32)
    edge_ref[:8, :] = pad_ref[rows : rows + 8, :].astype(BF16)
    edge_ref[8:, :] = pad_ref[8:16, :].astype(BF16)
    u = convolve(taps_ref, bias_ref, pad_ref, rows, width)
    u_ref[...] = u
    wide_ref[:, :, :sums] = project_rows(u, proj_ref).reshape(shards, 8, sums)
    late = tokens_ref[...].astype(F32)[0:1, :]
    room = wide_ref.shape[2] - sums
    row_ids = lax.broadcasted_iota(jnp.int32, (8, room), 0)
    block = jnp.zeros((8, room), F32)
    for p, (at, size) in enumerate(pieces(depth, room)):
        piece = late[:, at : at + size]
        if size < room:
            piece = jnp.concatenate([piece, jnp.zeros((1, room - size), F32)], axis=1)
        block = jnp.where(row_ids == p, jnp.broadcast_to(piece, (8, room)), block)
    wide_ref[:, :, sums:] = jnp.broadcast_to(block[None], (shards, 8, room))
    send_ref[...] = wide_ref[...].astype(BF16)
    copies[4].wait()


def late_kernel(
    got_ref, rim_ref, edge_ref, keep_ref, weight_hbm, taps_hbm, bias_hbm, proj_hbm,
    mix_ref, u_ref,
    wide_ref, first_ref, pad_ref, pay_ref, weight_ref, taps_ref, bias_ref, proj_ref, sems,
):
    shards, _, lanes = got_ref.shape
    depth = first_ref.shape[1]
    width = weight_ref.shape[1]
    sums = proj_ref.shape[0]
    copies = fetches(
        [
            (weight_hbm.at[pl.ds(z * depth, depth)], weight_part(keep_ref, weight_ref, z, depth))
            for z in range(KEEP, shards)
        ]
        + [(proj_hbm, proj_ref), (taps_hbm, taps_ref), (bias_hbm, bias_ref)],
        sems,
    )
    for copy in copies:
        copy.start()
    room = lanes - sums
    wide_ref[...] = got_ref[...].astype(F32)
    for p, (at, size) in enumerate(pieces(depth, room)):
        first_ref[:, at : at + size] = wide_ref[:, p, sums : sums + size]
    total = jnp.sum(wide_ref[:, :, :sums], axis=0)
    high = total.astype(BF16).astype(F32)
    rank = mix_ref.shape[2] - 256
    coefs = sums - rank
    pay_ref[...] = jnp.zeros_like(pay_ref)
    pay_ref[:, :sums] = high
    pay_ref[:, sums : sums + coefs] = total[:, rank:] - high[:, rank:]
    pad_ref[:8, :] = rim_ref[...].astype(F32)
    pad_ref[8:, :] = edge_ref[8:, :].astype(F32)
    first = first_ref[...]
    row_ids = lax.broadcasted_iota(jnp.int32, (shards, depth), 0)
    acc = jnp.zeros((shards, width), F32)
    for z in range(shards):
        if z >= KEEP:
            copies[z - KEEP].wait()
        w = weight_part(keep_ref, weight_ref, z, depth)[...]
        only = jnp.where(row_ids == z, first, 0.0).astype(BF16)
        acc = acc + jnp.dot(only, w, preferred_element_type=F32)
    for copy in copies[shards - KEEP :]:
        copy.wait()
    pad_ref[8:9, :] = jnp.sum(acc, axis=0, keepdims=True).astype(BF16).astype(F32)
    u = convolve(taps_ref, bias_ref, pad_ref, 8, width)
    u_ref[...] = u
    part = project_rows(u, proj_ref)
    half = sums // 2
    late = taps_ref.shape[0]
    at = sums + coefs
    pay_ref[:late, at : at + half] = part[:late, :half]
    pay_ref[late : 2 * late, at : at + half] = part[:late, half:]
    pay = pay_ref[...].astype(BF16)
    for z in range(shards):
        mix_ref[z] = pay


def split2(x):
    a = x.astype(BF16)
    return a, (x - a.astype(F32)).astype(BF16)


def running_sum(x):
    rows = x.shape[0]
    row_ids = lax.broadcasted_iota(jnp.int32, (rows, rows), 0)
    col_ids = lax.broadcasted_iota(jnp.int32, (rows, rows), 1)
    lower = (row_ids >= col_ids).astype(F32).astype(BF16)
    return sum(jnp.dot(lower, p, preferred_element_type=F32) for p in split2(x)[::-1])


def state_kernel(
    mix_ref, dtw_ref, dtb_ref, alog_ref, u_ref, late_u_ref,
    step_ref, coef_ref, pack_ref,
    uf_ref, flow_ref, left_ref, bx_ref, rate_ref, low_ref,
):
    shards, each, _ = mix_ref.shape
    rows, width = u_ref.shape
    rank = dtw_ref.shape[0]
    n = alog_ref.shape[0]
    sums = rank + 2 * n
    half = sums // 2
    at = sums + 2 * n
    late = each // 2
    tiles = rows // 8
    low_ref[...] = mix_ref[:, :, :rank].astype(F32).reshape(rows, rank)
    coef = mix_ref[:, :, rank:sums].astype(F32) + mix_ref[:, :, sums:at].astype(F32)
    coef_ref[...] = coef.reshape(rows, 2 * n)
    pairs = jnp.sum(mix_ref[:, :, at : at + half].astype(F32), axis=0)
    early = jnp.concatenate([pairs[:late], pairs[late:]], axis=1)
    low_ref[:late, :] = early[:, :rank]
    coef_ref[:late, :] = early[:, rank:]
    low = low_ref[...].astype(BF16)
    rate_ref[...] = -jnp.exp(alog_ref[...]) * LOG2E
    uf_ref[...] = u_ref[...].astype(F32)
    uf_ref[:8, :] = late_u_ref[...].astype(F32)
    b = coef_ref[:, :n]
    for i in range(n):
        bx_ref[:, i] = jnp.broadcast_to(b[:, i : i + 1], (rows, 128)).reshape(tiles, 8, 128)
    groups = width // 128
    span = 128
    for h in range(width // span):
        cols = slice(h * span, (h + 1) * span)
        v = jnp.dot(low, dtw_ref[:, cols], preferred_element_type=F32) + dtb_ref[:, cols]
        step = jnp.maximum(v, 0.0) + jnp.log1p(jnp.exp(-jnp.abs(v)))
        step_ref[:, cols] = step
        cum = running_sum(step)
        whole = cum[rows - 1 : rows, :]
        left_ref[:, :, cols] = (whole - cum).reshape(tiles, 8, span)
        flow_ref[:, :, cols] = (step * uf_ref[:, cols]).reshape(tiles, 8, span)
        for k in range(span // 128):
            g = h * (span // 128) + k
            lanes = slice(g * 128, (g + 1) * 128)
            hi, lo = split2(whole[:, k * 128 : (k + 1) * 128])
            ends = []
            for first in range(0, n, 8):
                rates = [jnp.broadcast_to(rate_ref[i : i + 1, lanes], (8, 128)) for i in range(first, first + 8)]
                accs = [None] * 8
                for t in range(tiles):
                    left = left_ref[t, :, lanes]
                    flow = flow_ref[t, :, lanes]
                    for i in range(8):
                        term = jnp.exp2(rates[i] * left) * (flow * bx_ref[t, first + i])
                        accs[i] = term if t == 0 else accs[i] + term
                ends += [jnp.sum(acc, axis=0, keepdims=True) for acc in accs]
            pack_ref[g * n : (g + 1) * n, :] = jnp.concatenate(ends, axis=0).astype(BF16)
            low_ref[g : g + 1, :128] = hi.astype(F32)
            low_ref[groups + g : groups + g + 1, :128] = lo.astype(F32)
    pack_ref[groups * n :, :] = low_ref[: 2 * groups, :128].astype(BF16)


def merge_kernel(mine_ref, own_ref, other_ref, alog_ref, pay_ref, pack_ref):
    n, width = alog_ref.shape
    groups = width // 128
    near = groups // 2
    second_core = lax.rem(mine_ref[0], 2) == 1
    own = own_ref[...].astype(F32)
    other = other_ref[...].astype(F32)
    early = jnp.where(second_core, other, own)
    later = jnp.where(second_core, own, other)
    rate2 = -jnp.exp(alog_ref[...]) * LOG2E

    def rows(block, g, first, size):
        low = block[first + g * size : first + (g + 1) * size, :]
        high = block[first + (near + g) * size : first + (near + g + 1) * size, :]
        return jnp.where(second_core, high, low)

    for g in range(near):
        at = groups * n
        sum_early = rows(early, g, at, 1) + rows(early, g, at + groups, 1)
        sum_later = rows(later, g, at, 1) + rows(later, g, at + groups, 1)
        rate_g = jnp.where(
            second_core,
            rate2[:, (near + g) * 128 : (near + g + 1) * 128],
            rate2[:, g * 128 : (g + 1) * 128],
        )
        pack_ref[g * n : (g + 1) * n, :] = (
            jnp.exp2(rate_g * sum_later) * rows(early, g, 0, n) + rows(later, g, 0, n)
        )
        hi, lo = split2(sum_early + sum_later)
        pack_ref[near * n + g : near * n + g + 1, :] = hi.astype(F32)
        pack_ref[near * n + near + g : near * n + near + g + 1, :] = lo.astype(F32)
    pack = pack_ref[...].astype(BF16)
    for p in range(pay_ref.shape[0]):
        pay_ref[p] = pack


def local_kernel(
    coef_ref, alog_ref, u_ref, late_u_ref, step_ref, skip_ref,
    y_ref, grow_ref, bt_ref, ct_ref, cx_ref, uf_ref, flow_ref, cum_ref,
):
    rows, width = u_ref.shape
    uf_ref[...] = u_ref[...].astype(F32)
    uf_ref[:8, :] = late_u_ref[...].astype(F32)
    flow_ref[...] = (step_ref[...] * uf_ref[...]).reshape(rows // 8, 8, width)
    cum_ref[...] = running_sum(step_ref[...])
    n = alog_ref.shape[0]
    blocks = rows // 16
    b, c = coef_ref[:, :n], coef_ref[:, n:]
    rate2 = -jnp.exp(alog_ref[...]) * LOG2E
    for i in range(n):
        cx_ref[:, i] = jnp.broadcast_to(c[:, i : i + 1], (rows, 128)).reshape(blocks, 16, 128)
    b_t, c_t = b.T, c.T
    for t in range(rows):
        bt_ref[t] = jnp.broadcast_to(b_t[:, t : t + 1], (n, 128))
        ct_ref[t] = jnp.broadcast_to(c_t[:, t : t + 1], (n, 128))
    groups = width // 128

    def block_turn(i, state):
        for r in range(8):
            t = i * 8 + r
            d = step_ref[pl.ds(t, 1), :]
            f = flow_ref[i, r : r + 1, :]
            bt = jnp.concatenate([bt_ref[t]] * groups, axis=1)
            ct = jnp.concatenate([ct_ref[t]] * groups, axis=1)
            state = jnp.exp2(rate2 * d) * state + bt * f
            y_ref[pl.ds(t, 1), :] = jnp.sum(ct * state, axis=0, keepdims=True)
        return state

    lax.fori_loop(0, rows // 8, block_turn, jnp.zeros((n, width), F32))
    y_ref[...] = y_ref[...] + skip_ref[...] * uf_ref[...]

    for g in range(groups):
        lanes = slice(g * 128, (g + 1) * 128)
        rate_g = jnp.broadcast_to(rate2[:, None, lanes], (n, 16, 128))

        def fill(i, _):
            cum = cum_ref[pl.ds(pl.multiple_of(i * 16, 16), 16), lanes]
            grow_ref[i, :, :, lanes] = (cx_ref[i] * jnp.exp2(rate_g * cum[None])).astype(BF16)
            return 0

        lax.fori_loop(0, blocks, fill, 0)


def final_kernel(mine_ref, all_ref, other_ref, alog_ref, y_ref, grow_ref, thr_ref, out_ref):
    rows, width = y_ref.shape
    n = alog_ref.shape[0]
    blocks = rows // 16
    chips = all_ref.shape[0] // 2
    mine = mine_ref[0]
    second_core = lax.rem(mine, 2) == 1
    rate2 = -jnp.exp(alog_ref[...]) * LOG2E
    groups = width // 128
    near = groups // 2
    other = other_ref[...].astype(F32)
    for g in range(groups):
        lanes = slice(g * 128, (g + 1) * 128)
        rate_g = rate2[:, lanes]
        half, place = g // near, g % near
        entry = jnp.zeros((n, 128), F32)
        for p in range(chips - 1):
            block = all_ref[2 * p + half].astype(F32)
            at = near * n + place
            whole = block[at : at + 1, :] + block[at + near : at + near + 1, :]
            longer = jnp.exp2(rate_g * whole) * entry + block[place * n : (place + 1) * n, :]
            entry = jnp.where(2 * p + 1 < mine, longer, entry)
        at = groups * n + g
        whole = other[at : at + 1, :] + other[at + groups : at + groups + 1, :]
        longer = jnp.exp2(rate_g * whole) * entry + other[g * n : (g + 1) * n, :]
        entry = jnp.where(second_core, longer, entry)
        entry_g = jnp.broadcast_to(entry[:, None, :], (n, 16, 128))
        thr = thr_ref[:, lanes]

        def turn(i, _):
            at = pl.ds(pl.multiple_of(i * 16, 16), 16)
            y = y_ref[at, lanes] + jnp.sum(grow_ref[i, :, :, lanes].astype(F32) * entry_g, axis=0)
            out_ref[at, lanes] = (y / (1.0 + jnp.exp(-4.0 * (y - thr)))).astype(BF16)
            return 0

        lax.fori_loop(0, blocks, turn, 0, unroll=blocks)


def call(kernel, outs, ins, scratch=(), flops=0, specs=None, vmem=12 << 20, outs_in=None):
    specs = specs or [VMEM] * len(ins)
    return pl.pallas_call(
        kernel,
        out_shape=outs,
        in_specs=specs,
        out_specs=outs_in or jax.tree.map(lambda _: VMEM, outs),
        scratch_shapes=scratch,
        cost_estimate=pl.CostEstimate(flops=flops, bytes_accessed=flops // 64, transcendentals=0),
        compiler_params=pltpu.CompilerParams(vmem_limit_bytes=vmem),
    )(*[pltpu.with_memory_space_constraint(x, pltpu.HBM) if spec is HBM else x for x, spec in zip(ins, specs)])


def per_device(
    tokens, in_weight, conv_weight, conv_bias, proj_weight, dt_weight, dt_bias, a_log, skip_gain, threshold
):
    rows = tokens.shape[0]
    width = in_weight.shape[1]
    taps = conv_weight.shape[0]
    rank = dt_weight.shape[0]
    n = a_log.shape[0]
    shards = lax.axis_size("tp")
    peers = lax.axis_size("seq")
    sums = rank + 2 * n
    lanes = -(-sums // 128) * 128
    bias = conv_bias[None]
    proj = proj_weight.T
    kept = (KEEP * tokens.shape[1], width)
    held = (
        pltpu.VMEM(conv_weight.shape, F32),
        pltpu.VMEM(bias.shape, F32),
        pltpu.VMEM(proj.shape, BF16),
    )

    most = call(
        rows_kernel,
        struct((rows - 1, tokens.shape[1]), BF16),
        (tokens,),
        (pltpu.VMEM(tokens.shape, BF16), pltpu.SemaphoreType.DMA),
        flops=1 << 34,
        specs=[HBM],
    )
    main = lax.all_gather(most, "tp")
    send, edge, u, keep = call(
        project_kernel,
        (struct((shards, 8, lanes), BF16), struct((16, width), BF16), struct((rows, width), BF16),
         struct(kept, BF16)),
        (main, in_weight, tokens, conv_weight, bias, proj),
        (pltpu.VMEM((rows + 8, width), F32), pltpu.VMEM((shards, 8, lanes), F32))
        + held
        + (pltpu.VMEM((8, tokens.shape[1]), BF16), pltpu.SemaphoreType.DMA((5,))),
        flops=1 << 29,
        specs=[VMEM] * 2 + [HBM] * 4,
    )
    rim = lax.ppermute(edge[:8], "seq", [(i, i + 1) for i in range(peers - 1)])
    got = lax.all_to_all(send, "tp", 0, 0)
    mix, late_u = call(
        late_kernel,
        (struct((shards, 8, rank + 256), BF16), struct((8, width), BF16)),
        (got, rim, edge, keep, in_weight, conv_weight, bias, proj),
        (
            pltpu.VMEM((shards, 8, lanes), F32),
            pltpu.VMEM((shards, tokens.shape[1]), F32),
            pltpu.VMEM((16, width), F32),
            pltpu.VMEM((8, rank + 256), F32),
        )
        + (pltpu.VMEM((in_weight.shape[0] - kept[0], width), BF16),)
        + held
        + (pltpu.SemaphoreType.DMA((shards + 3,)),),
        flops=1 << 28,
        specs=[VMEM] * 4 + [HBM] * 4,
    )
    mix = lax.all_to_all(mix, "tp", 0, 0)
    whole = struct((rows, width), F32)
    step, coef, own = call(
        state_kernel,
        (whole, struct((rows, 2 * n), F32), struct(((n + 2) * width // 128, 128), BF16)),
        (mix, dt_weight, dt_bias[None], a_log, u, late_u),
        (
            pltpu.VMEM((rows, width), F32),
            pltpu.VMEM((rows // 8, 8, width), F32),
            pltpu.VMEM((rows // 8, 8, width), F32),
            pltpu.VMEM((rows // 8, n, 8, 128), F32),
            pltpu.VMEM((n, width), F32),
            pltpu.VMEM((rows, rank), F32),
        ),
        flops=1 << 26,
    )
    mine = lax.axis_index("seq").astype(jnp.int32)[None]
    other = lax.ppermute(own, "seq", [(i, i ^ 1) for i in range(peers)])
    half = (n + 2) * width // 256
    pay = call(
        merge_kernel,
        struct((peers, half, 128), BF16),
        (mine, own, other, a_log),
        (pltpu.VMEM((half, 128), F32),),
        flops=1 << 20,
        specs=[SMEM] + [VMEM] * 3,
    )
    pay, coef = lax.optimization_barrier((pay, coef))
    everyone = lax.all_to_all(pay, "seq", 0, 0)
    y_local, grow = call(
        local_kernel,
        (whole, struct((rows // 16, n, 16, width), BF16)),
        (coef, a_log, u, late_u, step, skip_gain[None]),
        (
            pltpu.VMEM((rows, n, 128), F32),
            pltpu.VMEM((rows, n, 128), F32),
            pltpu.VMEM((rows // 16, n, 16, 128), F32),
            pltpu.VMEM((rows, width), F32),
            pltpu.VMEM((rows // 8, 8, width), F32),
            pltpu.VMEM((rows, width), F32),
        ),
        flops=1 << 28,
    )
    return call(
        final_kernel,
        struct((rows, width), BF16),
        (mine, everyone, other, a_log, y_local, grow, threshold[None]),
        flops=1 << 26,
        specs=[SMEM] + [VMEM] * 6,
    )


def solution(mesh):
    return jax.shard_map(
        per_device,
        mesh=mesh,
        in_specs=(
            P("seq", "tp"),
            P(None, "tp"),
            P(None, "tp"),
            P("tp"),
            P("tp", None),
            P(None, "tp"),
            P("tp"),
            P(None, "tp"),
            P("tp"),
            P("tp"),
        ),
        out_specs=P("seq", "tp"),
        check_vma=False,
    )
```

```python
import math

import jax
import jax.numpy as jnp
from jax import lax
from jax.experimental import pallas as pl
from jax.experimental.pallas import tpu as pltpu
from jax.sharding import PartitionSpec as P

LOG2E = math.log2(math.e)
F32 = jnp.float32
BF16 = jnp.bfloat16
VMEM = pl.BlockSpec(memory_space=pltpu.VMEM)
SMEM = pl.BlockSpec(memory_space=pltpu.SMEM)
HBM = pl.BlockSpec(memory_space=pltpu.HBM)


def struct(shape, dtype):
    return jax.ShapeDtypeStruct(shape, dtype)


def silu(v):
    return v / (1.0 + jnp.exp(-v))


def convolve(taps_ref, bias_ref, pad_ref, rows, width):
    taps = taps_ref.shape[0]
    pre = jnp.broadcast_to(bias_ref[...], (rows, width))
    for k in range(taps):
        first = 9 - taps + k
        pre = pre + taps_ref[k : k + 1, :] * pad_ref[first : first + rows, :]
    return silu(pre).astype(BF16)


def pieces(depth, room):
    return [(at, min(room, depth - at)) for at in range(0, depth, room)]


def project_rows(u, proj_ref):
    return lax.dot_general(u, proj_ref[...], (((1,), (1,)), ((), ())), preferred_element_type=F32)


KEEP = 12


def fetches(pairs, sems):
    return [pltpu.make_async_copy(src, dst, sems.at[i]) for i, (src, dst) in enumerate(pairs)]


def weight_part(keep_ref, buf_ref, z, depth):
    if z < KEEP:
        return keep_ref.at[pl.ds(z * depth, depth)]
    return buf_ref.at[pl.ds((z - KEEP) * depth, depth)]


def rows_kernel(tokens_hbm, out_ref, tokens_ref, sem):
    copy = pltpu.make_async_copy(tokens_hbm, tokens_ref, sem)
    copy.start()
    copy.wait()
    out_ref[...] = tokens_ref[...].astype(F32)[1:, :].astype(BF16)


def project_kernel(
    main_ref, weight_ref, tokens_hbm, taps_hbm, bias_hbm, proj_hbm,
    send_ref, edge_ref, u_ref, keep_ref,
    pad_ref, wide_ref, taps_ref, bias_ref, proj_ref, tokens_ref, sems,
):
    shards, held, depth = main_ref.shape
    rows, width = u_ref.shape
    sums = proj_ref.shape[0]
    copies = fetches(
        [(proj_hbm, proj_ref), (taps_hbm, taps_ref), (bias_hbm, bias_ref),
         (tokens_hbm.at[pl.ds(0, 8)], tokens_ref),
         (weight_ref.at[pl.ds(0, KEEP * depth)], keep_ref)],
        sems,
    )
    for copy in copies:
        copy.start()
    pad_ref[:16, :] = jnp.zeros((16, width), F32)
    acc = jnp.zeros((held, width), F32)
    for z in range(shards):
        w = weight_ref[z * depth : (z + 1) * depth, :]
        acc = acc + jnp.dot(main_ref[z], w, preferred_element_type=F32)
    for copy in copies[:4]:
        copy.wait()
    pad_ref[8 + rows - held :, :] = acc.astype(BF16).astype(F32)
    edge_ref[:8, :] = pad_ref[rows : rows + 8, :].astype(BF16)
    edge_ref[8:, :] = pad_ref[8:16, :].astype(BF16)
    u = convolve(taps_ref, bias_ref, pad_ref, rows, width)
    u_ref[...] = u
    wide_ref[:, :, :sums] = project_rows(u, proj_ref).reshape(shards, 8, sums)
    late = tokens_ref[...].astype(F32)[0:1, :]
    room = wide_ref.shape[2] - sums
    row_ids = lax.broadcasted_iota(jnp.int32, (8, room), 0)
    block = jnp.zeros((8, room), F32)
    for p, (at, size) in enumerate(pieces(depth, room)):
        piece = late[:, at : at + size]
        if size < room:
            piece = jnp.concatenate([piece, jnp.zeros((1, room - size), F32)], axis=1)
        block = jnp.where(row_ids == p, jnp.broadcast_to(piece, (8, room)), block)
    wide_ref[:, :, sums:] = jnp.broadcast_to(block[None], (shards, 8, room))
    send_ref[...] = wide_ref[...].astype(BF16)
    copies[4].wait()


def late_kernel(
    got_ref, rim_ref, edge_ref, keep_ref, weight_hbm, taps_hbm, bias_hbm, proj_hbm,
    mix_ref, u_ref,
    wide_ref, first_ref, pad_ref, pay_ref, weight_ref, taps_ref, bias_ref, proj_ref, sems,
):
    shards, _, lanes = got_ref.shape
    depth = first_ref.shape[1]
    width = weight_ref.shape[1]
    sums = proj_ref.shape[0]
    copies = fetches(
        [
            (weight_hbm.at[pl.ds(z * depth, depth)], weight_part(keep_ref, weight_ref, z, depth))
            for z in range(KEEP, shards)
        ]
        + [(proj_hbm, proj_ref), (taps_hbm, taps_ref), (bias_hbm, bias_ref)],
        sems,
    )
    for copy in copies:
        copy.start()
    room = lanes - sums
    wide_ref[...] = got_ref[...].astype(F32)
    for p, (at, size) in enumerate(pieces(depth, room)):
        first_ref[:, at : at + size] = wide_ref[:, p, sums : sums + size]
    total = jnp.sum(wide_ref[:, :, :sums], axis=0)
    high = total.astype(BF16).astype(F32)
    rank = mix_ref.shape[2] - 256
    coefs = sums - rank
    pay_ref[...] = jnp.zeros_like(pay_ref)
    pay_ref[:, :sums] = high
    pay_ref[:, sums : sums + coefs] = total[:, rank:] - high[:, rank:]
    pad_ref[:8, :] = rim_ref[...].astype(F32)
    pad_ref[8:, :] = edge_ref[8:, :].astype(F32)
    first = first_ref[...]
    row_ids = lax.broadcasted_iota(jnp.int32, (shards, depth), 0)
    acc = jnp.zeros((shards, width), F32)
    for z in range(shards):
        if z >= KEEP:
            copies[z - KEEP].wait()
        w = weight_part(keep_ref, weight_ref, z, depth)[...]
        only = jnp.where(row_ids == z, first, 0.0).astype(BF16)
        acc = acc + jnp.dot(only, w, preferred_element_type=F32)
    for copy in copies[shards - KEEP :]:
        copy.wait()
    pad_ref[8:9, :] = jnp.sum(acc, axis=0, keepdims=True).astype(BF16).astype(F32)
    u = convolve(taps_ref, bias_ref, pad_ref, 8, width)
    u_ref[...] = u
    part = project_rows(u, proj_ref)
    half = sums // 2
    late = taps_ref.shape[0]
    at = sums + coefs
    pay_ref[:late, at : at + half] = part[:late, :half]
    pay_ref[late : 2 * late, at : at + half] = part[:late, half:]
    pay = pay_ref[...].astype(BF16)
    for z in range(shards):
        mix_ref[z] = pay


def split2(x):
    a = x.astype(BF16)
    return a, (x - a.astype(F32)).astype(BF16)


def running_sum(x):
    rows = x.shape[0]
    row_ids = lax.broadcasted_iota(jnp.int32, (rows, rows), 0)
    col_ids = lax.broadcasted_iota(jnp.int32, (rows, rows), 1)
    lower = (row_ids >= col_ids).astype(F32).astype(BF16)
    return sum(jnp.dot(lower, p, preferred_element_type=F32) for p in split2(x)[::-1])


def state_kernel(
    mix_ref, dtw_ref, dtb_ref, alog_ref, u_ref, late_u_ref,
    step_ref, coef_ref, pay_ref,
    uf_ref, flow_ref, left_ref, bx_ref, rate_ref, low_ref, pack_ref,
):
    shards, each, _ = mix_ref.shape
    rows, width = u_ref.shape
    rank = dtw_ref.shape[0]
    n = alog_ref.shape[0]
    sums = rank + 2 * n
    half = sums // 2
    at = sums + 2 * n
    late = each // 2
    tiles = rows // 8
    low_ref[...] = mix_ref[:, :, :rank].astype(F32).reshape(rows, rank)
    coef = mix_ref[:, :, rank:sums].astype(F32) + mix_ref[:, :, sums:at].astype(F32)
    coef_ref[...] = coef.reshape(rows, 2 * n)
    pairs = jnp.sum(mix_ref[:, :, at : at + half].astype(F32), axis=0)
    early = jnp.concatenate([pairs[:late], pairs[late:]], axis=1)
    low_ref[:late, :] = early[:, :rank]
    coef_ref[:late, :] = early[:, rank:]
    low = low_ref[...].astype(BF16)
    rate_ref[...] = -jnp.exp(alog_ref[...]) * LOG2E
    uf_ref[...] = u_ref[...].astype(F32)
    uf_ref[:8, :] = late_u_ref[...].astype(F32)
    b = coef_ref[:, :n]
    for i in range(n):
        bx_ref[:, i] = jnp.broadcast_to(b[:, i : i + 1], (rows, 128)).reshape(tiles, 8, 128)
    groups = width // 128
    span = 128
    for h in range(width // span):
        cols = slice(h * span, (h + 1) * span)
        v = jnp.dot(low, dtw_ref[:, cols], preferred_element_type=F32) + dtb_ref[:, cols]
        step = jnp.maximum(v, 0.0) + jnp.log1p(jnp.exp(-jnp.abs(v)))
        step_ref[:, cols] = step
        cum = running_sum(step)
        whole = cum[rows - 1 : rows, :]
        left_ref[:, :, cols] = (whole - cum).reshape(tiles, 8, span)
        flow_ref[:, :, cols] = (step * uf_ref[:, cols]).reshape(tiles, 8, span)
        for k in range(span // 128):
            g = h * (span // 128) + k
            lanes = slice(g * 128, (g + 1) * 128)
            hi, lo = split2(whole[:, k * 128 : (k + 1) * 128])
            ends = []
            for first in range(0, n, 8):
                rates = [jnp.broadcast_to(rate_ref[i : i + 1, lanes], (8, 128)) for i in range(first, first + 8)]
                accs = [None] * 8
                for t in range(tiles):
                    left = left_ref[t, :, lanes]
                    flow = flow_ref[t, :, lanes]
                    for i in range(8):
                        term = jnp.exp2(rates[i] * left) * (flow * bx_ref[t, first + i])
                        accs[i] = term if t == 0 else accs[i] + term
                ends += [jnp.sum(acc, axis=0, keepdims=True) for acc in accs]
            pack_ref[g * n : (g + 1) * n, :] = jnp.concatenate(ends, axis=0).astype(BF16)
            low_ref[g : g + 1, :128] = hi.astype(F32)
            low_ref[groups + g : groups + g + 1, :128] = lo.astype(F32)
    pack_ref[groups * n :, :] = low_ref[: 2 * groups, :128].astype(BF16)
    pack = pack_ref[...]
    for p in range(pay_ref.shape[0]):
        pay_ref[p] = pack


def local_kernel(
    coef_ref, alog_ref, u_ref, late_u_ref, step_ref, skip_ref,
    y_ref, grow_ref, bt_ref, ct_ref, cx_ref, uf_ref, flow_ref, cum_ref,
):
    rows, width = u_ref.shape
    uf_ref[...] = u_ref[...].astype(F32)
    uf_ref[:8, :] = late_u_ref[...].astype(F32)
    flow_ref[...] = (step_ref[...] * uf_ref[...]).reshape(rows // 8, 8, width)
    cum_ref[...] = running_sum(step_ref[...])
    n = alog_ref.shape[0]
    blocks = rows // 16
    b, c = coef_ref[:, :n], coef_ref[:, n:]
    rate2 = -jnp.exp(alog_ref[...]) * LOG2E
    for i in range(n):
        cx_ref[:, i] = jnp.broadcast_to(c[:, i : i + 1], (rows, 128)).reshape(blocks, 16, 128)
    b_t, c_t = b.T, c.T
    for t in range(rows):
        bt_ref[t] = jnp.broadcast_to(b_t[:, t : t + 1], (n, 128))
        ct_ref[t] = jnp.broadcast_to(c_t[:, t : t + 1], (n, 128))
    groups = width // 128

    def block_turn(i, state):
        for r in range(8):
            t = i * 8 + r
            d = step_ref[pl.ds(t, 1), :]
            f = flow_ref[i, r : r + 1, :]
            bt = jnp.concatenate([bt_ref[t]] * groups, axis=1)
            ct = jnp.concatenate([ct_ref[t]] * groups, axis=1)
            state = jnp.exp2(rate2 * d) * state + bt * f
            y_ref[pl.ds(t, 1), :] = jnp.sum(ct * state, axis=0, keepdims=True)
        return state

    lax.fori_loop(0, rows // 8, block_turn, jnp.zeros((n, width), F32))
    y_ref[...] = y_ref[...] + skip_ref[...] * uf_ref[...]

    for g in range(groups):
        lanes = slice(g * 128, (g + 1) * 128)
        rate_g = jnp.broadcast_to(rate2[:, None, lanes], (n, 16, 128))

        def fill(i, _):
            cum = cum_ref[pl.ds(pl.multiple_of(i * 16, 16), 16), lanes]
            grow_ref[i, :, :, lanes] = (cx_ref[i] * jnp.exp2(rate_g * cum[None])).astype(BF16)
            return 0

        lax.fori_loop(0, blocks, fill, 0)


def final_kernel(mine_ref, all_ref, alog_ref, y_ref, grow_ref, thr_ref, out_ref):
    rows, width = y_ref.shape
    n = alog_ref.shape[0]
    blocks = rows // 16
    peers = all_ref.shape[0]
    mine = mine_ref[0]
    rate2 = -jnp.exp(alog_ref[...]) * LOG2E

    groups = width // 128
    for g in range(groups):
        lanes = slice(g * 128, (g + 1) * 128)
        rate_g = rate2[:, lanes]

        def join(p, state):
            block = all_ref[p].astype(F32)
            at = groups * n + g
            whole = block[at : at + 1, :] + block[at + groups : at + groups + 1, :]
            longer = jnp.exp2(rate_g * whole) * state + block[g * n : (g + 1) * n, :]
            return jnp.where(p < mine, longer, state)

        entry = jnp.zeros((n, 128), F32)
        for p in range(peers - 1):
            entry = join(p, entry)
        entry_g = jnp.broadcast_to(entry[:, None, :], (n, 16, 128))
        thr = thr_ref[:, lanes]

        def turn(i, _):
            at = pl.ds(pl.multiple_of(i * 16, 16), 16)
            y = y_ref[at, lanes] + jnp.sum(grow_ref[i, :, :, lanes].astype(F32) * entry_g, axis=0)
            out_ref[at, lanes] = (y / (1.0 + jnp.exp(-4.0 * (y - thr)))).astype(BF16)
            return 0

        lax.fori_loop(0, blocks, turn, 0, unroll=blocks)


def call(kernel, outs, ins, scratch=(), flops=0, specs=None, vmem=12 << 20, outs_in=None):
    specs = specs or [VMEM] * len(ins)
    return pl.pallas_call(
        kernel,
        out_shape=outs,
        in_specs=specs,
        out_specs=outs_in or jax.tree.map(lambda _: VMEM, outs),
        scratch_shapes=scratch,
        cost_estimate=pl.CostEstimate(flops=flops, bytes_accessed=flops // 64, transcendentals=0),
        compiler_params=pltpu.CompilerParams(vmem_limit_bytes=vmem),
    )(*[pltpu.with_memory_space_constraint(x, pltpu.HBM) if spec is HBM else x for x, spec in zip(ins, specs)])


def per_device(
    tokens, in_weight, conv_weight, conv_bias, proj_weight, dt_weight, dt_bias, a_log, skip_gain, threshold
):
    rows = tokens.shape[0]
    width = in_weight.shape[1]
    taps = conv_weight.shape[0]
    rank = dt_weight.shape[0]
    n = a_log.shape[0]
    shards = lax.axis_size("tp")
    peers = lax.axis_size("seq")
    sums = rank + 2 * n
    lanes = -(-sums // 128) * 128
    bias = conv_bias[None]
    proj = proj_weight.T
    kept = (KEEP * tokens.shape[1], width)
    held = (
        pltpu.VMEM(conv_weight.shape, F32),
        pltpu.VMEM(bias.shape, F32),
        pltpu.VMEM(proj.shape, BF16),
    )

    most = call(
        rows_kernel,
        struct((rows - 1, tokens.shape[1]), BF16),
        (tokens,),
        (pltpu.VMEM(tokens.shape, BF16), pltpu.SemaphoreType.DMA),
        flops=1 << 34,
        specs=[HBM],
    )
    main = lax.all_gather(most, "tp")
    send, edge, u, keep = call(
        project_kernel,
        (struct((shards, 8, lanes), BF16), struct((16, width), BF16), struct((rows, width), BF16),
         struct(kept, BF16)),
        (main, in_weight, tokens, conv_weight, bias, proj),
        (pltpu.VMEM((rows + 8, width), F32), pltpu.VMEM((shards, 8, lanes), F32))
        + held
        + (pltpu.VMEM((8, tokens.shape[1]), BF16), pltpu.SemaphoreType.DMA((5,))),
        flops=1 << 29,
        specs=[VMEM] * 2 + [HBM] * 4,
    )
    rim = lax.ppermute(edge[:8], "seq", [(i, i + 1) for i in range(peers - 1)])
    got = lax.all_to_all(send, "tp", 0, 0)
    mix, late_u = call(
        late_kernel,
        (struct((shards, 8, rank + 256), BF16), struct((8, width), BF16)),
        (got, rim, edge, keep, in_weight, conv_weight, bias, proj),
        (
            pltpu.VMEM((shards, 8, lanes), F32),
            pltpu.VMEM((shards, tokens.shape[1]), F32),
            pltpu.VMEM((16, width), F32),
            pltpu.VMEM((8, rank + 256), F32),
        )
        + (pltpu.VMEM((in_weight.shape[0] - kept[0], width), BF16),)
        + held
        + (pltpu.SemaphoreType.DMA((shards + 3,)),),
        flops=1 << 28,
        specs=[VMEM] * 4 + [HBM] * 4,
    )
    mix = lax.all_to_all(mix, "tp", 0, 0)
    whole = struct((rows, width), F32)
    step, coef, pay = call(
        state_kernel,
        (whole, struct((rows, 2 * n), F32), struct((peers, (n + 2) * width // 128, 128), BF16)),
        (mix, dt_weight, dt_bias[None], a_log, u, late_u),
        (
            pltpu.VMEM((rows, width), F32),
            pltpu.VMEM((rows // 8, 8, width), F32),
            pltpu.VMEM((rows // 8, 8, width), F32),
            pltpu.VMEM((rows // 8, n, 8, 128), F32),
            pltpu.VMEM((n, width), F32),
            pltpu.VMEM((rows, rank), F32),
            pltpu.VMEM(((n + 2) * width // 128, 128), BF16),
        ),
        flops=1 << 26,
    )
    everyone = lax.all_to_all(pay, "seq", 0, 0)
    y_local, grow = call(
        local_kernel,
        (whole, struct((rows // 16, n, 16, width), BF16)),
        (coef, a_log, u, late_u, step, skip_gain[None]),
        (
            pltpu.VMEM((rows, n, 128), F32),
            pltpu.VMEM((rows, n, 128), F32),
            pltpu.VMEM((rows // 16, n, 16, 128), F32),
            pltpu.VMEM((rows, width), F32),
            pltpu.VMEM((rows // 8, 8, width), F32),
            pltpu.VMEM((rows, width), F32),
        ),
        flops=1 << 28,
    )
    mine = lax.axis_index("seq").astype(jnp.int32)[None]
    return call(
        final_kernel,
        struct((rows, width), BF16),
        (mine, everyone, a_log, y_local, grow, threshold[None]),
        flops=1 << 26,
        specs=[SMEM] + [VMEM] * 5,
    )


def solution(mesh):
    return jax.shard_map(
        per_device,
        mesh=mesh,
        in_specs=(
            P("seq", "tp"),
            P(None, "tp"),
            P(None, "tp"),
            P("tp"),
            P("tp", None),
            P(None, "tp"),
            P("tp"),
            P(None, "tp"),
            P("tp"),
            P("tp"),
        ),
        out_specs=P("seq", "tp"),
        check_vma=False,
    )
```

```python
import math

import jax
import jax.numpy as jnp
from jax import lax
from jax.experimental import pallas as pl
from jax.experimental.pallas import tpu as pltpu
from jax.sharding import PartitionSpec as P

LOG2E = math.log2(math.e)
F32 = jnp.float32
BF16 = jnp.bfloat16
VMEM = pl.BlockSpec(memory_space=pltpu.VMEM)
SMEM = pl.BlockSpec(memory_space=pltpu.SMEM)
HBM = pl.BlockSpec(memory_space=pltpu.HBM)


def struct(shape, dtype):
    return jax.ShapeDtypeStruct(shape, dtype)


def silu(v):
    return v / (1.0 + jnp.exp(-v))


def convolve(taps_ref, bias_ref, pad_ref, rows, width):
    taps = taps_ref.shape[0]
    pre = jnp.broadcast_to(bias_ref[...], (rows, width))
    for k in range(taps):
        first = 9 - taps + k
        pre = pre + taps_ref[k : k + 1, :] * pad_ref[first : first + rows, :]
    return silu(pre).astype(BF16)


def pieces(depth, room):
    return [(at, min(room, depth - at)) for at in range(0, depth, room)]


def project_rows(u, proj_ref):
    return lax.dot_general(u, proj_ref[...], (((1,), (1,)), ((), ())), preferred_element_type=F32)


KEEP = 12


def fetches(pairs, sems):
    return [pltpu.make_async_copy(src, dst, sems.at[i]) for i, (src, dst) in enumerate(pairs)]


def weight_part(keep_ref, buf_ref, z, depth):
    if z < KEEP:
        return keep_ref.at[pl.ds(z * depth, depth)]
    return buf_ref.at[pl.ds((z - KEEP) * depth, depth)]


def rows_kernel(tokens_hbm, out_ref, tokens_ref, sem):
    copy = pltpu.make_async_copy(tokens_hbm, tokens_ref, sem)
    copy.start()
    copy.wait()
    out_ref[...] = tokens_ref[...].astype(F32)[1:, :].astype(BF16)


def project_kernel(
    main_ref, weight_ref, tokens_hbm, taps_hbm, bias_hbm, proj_hbm,
    send_ref, edge_ref, u_ref, keep_ref,
    pad_ref, wide_ref, taps_ref, bias_ref, proj_ref, tokens_ref, sems,
):
    shards, held, depth = main_ref.shape
    rows, width = u_ref.shape
    sums = proj_ref.shape[0]
    copies = fetches(
        [(proj_hbm, proj_ref), (taps_hbm, taps_ref), (bias_hbm, bias_ref),
         (tokens_hbm.at[pl.ds(0, 8)], tokens_ref)]
        + [(weight_ref.at[pl.ds(0, KEEP * depth)], keep_ref)],
        sems,
    )
    for copy in copies:
        copy.start()
    pad_ref[:16, :] = jnp.zeros((16, width), F32)
    acc = jnp.zeros((held, width), F32)
    for z in range(shards):
        w = weight_ref[z * depth : (z + 1) * depth, :]
        acc = acc + jnp.dot(main_ref[z], w, preferred_element_type=F32)
    for copy in copies[:4]:
        copy.wait()
    pad_ref[8 + rows - held :, :] = acc.astype(BF16).astype(F32)
    edge_ref[:8, :] = pad_ref[rows : rows + 8, :].astype(BF16)
    edge_ref[8:, :] = pad_ref[8:16, :].astype(BF16)
    u = convolve(taps_ref, bias_ref, pad_ref, rows, width)
    u_ref[...] = u
    wide_ref[:, :, :sums] = project_rows(u, proj_ref).reshape(shards, 8, sums)
    late = tokens_ref[...].astype(F32)[0:1, :]
    room = wide_ref.shape[2] - sums
    row_ids = lax.broadcasted_iota(jnp.int32, (8, room), 0)
    block = jnp.zeros((8, room), F32)
    for p, (at, size) in enumerate(pieces(depth, room)):
        piece = late[:, at : at + size]
        if size < room:
            piece = jnp.concatenate([piece, jnp.zeros((1, room - size), F32)], axis=1)
        block = jnp.where(row_ids == p, jnp.broadcast_to(piece, (8, room)), block)
    wide_ref[:, :, sums:] = jnp.broadcast_to(block[None], (shards, 8, room))
    send_ref[...] = wide_ref[...].astype(BF16)
    copies[4].wait()


def late_kernel(
    got_ref, rim_ref, edge_ref, keep_ref, weight_hbm, taps_hbm, bias_hbm, proj_hbm,
    mix_ref, u_ref,
    wide_ref, first_ref, pad_ref, pay_ref, weight_ref, taps_ref, bias_ref, proj_ref, sems,
):
    shards, _, lanes = got_ref.shape
    depth = first_ref.shape[1]
    width = weight_ref.shape[1]
    sums = proj_ref.shape[0]
    copies = fetches(
        [
            (weight_hbm.at[pl.ds(z * depth, depth)], weight_part(keep_ref, weight_ref, z, depth))
            for z in range(KEEP, shards)
        ]
        + [(proj_hbm, proj_ref), (taps_hbm, taps_ref), (bias_hbm, bias_ref)],
        sems,
    )
    for copy in copies:
        copy.start()
    room = lanes - sums
    wide_ref[...] = got_ref[...].astype(F32)
    for p, (at, size) in enumerate(pieces(depth, room)):
        first_ref[:, at : at + size] = wide_ref[:, p, sums : sums + size]
    total = jnp.sum(wide_ref[:, :, :sums], axis=0)
    high = total.astype(BF16).astype(F32)
    rank = mix_ref.shape[2] - 256
    coefs = sums - rank
    pay_ref[...] = jnp.zeros_like(pay_ref)
    pay_ref[:, :sums] = high
    pay_ref[:, sums : sums + coefs] = total[:, rank:] - high[:, rank:]
    pad_ref[:8, :] = rim_ref[...].astype(F32)
    pad_ref[8:, :] = edge_ref[8:, :].astype(F32)
    first = first_ref[...]
    row_ids = lax.broadcasted_iota(jnp.int32, (shards, depth), 0)
    acc = jnp.zeros((shards, width), F32)
    for z in range(shards):
        if z >= KEEP:
            copies[z - KEEP].wait()
        w = weight_part(keep_ref, weight_ref, z, depth)[...]
        only = jnp.where(row_ids == z, first, 0.0).astype(BF16)
        acc = acc + jnp.dot(only, w, preferred_element_type=F32)
    for copy in copies[shards - KEEP :]:
        copy.wait()
    pad_ref[8:9, :] = jnp.sum(acc, axis=0, keepdims=True).astype(BF16).astype(F32)
    u = convolve(taps_ref, bias_ref, pad_ref, 8, width)
    u_ref[...] = u
    part = project_rows(u, proj_ref)
    half = sums // 2
    late = taps_ref.shape[0]
    at = sums + coefs
    pay_ref[:late, at : at + half] = part[:late, :half]
    pay_ref[late : 2 * late, at : at + half] = part[:late, half:]
    pay = pay_ref[...].astype(BF16)
    for z in range(shards):
        mix_ref[z] = pay


def split2(x):
    a = x.astype(BF16)
    return a, (x - a.astype(F32)).astype(BF16)


def running_sum(x):
    rows = x.shape[0]
    row_ids = lax.broadcasted_iota(jnp.int32, (rows, rows), 0)
    col_ids = lax.broadcasted_iota(jnp.int32, (rows, rows), 1)
    lower = (row_ids >= col_ids).astype(F32).astype(BF16)
    return sum(jnp.dot(lower, p, preferred_element_type=F32) for p in split2(x)[::-1])


def state_kernel(
    mix_ref, dtw_ref, dtb_ref, alog_ref, u_ref, late_u_ref,
    step_ref, coef_ref, pack_ref,
    uf_ref, flow_ref, left_ref, bx_ref, rate_ref, low_ref,
):
    shards, each, _ = mix_ref.shape
    rows, width = u_ref.shape
    rank = dtw_ref.shape[0]
    n = alog_ref.shape[0]
    sums = rank + 2 * n
    half = sums // 2
    at = sums + 2 * n
    late = each // 2
    tiles = rows // 8
    low_ref[...] = mix_ref[:, :, :rank].astype(F32).reshape(rows, rank)
    coef = mix_ref[:, :, rank:sums].astype(F32) + mix_ref[:, :, sums:at].astype(F32)
    coef_ref[...] = coef.reshape(rows, 2 * n)
    pairs = jnp.sum(mix_ref[:, :, at : at + half].astype(F32), axis=0)
    early = jnp.concatenate([pairs[:late], pairs[late:]], axis=1)
    low_ref[:late, :] = early[:, :rank]
    coef_ref[:late, :] = early[:, rank:]
    low = low_ref[...].astype(BF16)
    rate_ref[...] = -jnp.exp(alog_ref[...]) * LOG2E
    uf_ref[...] = u_ref[...].astype(F32)
    uf_ref[:8, :] = late_u_ref[...].astype(F32)
    b = coef_ref[:, :n]
    for i in range(n):
        bx_ref[:, i] = jnp.broadcast_to(b[:, i : i + 1], (rows, 128)).reshape(tiles, 8, 128)
    groups = width // 128
    span = 128
    for h in range(width // span):
        cols = slice(h * span, (h + 1) * span)
        v = jnp.dot(low, dtw_ref[:, cols], preferred_element_type=F32) + dtb_ref[:, cols]
        step = jnp.maximum(v, 0.0) + jnp.log1p(jnp.exp(-jnp.abs(v)))
        step_ref[:, cols] = step
        cum = running_sum(step)
        whole = cum[rows - 1 : rows, :]
        left_ref[:, :, cols] = (whole - cum).reshape(tiles, 8, span)
        flow_ref[:, :, cols] = (step * uf_ref[:, cols]).reshape(tiles, 8, span)
        for k in range(span // 128):
            g = h * (span // 128) + k
            lanes = slice(g * 128, (g + 1) * 128)
            hi, lo = split2(whole[:, k * 128 : (k + 1) * 128])
            ends = []
            for first in range(0, n, 8):
                rates = [jnp.broadcast_to(rate_ref[i : i + 1, lanes], (8, 128)) for i in range(first, first + 8)]
                accs = [None] * 8
                for t in range(tiles):
                    left = left_ref[t, :, lanes]
                    flow = flow_ref[t, :, lanes]
                    for i in range(8):
                        term = jnp.exp2(rates[i] * left) * (flow * bx_ref[t, first + i])
                        accs[i] = term if t == 0 else accs[i] + term
                ends += [jnp.sum(acc, axis=0, keepdims=True) for acc in accs]
            pack_ref[g * n : (g + 1) * n, :] = jnp.concatenate(ends, axis=0).astype(BF16)
            low_ref[g : g + 1, :128] = hi.astype(F32)
            low_ref[groups + g : groups + g + 1, :128] = lo.astype(F32)
    pack_ref[groups * n :, :] = low_ref[: 2 * groups, :128].astype(BF16)


def merge_kernel(mine_ref, own_ref, other_ref, alog_ref, pay_ref, pack_ref):
    n, width = alog_ref.shape
    groups = width // 128
    near = groups // 2
    second_core = lax.rem(mine_ref[0], 2) == 1
    own = own_ref[...].astype(F32)
    other = other_ref[...].astype(F32)
    early = jnp.where(second_core, other, own)
    later = jnp.where(second_core, own, other)
    rate2 = -jnp.exp(alog_ref[...]) * LOG2E

    def rows(block, g, first, size):
        low = block[first + g * size : first + (g + 1) * size, :]
        high = block[first + (near + g) * size : first + (near + g + 1) * size, :]
        return jnp.where(second_core, high, low)

    for g in range(near):
        at = groups * n
        sum_early = rows(early, g, at, 1) + rows(early, g, at + groups, 1)
        sum_later = rows(later, g, at, 1) + rows(later, g, at + groups, 1)
        rate_g = jnp.where(
            second_core,
            rate2[:, (near + g) * 128 : (near + g + 1) * 128],
            rate2[:, g * 128 : (g + 1) * 128],
        )
        pack_ref[g * n : (g + 1) * n, :] = (
            jnp.exp2(rate_g * sum_later) * rows(early, g, 0, n) + rows(later, g, 0, n)
        )
        hi, lo = split2(sum_early + sum_later)
        pack_ref[near * n + g : near * n + g + 1, :] = hi.astype(F32)
        pack_ref[near * n + near + g : near * n + near + g + 1, :] = lo.astype(F32)
    pack = pack_ref[...].astype(BF16)
    for p in range(pay_ref.shape[0]):
        pay_ref[p] = pack


def local_kernel(
    coef_ref, alog_ref, u_ref, late_u_ref, step_ref, skip_ref,
    y_ref, grow_ref, bt_ref, ct_ref, cx_ref, uf_ref, flow_ref, cum_ref,
):
    rows, width = u_ref.shape
    uf_ref[...] = u_ref[...].astype(F32)
    uf_ref[:8, :] = late_u_ref[...].astype(F32)
    flow_ref[...] = (step_ref[...] * uf_ref[...]).reshape(rows // 8, 8, width)
    cum_ref[...] = running_sum(step_ref[...])
    n = alog_ref.shape[0]
    blocks = rows // 16
    b, c = coef_ref[:, :n], coef_ref[:, n:]
    rate2 = -jnp.exp(alog_ref[...]) * LOG2E
    for i in range(n):
        cx_ref[:, i] = jnp.broadcast_to(c[:, i : i + 1], (rows, 128)).reshape(blocks, 16, 128)
    b_t, c_t = b.T, c.T
    for t in range(rows):
        bt_ref[t] = jnp.broadcast_to(b_t[:, t : t + 1], (n, 128))
        ct_ref[t] = jnp.broadcast_to(c_t[:, t : t + 1], (n, 128))
    groups = width // 128

    def block_turn(i, state):
        for r in range(8):
            t = i * 8 + r
            d = step_ref[pl.ds(t, 1), :]
            f = flow_ref[i, r : r + 1, :]
            bt = jnp.concatenate([bt_ref[t]] * groups, axis=1)
            ct = jnp.concatenate([ct_ref[t]] * groups, axis=1)
            state = jnp.exp2(rate2 * d) * state + bt * f
            y_ref[pl.ds(t, 1), :] = jnp.sum(ct * state, axis=0, keepdims=True)
        return state

    lax.fori_loop(0, rows // 8, block_turn, jnp.zeros((n, width), F32))
    y_ref[...] = y_ref[...] + skip_ref[...] * uf_ref[...]

    for g in range(groups):
        lanes = slice(g * 128, (g + 1) * 128)
        rate_g = jnp.broadcast_to(rate2[:, None, lanes], (n, 16, 128))

        def fill(i, _):
            cum = cum_ref[pl.ds(pl.multiple_of(i * 16, 16), 16), lanes]
            grow_ref[i, :, :, lanes] = (cx_ref[i] * jnp.exp2(rate_g * cum[None])).astype(BF16)
            return 0

        lax.fori_loop(0, blocks, fill, 0)


def final_kernel(mine_ref, all_ref, other_ref, alog_ref, y_ref, grow_ref, thr_ref, out_ref):
    rows, width = y_ref.shape
    n = alog_ref.shape[0]
    blocks = rows // 16
    chips = all_ref.shape[0] // 2
    mine = mine_ref[0]
    second_core = lax.rem(mine, 2) == 1
    rate2 = -jnp.exp(alog_ref[...]) * LOG2E
    groups = width // 128
    near = groups // 2
    other = other_ref[...].astype(F32)
    for g in range(groups):
        lanes = slice(g * 128, (g + 1) * 128)
        rate_g = rate2[:, lanes]
        half, place = g // near, g % near
        entry = jnp.zeros((n, 128), F32)
        for p in range(chips - 1):
            block = all_ref[2 * p + half].astype(F32)
            at = near * n + place
            whole = block[at : at + 1, :] + block[at + near : at + near + 1, :]
            longer = jnp.exp2(rate_g * whole) * entry + block[place * n : (place + 1) * n, :]
            entry = jnp.where(2 * p + 1 < mine, longer, entry)
        at = groups * n + g
        whole = other[at : at + 1, :] + other[at + groups : at + groups + 1, :]
        longer = jnp.exp2(rate_g * whole) * entry + other[g * n : (g + 1) * n, :]
        entry = jnp.where(second_core, longer, entry)
        entry_g = jnp.broadcast_to(entry[:, None, :], (n, 16, 128)).astype(BF16)
        thr = thr_ref[:, lanes]

        def turn(i, _):
            at = pl.ds(pl.multiple_of(i * 16, 16), 16)
            y = y_ref[at, lanes] + jnp.sum((grow_ref[i, :, :, lanes] * entry_g).astype(F32), axis=0)
            out_ref[at, lanes] = (y / (1.0 + jnp.exp(-4.0 * (y - thr)))).astype(BF16)
            return 0

        lax.fori_loop(0, blocks, turn, 0, unroll=blocks)


def call(kernel, outs, ins, scratch=(), flops=0, specs=None, vmem=12 << 20, outs_in=None):
    specs = specs or [VMEM] * len(ins)
    return pl.pallas_call(
        kernel,
        out_shape=outs,
        in_specs=specs,
        out_specs=outs_in or jax.tree.map(lambda _: VMEM, outs),
        scratch_shapes=scratch,
        cost_estimate=pl.CostEstimate(flops=flops, bytes_accessed=flops // 64, transcendentals=0),
        compiler_params=pltpu.CompilerParams(vmem_limit_bytes=vmem),
    )(*[pltpu.with_memory_space_constraint(x, pltpu.HBM) if spec is HBM else x for x, spec in zip(ins, specs)])


def per_device(
    tokens, in_weight, conv_weight, conv_bias, proj_weight, dt_weight, dt_bias, a_log, skip_gain, threshold
):
    rows = tokens.shape[0]
    width = in_weight.shape[1]
    taps = conv_weight.shape[0]
    rank = dt_weight.shape[0]
    n = a_log.shape[0]
    shards = lax.axis_size("tp")
    peers = lax.axis_size("seq")
    sums = rank + 2 * n
    lanes = -(-sums // 128) * 128
    bias = conv_bias[None]
    proj = proj_weight.T
    kept = (KEEP * tokens.shape[1], width)
    held = (
        pltpu.VMEM(conv_weight.shape, F32),
        pltpu.VMEM(bias.shape, F32),
        pltpu.VMEM(proj.shape, BF16),
    )

    most = call(
        rows_kernel,
        struct((rows - 1, tokens.shape[1]), BF16),
        (tokens,),
        (pltpu.VMEM(tokens.shape, BF16), pltpu.SemaphoreType.DMA),
        flops=1 << 34,
        specs=[HBM],
    )
    main = lax.all_gather(most, "tp")
    send, edge, u, keep = call(
        project_kernel,
        (struct((shards, 8, lanes), BF16), struct((16, width), BF16), struct((rows, width), BF16),
         struct(kept, BF16)),
        (main, in_weight, tokens, conv_weight, bias, proj),
        (pltpu.VMEM((rows + 8, width), F32), pltpu.VMEM((shards, 8, lanes), F32))
        + held
        + (pltpu.VMEM((8, tokens.shape[1]), BF16), pltpu.SemaphoreType.DMA((5,))),
        flops=1 << 29,
        specs=[VMEM] * 2 + [HBM] * 4,
    )
    rim = lax.ppermute(edge[:8], "seq", [(i, i + 1) for i in range(peers - 1)])
    got = lax.all_to_all(send, "tp", 0, 0)
    mix, late_u = call(
        late_kernel,
        (struct((shards, 8, rank + 256), BF16), struct((8, width), BF16)),
        (got, rim, edge, keep, in_weight, conv_weight, bias, proj),
        (
            pltpu.VMEM((shards, 8, lanes), F32),
            pltpu.VMEM((shards, tokens.shape[1]), F32),
            pltpu.VMEM((16, width), F32),
            pltpu.VMEM((8, rank + 256), F32),
        )
        + (pltpu.VMEM((in_weight.shape[0] - kept[0], width), BF16),)
        + held
        + (pltpu.SemaphoreType.DMA((shards + 3,)),),
        flops=1 << 28,
        specs=[VMEM] * 4 + [HBM] * 4,
    )
    mix = lax.all_to_all(mix, "tp", 0, 0)
    whole = struct((rows, width), F32)
    step, coef, own = call(
        state_kernel,
        (whole, struct((rows, 2 * n), F32), struct(((n + 2) * width // 128, 128), BF16)),
        (mix, dt_weight, dt_bias[None], a_log, u, late_u),
        (
            pltpu.VMEM((rows, width), F32),
            pltpu.VMEM((rows // 8, 8, width), F32),
            pltpu.VMEM((rows // 8, 8, width), F32),
            pltpu.VMEM((rows // 8, n, 8, 128), F32),
            pltpu.VMEM((n, width), F32),
            pltpu.VMEM((rows, rank), F32),
        ),
        flops=1 << 26,
    )
    mine = lax.axis_index("seq").astype(jnp.int32)[None]
    other = lax.ppermute(own, "seq", [(i, i ^ 1) for i in range(peers)])
    half = (n + 2) * width // 256
    pay = call(
        merge_kernel,
        struct((peers, half, 128), BF16),
        (mine, own, other, a_log),
        (pltpu.VMEM((half, 128), F32),),
        flops=1 << 20,
        specs=[SMEM] + [VMEM] * 3,
    )
    pay, coef = lax.optimization_barrier((pay, coef))
    everyone = lax.all_to_all(pay, "seq", 0, 0)
    y_local, grow = call(
        local_kernel,
        (whole, struct((rows // 16, n, 16, width), BF16)),
        (coef, a_log, u, late_u, step, skip_gain[None]),
        (
            pltpu.VMEM((rows, n, 128), F32),
            pltpu.VMEM((rows, n, 128), F32),
            pltpu.VMEM((rows // 16, n, 16, 128), F32),
            pltpu.VMEM((rows, width), F32),
            pltpu.VMEM((rows // 8, 8, width), F32),
            pltpu.VMEM((rows, width), F32),
        ),
        flops=1 << 28,
    )
    return call(
        final_kernel,
        struct((rows, width), BF16),
        (mine, everyone, other, a_log, y_local, grow, threshold[None]),
        flops=1 << 26,
        specs=[SMEM] + [VMEM] * 6,
    )


def solution(mesh):
    return jax.shard_map(
        per_device,
        mesh=mesh,
        in_specs=(
            P("seq", "tp"),
            P(None, "tp"),
            P(None, "tp"),
            P("tp"),
            P("tp", None),
            P(None, "tp"),
            P("tp"),
            P(None, "tp"),
            P("tp"),
            P("tp"),
        ),
        out_specs=P("seq", "tp"),
        check_vma=False,
    )
```

```python
import math

import jax
import jax.numpy as jnp
from jax import lax
from jax.experimental import pallas as pl
from jax.experimental.pallas import tpu as pltpu
from jax.sharding import PartitionSpec as P

LOG2E = math.log2(math.e)
F32 = jnp.float32
BF16 = jnp.bfloat16
VMEM = pl.BlockSpec(memory_space=pltpu.VMEM)
SMEM = pl.BlockSpec(memory_space=pltpu.SMEM)
HBM = pl.BlockSpec(memory_space=pltpu.HBM)


def struct(shape, dtype):
    return jax.ShapeDtypeStruct(shape, dtype)


def silu(v):
    return v / (1.0 + jnp.exp(-v))


def convolve(taps_ref, bias_ref, pad_ref, rows, width):
    taps = taps_ref.shape[0]
    pre = jnp.broadcast_to(bias_ref[...], (rows, width))
    for k in range(taps):
        first = 9 - taps + k
        pre = pre + taps_ref[k : k + 1, :] * pad_ref[first : first + rows, :]
    return silu(pre).astype(BF16)


def pieces(depth, room):
    return [(at, min(room, depth - at)) for at in range(0, depth, room)]


def project_rows(u, proj_ref):
    return lax.dot_general(u, proj_ref[...], (((1,), (1,)), ((), ())), preferred_element_type=F32)


KEEP = 11


def fetches(pairs, sems):
    return [pltpu.make_async_copy(src, dst, sems.at[i]) for i, (src, dst) in enumerate(pairs)]


def weight_part(keep_ref, buf_ref, z, depth):
    if z < KEEP:
        return keep_ref.at[pl.ds(z * depth, depth)]
    return buf_ref.at[pl.ds((z - KEEP) * depth, depth)]


def rows_kernel(tokens_hbm, out_ref, tokens_ref, sem):
    copy = pltpu.make_async_copy(tokens_hbm, tokens_ref, sem)
    copy.start()
    copy.wait()
    out_ref[...] = tokens_ref[...].astype(F32)[1:, :].astype(BF16)


def project_kernel(
    main_ref, weight_ref, tokens_hbm, taps_hbm, bias_hbm, proj_hbm,
    send_ref, edge_ref, u_ref, keep_ref,
    pad_ref, wide_ref, taps_ref, bias_ref, proj_ref, tokens_ref, sems,
):
    shards, held, depth = main_ref.shape
    rows, width = u_ref.shape
    sums = proj_ref.shape[0]
    copies = fetches(
        [(proj_hbm, proj_ref), (taps_hbm, taps_ref), (bias_hbm, bias_ref),
         (tokens_hbm.at[pl.ds(0, 8)], tokens_ref)]
        + [(weight_ref.at[pl.ds(0, KEEP * depth)], keep_ref)],
        sems,
    )
    for copy in copies:
        copy.start()
    pad_ref[:16, :] = jnp.zeros((16, width), F32)
    acc = jnp.zeros((held, width), F32)
    for z in range(shards):
        w = weight_ref[z * depth : (z + 1) * depth, :]
        acc = acc + jnp.dot(main_ref[z], w, preferred_element_type=F32)
    for copy in copies[:4]:
        copy.wait()
    pad_ref[8 + rows - held :, :] = acc.astype(BF16).astype(F32)
    edge_ref[:8, :] = pad_ref[rows : rows + 8, :].astype(BF16)
    edge_ref[8:, :] = pad_ref[8:16, :].astype(BF16)
    u = convolve(taps_ref, bias_ref, pad_ref, rows, width)
    u_ref[...] = u
    wide_ref[:, :, :sums] = project_rows(u, proj_ref).reshape(shards, 8, sums)
    late = tokens_ref[...].astype(F32)[0:1, :]
    room = wide_ref.shape[2] - sums
    row_ids = lax.broadcasted_iota(jnp.int32, (8, room), 0)
    block = jnp.zeros((8, room), F32)
    for p, (at, size) in enumerate(pieces(depth, room)):
        piece = late[:, at : at + size]
        if size < room:
            piece = jnp.concatenate([piece, jnp.zeros((1, room - size), F32)], axis=1)
        block = jnp.where(row_ids == p, jnp.broadcast_to(piece, (8, room)), block)
    wide_ref[:, :, sums:] = jnp.broadcast_to(block[None], (shards, 8, room))
    send_ref[...] = wide_ref[...].astype(BF16)
    copies[4].wait()


def late_kernel(
    got_ref, rim_ref, edge_ref, keep_ref, weight_hbm, taps_hbm, bias_hbm, proj_hbm,
    mix_ref, u_ref,
    wide_ref, first_ref, pad_ref, pay_ref, weight_ref, taps_ref, bias_ref, proj_ref, sems,
):
    shards, _, lanes = got_ref.shape
    depth = first_ref.shape[1]
    width = weight_ref.shape[1]
    sums = proj_ref.shape[0]
    copies = fetches(
        [
            (weight_hbm.at[pl.ds(z * depth, depth)], weight_part(keep_ref, weight_ref, z, depth))
            for z in range(KEEP, shards)
        ]
        + [(proj_hbm, proj_ref), (taps_hbm, taps_ref), (bias_hbm, bias_ref)],
        sems,
    )
    for copy in copies:
        copy.start()
    room = lanes - sums
    wide_ref[...] = got_ref[...].astype(F32)
    for p, (at, size) in enumerate(pieces(depth, room)):
        first_ref[:, at : at + size] = wide_ref[:, p, sums : sums + size]
    total = jnp.sum(wide_ref[:, :, :sums], axis=0)
    high = total.astype(BF16).astype(F32)
    rank = mix_ref.shape[2] - 256
    coefs = sums - rank
    pay_ref[...] = jnp.zeros_like(pay_ref)
    pay_ref[:, :sums] = high
    pay_ref[:, sums : sums + coefs] = total[:, rank:] - high[:, rank:]
    pad_ref[:8, :] = rim_ref[...].astype(F32)
    pad_ref[8:, :] = edge_ref[8:, :].astype(F32)
    first = first_ref[...]
    row_ids = lax.broadcasted_iota(jnp.int32, (shards, depth), 0)
    acc = jnp.zeros((shards, width), F32)
    for z in range(shards):
        if z >= KEEP:
            copies[z - KEEP].wait()
        w = weight_part(keep_ref, weight_ref, z, depth)[...]
        only = jnp.where(row_ids == z, first, 0.0).astype(BF16)
        acc = acc + jnp.dot(only, w, preferred_element_type=F32)
    for copy in copies[shards - KEEP :]:
        copy.wait()
    pad_ref[8:9, :] = jnp.sum(acc, axis=0, keepdims=True).astype(BF16).astype(F32)
    u = convolve(taps_ref, bias_ref, pad_ref, 8, width)
    u_ref[...] = u
    part = project_rows(u, proj_ref)
    half = sums // 2
    late = taps_ref.shape[0]
    at = sums + coefs
    pay_ref[:late, at : at + half] = part[:late, :half]
    pay_ref[late : 2 * late, at : at + half] = part[:late, half:]
    pay = pay_ref[...].astype(BF16)
    for z in range(shards):
        mix_ref[z] = pay


def split2(x):
    a = x.astype(BF16)
    return a, (x - a.astype(F32)).astype(BF16)


def running_sum(x):
    rows = x.shape[0]
    row_ids = lax.broadcasted_iota(jnp.int32, (rows, rows), 0)
    col_ids = lax.broadcasted_iota(jnp.int32, (rows, rows), 1)
    lower = (row_ids >= col_ids).astype(F32).astype(BF16)
    return sum(jnp.dot(lower, p, preferred_element_type=F32) for p in split2(x)[::-1])


def state_kernel(
    mix_ref, dtw_ref, dtb_ref, alog_ref, u_ref, late_u_ref,
    step_ref, coef_ref, pack_ref,
    uf_ref, flow_ref, left_ref, bx_ref, rate_ref, low_ref,
):
    shards, each, _ = mix_ref.shape
    rows, width = u_ref.shape
    rank = dtw_ref.shape[0]
    n = alog_ref.shape[0]
    sums = rank + 2 * n
    half = sums // 2
    at = sums + 2 * n
    late = each // 2
    tiles = rows // 8
    low_ref[...] = mix_ref[:, :, :rank].astype(F32).reshape(rows, rank)
    coef = mix_ref[:, :, rank:sums].astype(F32) + mix_ref[:, :, sums:at].astype(F32)
    coef_ref[...] = coef.reshape(rows, 2 * n)
    pairs = jnp.sum(mix_ref[:, :, at : at + half].astype(F32), axis=0)
    early = jnp.concatenate([pairs[:late], pairs[late:]], axis=1)
    low_ref[:late, :] = early[:, :rank]
    coef_ref[:late, :] = early[:, rank:]
    low = low_ref[...].astype(BF16)
    rate_ref[...] = -jnp.exp(alog_ref[...]) * LOG2E
    uf_ref[...] = u_ref[...].astype(F32)
    uf_ref[:8, :] = late_u_ref[...].astype(F32)
    b = coef_ref[:, :n]
    for i in range(n):
        bx_ref[:, i] = jnp.broadcast_to(b[:, i : i + 1], (rows, 128)).reshape(tiles, 8, 128)
    groups = width // 128
    span = 128
    for h in range(width // span):
        cols = slice(h * span, (h + 1) * span)
        v = jnp.dot(low, dtw_ref[:, cols], preferred_element_type=F32) + dtb_ref[:, cols]
        step = jnp.maximum(v, 0.0) + jnp.log1p(jnp.exp(-jnp.abs(v)))
        step_ref[:, cols] = step
        cum = running_sum(step)
        whole = cum[rows - 1 : rows, :]
        left_ref[:, :, cols] = (whole - cum).reshape(tiles, 8, span)
        flow_ref[:, :, cols] = (step * uf_ref[:, cols]).reshape(tiles, 8, span)
        for k in range(span // 128):
            g = h * (span // 128) + k
            lanes = slice(g * 128, (g + 1) * 128)
            hi, lo = split2(whole[:, k * 128 : (k + 1) * 128])
            ends = []
            for first in range(0, n, 8):
                rates = [jnp.broadcast_to(rate_ref[i : i + 1, lanes], (8, 128)) for i in range(first, first + 8)]
                accs = [None] * 8
                for t in range(tiles):
                    left = left_ref[t, :, lanes]
                    flow = flow_ref[t, :, lanes]
                    for i in range(8):
                        term = jnp.exp2(rates[i] * left) * (flow * bx_ref[t, first + i])
                        accs[i] = term if t == 0 else accs[i] + term
                ends += [jnp.sum(acc, axis=0, keepdims=True) for acc in accs]
            pack_ref[g * n : (g + 1) * n, :] = jnp.concatenate(ends, axis=0).astype(BF16)
            low_ref[g : g + 1, :128] = hi.astype(F32)
            low_ref[groups + g : groups + g + 1, :128] = lo.astype(F32)
    pack_ref[groups * n :, :] = low_ref[: 2 * groups, :128].astype(BF16)


def merge_kernel(mine_ref, own_ref, other_ref, alog_ref, pay_ref, pack_ref):
    n, width = alog_ref.shape
    groups = width // 128
    near = groups // 2
    second_core = lax.rem(mine_ref[0], 2) == 1
    own = own_ref[...].astype(F32)
    other = other_ref[...].astype(F32)
    early = jnp.where(second_core, other, own)
    later = jnp.where(second_core, own, other)
    rate2 = -jnp.exp(alog_ref[...]) * LOG2E

    def rows(block, g, first, size):
        low = block[first + g * size : first + (g + 1) * size, :]
        high = block[first + (near + g) * size : first + (near + g + 1) * size, :]
        return jnp.where(second_core, high, low)

    for g in range(near):
        at = groups * n
        sum_early = rows(early, g, at, 1) + rows(early, g, at + groups, 1)
        sum_later = rows(later, g, at, 1) + rows(later, g, at + groups, 1)
        rate_g = jnp.where(
            second_core,
            rate2[:, (near + g) * 128 : (near + g + 1) * 128],
            rate2[:, g * 128 : (g + 1) * 128],
        )
        pack_ref[g * n : (g + 1) * n, :] = (
            jnp.exp2(rate_g * sum_later) * rows(early, g, 0, n) + rows(later, g, 0, n)
        )
        hi, lo = split2(sum_early + sum_later)
        pack_ref[near * n + g : near * n + g + 1, :] = hi.astype(F32)
        pack_ref[near * n + near + g : near * n + near + g + 1, :] = lo.astype(F32)
    pack = pack_ref[...].astype(BF16)
    for p in range(pay_ref.shape[0]):
        pay_ref[p] = pack


def local_kernel(
    coef_ref, alog_ref, u_ref, late_u_ref, step_ref, skip_ref,
    y_ref, grow_ref, bt_ref, ct_ref, cx_ref, uf_ref, flow_ref, cum_ref,
):
    rows, width = u_ref.shape
    uf_ref[...] = u_ref[...].astype(F32)
    uf_ref[:8, :] = late_u_ref[...].astype(F32)
    flow_ref[...] = (step_ref[...] * uf_ref[...]).reshape(rows // 8, 8, width)
    cum_ref[...] = running_sum(step_ref[...])
    n = alog_ref.shape[0]
    blocks = rows // 16
    b, c = coef_ref[:, :n], coef_ref[:, n:]
    rate2 = -jnp.exp(alog_ref[...]) * LOG2E
    for i in range(n):
        cx_ref[:, i] = jnp.broadcast_to(c[:, i : i + 1], (rows, 128)).reshape(blocks, 16, 128)
    b_t, c_t = b.T, c.T
    for t in range(rows):
        bt_ref[t] = jnp.broadcast_to(b_t[:, t : t + 1], (n, 128))
        ct_ref[t] = jnp.broadcast_to(c_t[:, t : t + 1], (n, 128))
    groups = width // 128

    def block_turn(i, state):
        for r in range(8):
            t = i * 8 + r
            d = step_ref[pl.ds(t, 1), :]
            f = flow_ref[i, r : r + 1, :]
            bt = jnp.concatenate([bt_ref[t]] * groups, axis=1)
            ct = jnp.concatenate([ct_ref[t]] * groups, axis=1)
            state = jnp.exp2(rate2 * d) * state + bt * f
            y_ref[pl.ds(t, 1), :] = jnp.sum(ct * state, axis=0, keepdims=True)
        return state

    lax.fori_loop(0, rows // 8, block_turn, jnp.zeros((n, width), F32))
    y_ref[...] = y_ref[...] + skip_ref[...] * uf_ref[...]

    for g in range(groups):
        lanes = slice(g * 128, (g + 1) * 128)
        rate_g = jnp.broadcast_to(rate2[:, None, lanes], (n, 16, 128))

        def fill(i, _):
            cum = cum_ref[pl.ds(pl.multiple_of(i * 16, 16), 16), lanes]
            grow_ref[i, :, :, lanes] = (cx_ref[i] * jnp.exp2(rate_g * cum[None])).astype(BF16)
            return 0

        lax.fori_loop(0, blocks, fill, 0)


def final_kernel(mine_ref, all_ref, other_ref, alog_ref, y_ref, grow_ref, thr_ref, out_ref):
    rows, width = y_ref.shape
    n = alog_ref.shape[0]
    blocks = rows // 16
    chips = all_ref.shape[0] // 2
    mine = mine_ref[0]
    second_core = lax.rem(mine, 2) == 1
    rate2 = -jnp.exp(alog_ref[...]) * LOG2E
    groups = width // 128
    near = groups // 2
    other = other_ref[...].astype(F32)
    for g in range(groups):
        lanes = slice(g * 128, (g + 1) * 128)
        rate_g = rate2[:, lanes]
        half, place = g // near, g % near
        entry = jnp.zeros((n, 128), F32)
        for p in range(chips - 1):
            block = all_ref[2 * p + half].astype(F32)
            at = near * n + place
            whole = block[at : at + 1, :] + block[at + near : at + near + 1, :]
            longer = jnp.exp2(rate_g * whole) * entry + block[place * n : (place + 1) * n, :]
            entry = jnp.where(2 * p + 1 < mine, longer, entry)
        at = groups * n + g
        whole = other[at : at + 1, :] + other[at + groups : at + groups + 1, :]
        longer = jnp.exp2(rate_g * whole) * entry + other[g * n : (g + 1) * n, :]
        entry = jnp.where(second_core, longer, entry)
        entry_g = jnp.broadcast_to(entry[:, None, :], (n, 16, 128))
        thr = thr_ref[:, lanes]

        def turn(i, _):
            at = pl.ds(pl.multiple_of(i * 16, 16), 16)
            y = y_ref[at, lanes] + jnp.sum(grow_ref[i, :, :, lanes].astype(F32) * entry_g, axis=0)
            out_ref[at, lanes] = (y / (1.0 + jnp.exp(-4.0 * (y - thr)))).astype(BF16)
            return 0

        lax.fori_loop(0, blocks, turn, 0, unroll=blocks)


def call(kernel, outs, ins, scratch=(), flops=0, specs=None, vmem=12 << 20, outs_in=None):
    specs = specs or [VMEM] * len(ins)
    return pl.pallas_call(
        kernel,
        out_shape=outs,
        in_specs=specs,
        out_specs=outs_in or jax.tree.map(lambda _: VMEM, outs),
        scratch_shapes=scratch,
        cost_estimate=pl.CostEstimate(flops=flops, bytes_accessed=flops // 64, transcendentals=0),
        compiler_params=pltpu.CompilerParams(vmem_limit_bytes=vmem),
    )(*[pltpu.with_memory_space_constraint(x, pltpu.HBM) if spec is HBM else x for x, spec in zip(ins, specs)])


def per_device(
    tokens, in_weight, conv_weight, conv_bias, proj_weight, dt_weight, dt_bias, a_log, skip_gain, threshold
):
    rows = tokens.shape[0]
    width = in_weight.shape[1]
    taps = conv_weight.shape[0]
    rank = dt_weight.shape[0]
    n = a_log.shape[0]
    shards = lax.axis_size("tp")
    peers = lax.axis_size("seq")
    sums = rank + 2 * n
    lanes = -(-sums // 128) * 128
    bias = conv_bias[None]
    proj = proj_weight.T
    kept = (KEEP * tokens.shape[1], width)
    held = (
        pltpu.VMEM(conv_weight.shape, F32),
        pltpu.VMEM(bias.shape, F32),
        pltpu.VMEM(proj.shape, BF16),
    )

    most = call(
        rows_kernel,
        struct((rows - 1, tokens.shape[1]), BF16),
        (tokens,),
        (pltpu.VMEM(tokens.shape, BF16), pltpu.SemaphoreType.DMA),
        flops=1 << 34,
        specs=[HBM],
    )
    main = lax.all_gather(most, "tp")
    send, edge, u, keep = call(
        project_kernel,
        (struct((shards, 8, lanes), BF16), struct((16, width), BF16), struct((rows, width), BF16),
         struct(kept, BF16)),
        (main, in_weight, tokens, conv_weight, bias, proj),
        (pltpu.VMEM((rows + 8, width), F32), pltpu.VMEM((shards, 8, lanes), F32))
        + held
        + (pltpu.VMEM((8, tokens.shape[1]), BF16), pltpu.SemaphoreType.DMA((5,))),
        flops=1 << 29,
        specs=[VMEM] * 2 + [HBM] * 4,
    )
    rim = lax.ppermute(edge[:8], "seq", [(i, i + 1) for i in range(peers - 1)])
    got = lax.all_to_all(send, "tp", 0, 0)
    mix, late_u = call(
        late_kernel,
        (struct((shards, 8, rank + 256), BF16), struct((8, width), BF16)),
        (got, rim, edge, keep, in_weight, conv_weight, bias, proj),
        (
            pltpu.VMEM((shards, 8, lanes), F32),
            pltpu.VMEM((shards, tokens.shape[1]), F32),
            pltpu.VMEM((16, width), F32),
            pltpu.VMEM((8, rank + 256), F32),
        )
        + (pltpu.VMEM((in_weight.shape[0] - kept[0], width), BF16),)
        + held
        + (pltpu.SemaphoreType.DMA((shards + 3,)),),
        flops=1 << 28,
        specs=[VMEM] * 4 + [HBM] * 4,
    )
    mix = lax.all_to_all(mix, "tp", 0, 0)
    whole = struct((rows, width), F32)
    step, coef, own = call(
        state_kernel,
        (whole, struct((rows, 2 * n), F32), struct(((n + 2) * width // 128, 128), BF16)),
        (mix, dt_weight, dt_bias[None], a_log, u, late_u),
        (
            pltpu.VMEM((rows, width), F32),
            pltpu.VMEM((rows // 8, 8, width), F32),
            pltpu.VMEM((rows // 8, 8, width), F32),
            pltpu.VMEM((rows // 8, n, 8, 128), F32),
            pltpu.VMEM((n, width), F32),
            pltpu.VMEM((rows, rank), F32),
        ),
        flops=1 << 26,
    )
    mine = lax.axis_index("seq").astype(jnp.int32)[None]
    other = lax.ppermute(own, "seq", [(i, i ^ 1) for i in range(peers)])
    half = (n + 2) * width // 256
    pay = call(
        merge_kernel,
        struct((peers, half, 128), BF16),
        (mine, own, other, a_log),
        (pltpu.VMEM((half, 128), F32),),
        flops=1 << 20,
        specs=[SMEM] + [VMEM] * 3,
    )
    pay, coef = lax.optimization_barrier((pay, coef))
    everyone = lax.all_to_all(pay, "seq", 0, 0)
    y_local, grow = call(
        local_kernel,
        (whole, struct((rows // 16, n, 16, width), BF16)),
        (coef, a_log, u, late_u, step, skip_gain[None]),
        (
            pltpu.VMEM((rows, n, 128), F32),
            pltpu.VMEM((rows, n, 128), F32),
            pltpu.VMEM((rows // 16, n, 16, 128), F32),
            pltpu.VMEM((rows, width), F32),
            pltpu.VMEM((rows // 8, 8, width), F32),
            pltpu.VMEM((rows, width), F32),
        ),
        flops=1 << 28,
    )
    return call(
        final_kernel,
        struct((rows, width), BF16),
        (mine, everyone, other, a_log, y_local, grow, threshold[None]),
        flops=1 << 26,
        specs=[SMEM] + [VMEM] * 6,
    )


def solution(mesh):
    return jax.shard_map(
        per_device,
        mesh=mesh,
        in_specs=(
            P("seq", "tp"),
            P(None, "tp"),
            P(None, "tp"),
            P("tp"),
            P("tp", None),
            P(None, "tp"),
            P("tp"),
            P(None, "tp"),
            P("tp"),
            P("tp"),
        ),
        out_specs=P("seq", "tp"),
        check_vma=False,
    )
```
